32 devices in a mesh: groups: 2 (over y), seq: 8 (over z, x), track: 2 (over core).
Axes of the slice: x: 2, y: 2, z: 4, core: 2. Of those that a mesh axis runs over, the one named last changes fastest.
Arguments:
- section_input: bfloat16 [1536, 4096], P('track', ('groups', 'seq')), parts along dimension 1, may hold values from -6 to 6
- conv_taps: float32 [1536, 3], P(('track', 'seq')), may hold values from -3 to 3
- dilation_level: int32 [1536], P(('track', 'seq')), may hold values from 0 to 4, as said below
- pointwise_matrix: bfloat16 [1536, 1536], P('track', 'seq'), may hold values from -0.15625 to 0.15625
- head_weight: bfloat16 [1536, 5312], P('seq', 'track'), may hold values from -0.078125 to 0.078125
- pred_error: bfloat16 [4096, 5312], P(('groups', 'seq'), 'track'), parts along dimension 0, may hold values from -6 to 6
- tail_mask: int32 [4096, 5312], P(('groups', 'seq'), 'track'), parts along dimension 0, may hold values 0 or 1
- track_scale: float32 [5312], P('track'), may hold values from 0.5 to 2
Outputs:
- input_grad: bfloat16 [1536, 4096], P('track', ('groups', 'seq')), parts along dimension 1
- taps_grad: float32 [3072, 3], P(('groups', 'track', 'seq')), parts along dimension 0
The draws below stay inside these ranges and needn't reach their ends.
There are 2 independent parts, one for each index of `groups`. The reference program is written for one: setup_inputs(seed, part) draws one part's arguments, and reference() takes and returns one part's arrays. A program takes and returns all parts, laid end to end along the dimension named above; an argument that names none is the same for every part. Nothing has to cross between parts.
Inputs may be any that keep to these rules, and one draw needn't show every extreme that they name: `dilation_level`: every level 0 and 4 occurs.
All inputs are finite; a program needn't handle non-finite values. No bound on the sum of `tail_mask` on one device may be relied on, other than what follows from the above.
Results may differ from the reference program's by a relative error of at most 0.0057.
Values may be sent and summed in bfloat16 or wider, within the bound.
A program may use at most 128 MiB of HBM per device.

```python
import math
import jax
import jax.numpy as jnp
from jax import lax

C = 1536
TR = 5312
ROWS = 256
KW = 3
DILATION_COUNT = 5
BASE_DILATION = 32
LENGTH = 2048


def draw_dilation_level(key, part):
    leading_key, trailing_key = jax.random.split(key)
    levels = jax.random.randint(leading_key, (C,), 0, DILATION_COUNT, dtype=jnp.int32)
    chosen = jax.random.permutation(trailing_key, C)
    return levels.at[chosen[0]].set(0).at[chosen[1]].set(DILATION_COUNT - 1)


def with_ends(entries, stream_key, low, largest):
    longest = entries.shape.index(max(entries.shape))
    spots = []
    for shift in (0, 1):
        where = [jax.random.randint(jax.random.fold_in(stream_key, axis), (), 0, length) for axis, length in enumerate(entries.shape)]
        where[longest] = (where[longest] + shift) % entries.shape[longest]
        spots.append(tuple(where))
    return entries.at[spots[0]].set(low).at[spots[1]].set(largest)


def level_of(own_key, dims, shards, low, high):
    loudness = 1.0
    for axis_at, shards_of in shards:
        steps = jax.random.uniform(jax.random.fold_in(jax.random.fold_in(own_key, 6), axis_at), (shards_of,), jnp.float32, low / len(shards), high / len(shards))
        loudness = loudness * jnp.repeat(jnp.exp(steps), dims[axis_at] // shards_of).reshape((-1,) + (1,) * (len(dims) - 1 - axis_at))
    return loudness


def normal_values(own_key, dims, width, most, cuts=(), kind=jnp.bfloat16):
    values = width * jax.random.normal(own_key, dims, jnp.float32)
    if cuts:
        values = values * level_of(own_key, dims, cuts, -0.22, 0.18)
    return jnp.clip(values, -most, most).astype(kind)


def setup_inputs(seed: int = 0, part: int = 0) -> dict:
    arg_keys = jax.random.split(jax.random.key(seed), 9)
    part_keys = jax.random.split(jax.random.fold_in(arg_keys[8], part), 9)
    return {
        "section_input": normal_values(part_keys[0], (C, LENGTH), 1.0, 6.0, ((0, 2), (1, 8))),
        "conv_taps": normal_values(arg_keys[1], (C, KW), 0.6, 3.0, ((0, 16),), jnp.float32),
        "dilation_level": draw_dilation_level(jax.random.fold_in(arg_keys[8], 71), part),
        "pointwise_matrix": normal_values(arg_keys[3], (C, C), C ** -0.5, 0.15625, ((0, 2), (1, 8))),
        "head_weight": normal_values(arg_keys[4], (C, TR), TR ** -0.5, 0.078125, ((0, 8), (1, 2))),
        "pred_error": normal_values(part_keys[5], (LENGTH, TR), 1.0, 6.0, ((0, 8), (1, 2))),
        "tail_mask": with_ends((jax.random.randint(part_keys[6], (LENGTH, TR), 0, 3) < 1).astype(jnp.int32), jax.random.fold_in(part_keys[6], 1), 0, 1),
        "track_scale": jnp.clip(jnp.exp(math.log(2.0) - 1.3862944 * jax.random.uniform(arg_keys[7], (TR,), jnp.float32) ** level_of(arg_keys[7], (TR,), ((0, 2),), -0.2, 0.2)), 0.5, 2.0),
    }


root_half = 0.7071067811865476
norm_const = 0.3989422804014327

def gelu_slope(value):
    return 0.5 * (1.0 + jax.scipy.special.erf(value * root_half)) + value * norm_const * jnp.exp(-0.5 * value * value)

def taps_at(buffer, onehot, margin, sign):
    width_own = buffer.shape[1] - 2 * margin
    result = jnp.zeros((buffer.shape[0], width_own), jnp.float32)
    for level_index in range(onehot.shape[1]):
        receptive_span = BASE_DILATION * 2 ** level_index
        begin = margin + sign * receptive_span
        result = result + onehot[:, level_index:level_index + 1] * buffer[:, begin:begin + width_own]
    return result

def spread(values, onehot, margin, sign):
    result = jnp.zeros((values.shape[0], values.shape[1] + 2 * margin), jnp.float32)
    for level_index in range(onehot.shape[1]):
        receptive_span = BASE_DILATION * 2 ** level_index
        placed = onehot[:, level_index:level_index + 1] * values
        result = result + jnp.pad(placed, ((0, 0), (margin + sign * receptive_span, margin - sign * receptive_span)))
    return result

def channel_grads(buffer, hidden_grad, taps, onehot, margin):
    width_own = buffer.shape[1] - 2 * margin
    minus_side = taps_at(buffer, onehot, margin, -1)
    center = buffer[:, margin:margin + width_own]
    plus_side = taps_at(buffer, onehot, margin, 1)
    pre_act = taps[:, 0:1] * minus_side + taps[:, 1:2] * center + taps[:, 2:3] * plus_side
    pre_grad = hidden_grad.astype(jnp.float32) * gelu_slope(pre_act)
    taps_part = jnp.stack([lax.optimization_barrier(jnp.sum(pre_grad * minus_side, axis=1)), lax.optimization_barrier(jnp.sum(pre_grad * center, axis=1)), lax.optimization_barrier(jnp.sum(pre_grad * plus_side, axis=1))], axis=1)
    contrib = spread(taps[:, 0:1] * pre_grad, onehot, margin, -1) + spread(taps[:, 2:3] * pre_grad, onehot, margin, 1)
    contrib = contrib + jnp.pad(taps[:, 1:2] * pre_grad, ((0, 0), (margin, margin)))
    return (contrib, taps_part)

def reference(section_input, conv_taps, dilation_level, pointwise_matrix, head_weight, pred_error, tail_mask, track_scale):
    blocks = LENGTH // ROWS

    def head_block(pair):
        errors, masks = pair
        adjoint = (masks.astype(jnp.float32) * track_scale[None, :] * errors.astype(jnp.float32)).astype(jnp.bfloat16)
        return lax.dot_general(head_weight, adjoint, (((1,), (1,)), ((), ())), preferred_element_type=jnp.float32)
    pieces = lax.map(head_block, (pred_error.reshape(blocks, ROWS, TR), tail_mask.reshape(blocks, ROWS, TR)))
    out_grad = jnp.transpose(pieces, (1, 0, 2)).reshape(C, LENGTH)
    hidden_grad = jnp.dot(pointwise_matrix, out_grad.astype(jnp.bfloat16), preferred_element_type=jnp.float32).astype(jnp.bfloat16)
    onehot = (dilation_level[:, None] == jnp.arange(DILATION_COUNT, dtype=jnp.int32)[None, :]).astype(jnp.float32)
    largest_span = BASE_DILATION * 2 ** (DILATION_COUNT - 1)
    groups_count = C // 128

    def conv_block(items):
        inputs, grads, taps, selector, upstream = items
        padded = jnp.pad(inputs.astype(jnp.float32), ((0, 0), (largest_span, largest_span)))
        contrib, taps_part = channel_grads(padded, grads, taps, selector, largest_span)
        conv_part = contrib[:, largest_span:largest_span + LENGTH]
        return ((upstream + conv_part).astype(jnp.bfloat16), taps_part)

    def regroup(array):
        return array.reshape((groups_count, 128) + array.shape[1:])
    grad_blocks, taps_blocks = lax.map(conv_block, (regroup(section_input), regroup(hidden_grad), regroup(conv_taps), regroup(onehot), regroup(out_grad)))
    scale = 1.0 / math.sqrt(LENGTH)
    return (grad_blocks.reshape(C, LENGTH), taps_blocks.reshape(C, KW) * scale)
```

```python
import functools
import math

import jax
import jax.numpy as jnp
from jax import lax
from jax.experimental import pallas as pl
from jax.experimental.pallas import tpu as pltpu
from jax.sharding import PartitionSpec as P

DILATION_COUNT = 5
BASE_DILATION = 32


root_half = 0.7071067811865476
norm_const = 0.3989422804014327


def gelu_slope(value):
    return 0.5 * (1.0 + jax.scipy.special.erf(value * root_half)) + value * norm_const * jnp.exp(
        -0.5 * value * value
    )


def taps_at(buffer, onehot, margin, sign):
    width_own = buffer.shape[1] - 2 * margin
    result = jnp.zeros((buffer.shape[0], width_own), jnp.float32)
    for level_index in range(onehot.shape[1]):
        receptive_span = BASE_DILATION * 2**level_index
        begin = margin + sign * receptive_span
        result = (
            result + onehot[:, level_index : level_index + 1] * buffer[:, begin : begin + width_own]
        )
    return result


def spread(values, onehot, margin, sign):
    result = jnp.zeros((values.shape[0], values.shape[1] + 2 * margin), jnp.float32)
    for level_index in range(onehot.shape[1]):
        receptive_span = BASE_DILATION * 2**level_index
        placed = onehot[:, level_index : level_index + 1] * values
        result = result + jnp.pad(
            placed, ((0, 0), (margin + sign * receptive_span, margin - sign * receptive_span))
        )
    return result


def channel_grads(buffer, hidden_grad, taps, onehot, margin):
    width_own = buffer.shape[1] - 2 * margin
    minus_side = taps_at(buffer, onehot, margin, -1)
    center = buffer[:, margin : margin + width_own]
    plus_side = taps_at(buffer, onehot, margin, 1)
    pre_act = taps[:, 0:1] * minus_side + taps[:, 1:2] * center + taps[:, 2:3] * plus_side
    pre_grad = hidden_grad.astype(jnp.float32) * gelu_slope(pre_act)
    taps_part = jnp.stack(
        [
            jnp.sum(pre_grad * minus_side, axis=1),
            jnp.sum(pre_grad * center, axis=1),
            jnp.sum(pre_grad * plus_side, axis=1),
        ],
        axis=1,
    )
    contrib = spread(taps[:, 0:1] * pre_grad, onehot, margin, -1) + spread(
        taps[:, 2:3] * pre_grad, onehot, margin, 1
    )
    contrib = contrib + jnp.pad(taps[:, 1:2] * pre_grad, ((0, 0), (margin, margin)))
    return (contrib, taps_part)


def local(
    section_input,
    conv_taps,
    dilation_level,
    pointwise_matrix,
    head_weight,
    pred_error,
    tail_mask,
    track_scale,
):
    own_channels = section_input.shape[0]
    own_rows = section_input.shape[1]
    adjoint = (
        tail_mask.astype(jnp.float32) * track_scale[None, :] * pred_error.astype(jnp.float32)
    ).astype(jnp.bfloat16)
    full_grad = lax.dot_general(
        lax.all_gather(head_weight, "seq", axis=0, tiled=True),
        adjoint,
        (((1,), (1,)), ((), ())),
        preferred_element_type=jnp.float32,
    )
    total = lax.psum(full_grad, "track")
    out_grad_b = total.astype(jnp.bfloat16)
    out_grad = lax.dynamic_slice_in_dim(
        total, lax.axis_index("track") * own_channels, own_channels, 0
    )
    hidden_grad = jnp.dot(
        lax.all_gather(pointwise_matrix, "seq", axis=1, tiled=True),
        out_grad_b,
        preferred_element_type=jnp.float32,
    ).astype(jnp.bfloat16)
    largest_span = BASE_DILATION * 2 ** (DILATION_COUNT - 1)
    scale = 1.0 / math.sqrt(own_rows * lax.axis_size("seq"))
    onehot = (
        dilation_level[:, None] == jnp.arange(DILATION_COUNT, dtype=jnp.int32)[None, :]
    ).astype(jnp.float32)
    owned_input, owned_grad = (
        lax.all_to_all(section_input, "seq", split_axis=0, concat_axis=1, tiled=True),
        lax.all_to_all(hidden_grad, "seq", split_axis=0, concat_axis=1, tiled=True),
    )
    padded = jnp.pad(owned_input.astype(jnp.float32), ((0, 0), (largest_span, largest_span)))
    contrib, taps_part = channel_grads(padded, owned_grad, conv_taps, onehot, largest_span)
    window = contrib[:, largest_span : largest_span + owned_input.shape[1]]
    conv_part = lax.all_to_all(window, "seq", split_axis=1, concat_axis=0, tiled=True)
    taps_grad = taps_part * scale
    input_grad = (out_grad + conv_part).astype(jnp.bfloat16)
    return (input_grad, taps_grad)


MESH = pl.DeviceIdType.MESH
CROSS = 2
PARTS = 6
ADJ_PARTS = 4
EARLY_PARTS = 2
P_PARTS = 3
STEP = 16
CHUNKS = 2


def fused_kernel(
    chain,
    sec,
    taps,
    level,
    pw,
    hw,
    err,
    mask,
    scale,
    out,
    tg,
    wb,
    ab,
    ev,
    mv,
    pb,
    gp,
    gr,
    ob,
    hs,
    hf,
    hx,
    xo,
    xh,
    go,
    gs,
    gh,
    fs,
    tile,
    tt,
    cols,
    sums,
    su,
    sv,
    ld_sem,
    w_send,
    w_recv,
    wy_send,
    wy_recv,
    p_send,
    p_recv,
    py_send,
    py_recv,
    a_send,
    a_recv,
    g_send,
    g_recv,
    x_send,
    x_recv,
    xz_send,
    xz_recv,
    t_send,
    t_recv,
    c_send,
    c_recv,
    gz_send,
    gz_recv,
    s_send,
    s_recv,
    f_send,
    f_recv,
):
    g = lax.axis_index("groups")
    s = lax.axis_index("seq")
    t = lax.axis_index("track")
    z = s // CROSS
    x = s % CROSS
    head_rows = hw.shape[0]
    half = head_rows // 2
    piece = half // PARTS
    tracks, own_rows = err.shape
    own = sec.shape[0]
    owned = own // (chain * CROSS)
    phalf = pw.shape[0] // 2
    step = tracks // ADJ_PARTS // 128 * 128
    cuts = [c * step for c in range(ADJ_PARTS)] + [tracks]
    pair_rows = CROSS * own_rows
    length = chain * pair_rows
    steps = chain - 1
    blocks = chain // CROSS
    slots = blocks * CROSS
    small = owned // CHUNKS

    sibling = (g, s, 1 - t)
    twin = (1 - g, s, t)
    across = (g, z * CROSS + 1 - x, t)
    has_up = z < chain - 1
    has_down = z > 0
    is_end = (z == 0) | (z == chain - 1)

    barrier = pltpu.get_barrier_semaphore()
    for device in (sibling, twin, across):
        pl.semaphore_signal(barrier, inc=1, device_id=device, device_id_type=MESH)

    @pl.when(has_up)
    def _():
        pl.semaphore_signal(barrier, inc=1, device_id=(g, s + CROSS, t), device_id_type=MESH)

    @pl.when(has_down)
    def _():
        pl.semaphore_signal(barrier, inc=1, device_id=(g, s - CROSS, t), device_id_type=MESH)

    own_w = pltpu.make_async_copy(
        hw, wb.at[pl.ds(pl.multiple_of(z * head_rows, 16), head_rows), :], ld_sem.at[0]
    )
    own_p = pltpu.make_async_copy(pw, pb.at[z], ld_sem.at[1])

    def block_rows(k, parity):
        return pl.ds(pl.multiple_of((CROSS * k + parity) * head_rows, 16), head_rows)

    def pair_lanes(which):
        return pl.ds(pl.multiple_of(which * own_rows, 128), own_rows)

    def kept_rows(k):
        return pl.ds(k * head_rows, head_rows)

    own_x = [
        pltpu.make_async_copy(
            sec.at[block_rows(k, x), :], xo.at[kept_rows(k), pair_lanes(x)], ld_sem.at[2 + k]
        )
        for k in range(blocks)
    ]
    loads = []
    for c in range(ADJ_PARTS):
        rows = pl.ds(cuts[c], cuts[c + 1] - cuts[c])
        at = 2 + blocks + 2 * c
        loads.append(
            (
                pltpu.make_async_copy(err.at[rows, :], ev.at[rows, :], ld_sem.at[at]),
                pltpu.make_async_copy(mask.at[rows, :], mv.at[rows, :], ld_sem.at[at + 1]),
            )
        )
    for first, second in loads:
        first.start()
        second.start()
    own_w.start()
    own_p.start()
    for k in range(blocks):
        own_x[k].start()

    def fill_part(c):
        loads[c][0].wait()
        loads[c][1].wait()

        def fill(begin, count):
            rows = pl.ds(begin, count)
            line = scale[rows].reshape(1, count)
            if count < 128:
                line = jnp.concatenate([line, jnp.zeros((1, 128 - count), jnp.float32)], axis=1)
            column = jnp.transpose(jnp.broadcast_to(line, (128, 128)))[:count]
            column = jnp.concatenate([column] * (own_rows // 128), axis=1)
            value = mv[rows, :].astype(jnp.float32) * column * ev[rows, :].astype(jnp.float32)
            ab[x, rows, :] = value.astype(jnp.bfloat16)

        def fill_step(i, carry):
            fill(pl.multiple_of(cuts[c] + i * 128, 128), 128)
            return carry

        whole, rest = divmod(cuts[c + 1] - cuts[c], 128)
        lax.fori_loop(0, whole, fill_step, 0)
        if rest:
            fill(cuts[c] + whole * 128, rest)

    for c in range(EARLY_PARTS):
        fill_part(c)

    pl.semaphore_wait(barrier, jnp.where(is_end, 4, 5))

    def w_rows(shard, c, which):
        return pl.ds(pl.multiple_of(shard * head_rows + which * half + c * piece, 16), piece)

    def w_hop(shard, c, src, toward, direction):
        slot = shard * PARTS + c
        return pltpu.make_async_remote_copy(
            src_ref=src,
            dst_ref=wb.at[w_rows(shard, c, g), :],
            send_sem=w_send.at[direction, slot],
            recv_sem=w_recv.at[slot],
            device_id=(g, toward * CROSS + x, t),
            device_id_type=MESH,
        )

    def w_swap(shard, c, which):
        slot = shard * PARTS + c
        block = wb.at[w_rows(shard, c, which), :]
        return pltpu.make_async_remote_copy(
            src_ref=block,
            dst_ref=block,
            send_sem=wy_send.at[slot],
            recv_sem=wy_recv.at[slot],
            device_id=twin,
            device_id_type=MESH,
        )

    p_piece = phalf // P_PARTS

    def p_rows(c, which):
        return pl.ds(pl.multiple_of(which * phalf + c * p_piece, 16), p_piece)

    def p_hop(shard, c, src, toward, direction):
        slot = shard * P_PARTS + c
        return pltpu.make_async_remote_copy(
            src_ref=src,
            dst_ref=pb.at[shard, p_rows(c, g), :],
            send_sem=p_send.at[direction, slot],
            recv_sem=p_recv.at[slot],
            device_id=(g, toward * CROSS + x, t),
            device_id_type=MESH,
        )

    def p_swap(shard, c, which):
        slot = shard * P_PARTS + c
        block = pb.at[shard, p_rows(c, which), :]
        return pltpu.make_async_remote_copy(
            src_ref=block,
            dst_ref=block,
            send_sem=py_send.at[slot],
            recv_sem=py_recv.at[slot],
            device_id=twin,
            device_id_type=MESH,
        )

    def own_piece(c):
        return hw.at[pl.ds(pl.multiple_of(g * half + c * piece, 16), piece), :]

    def a_copy(c, which):
        block = ab.at[which, pl.ds(cuts[c], cuts[c + 1] - cuts[c]), :]
        return pltpu.make_async_remote_copy(
            src_ref=block,
            dst_ref=block,
            send_sem=a_send.at[c],
            recv_sem=a_recv.at[c],
            device_id=across,
            device_id_type=MESH,
        )

    @pl.when(has_up)
    def _():
        for c in range(PARTS):
            w_hop(z, c, own_piece(c), z + 1, 0).start()

    @pl.when(has_down)
    def _():
        for c in range(PARTS):
            w_hop(z, c, own_piece(c), z - 1, 1).start()

    for c in range(EARLY_PARTS):
        a_copy(c, x).start()
    for c in range(EARLY_PARTS, ADJ_PARTS):
        fill_part(c)
        a_copy(c, x).start()

    @pl.when(has_up)
    def _():
        for c in range(P_PARTS):
            p_hop(z, c, pw.at[p_rows(c, g), :], z + 1, 0).start()

    @pl.when(has_down)
    def _():
        for c in range(P_PARTS):
            p_hop(z, c, pw.at[p_rows(c, g), :], z - 1, 1).start()

    below = z
    above = chain - 1 - z
    near = jnp.minimum(below, above)

    def order(j):
        jump = (j + 1) // 2
        alternate = jnp.where(j % 2 == 1, z - jump, z + jump)
        one_sided = jnp.where(above > below, z + (j - near), z - (j - near))
        return jnp.where(j <= 2 * near, alternate, one_sided)

    def shard_rows(shard):
        return pl.ds(pl.multiple_of(shard * head_rows, 16), head_rows)

    def g_copy(shard, xs):
        return pltpu.make_async_remote_copy(
            src_ref=gp.at[xs, shard_rows(shard), :],
            dst_ref=gr.at[xs, shard_rows(shard), :],
            send_sem=g_send.at[shard, xs],
            recv_sem=g_recv.at[shard, xs],
            device_id=sibling,
            device_id_type=MESH,
        )

    def head_dot(shard, xs):
        rows = shard_rows(shard)
        gp[xs, rows, :] = lax.dot_general(
            wb[rows, :],
            ab[xs],
            (((1,), (0,)), ((), ())),
            preferred_element_type=jnp.float32,
        )
        g_copy(shard, xs).start()

    def w_relay(e, carry):
        paired = (near >= 1) & (e < 2 * PARTS)
        j = jnp.where(paired, 1 + e % 2, e // PARTS + 1)
        c = jnp.where(paired, e // 2, e % PARTS)
        shard = order(j)
        block = wb.at[w_rows(shard, c, g), :]
        w_hop(shard, c, block, z, 0).wait_recv()

        @pl.when((shard < z) & has_up)
        def _():
            w_hop(shard, c, block, z + 1, 0).start()

        @pl.when((shard > z) & has_down)
        def _():
            w_hop(shard, c, block, z - 1, 1).start()

        w_swap(shard, c, g).start()
        return carry

    def wait_swaps(shard):
        def one(c, carry):
            w_swap(shard, c, 1 - g).wait_recv()
            return carry

        lax.fori_loop(0, PARTS, one, 0)

    def near_dot(j, carry):
        shard = order(j)
        wait_swaps(shard)
        head_dot(shard, x)
        return carry

    def p_relay(e, carry):
        shard = order(e // P_PARTS + 1)
        c = e % P_PARTS
        block = pb.at[shard, p_rows(c, g), :]
        p_hop(shard, c, block, z, 0).wait_recv()

        @pl.when((shard < z) & has_up)
        def _():
            p_hop(shard, c, block, z + 1, 0).start()

        @pl.when((shard > z) & has_down)
        def _():
            p_hop(shard, c, block, z - 1, 1).start()

        p_swap(shard, c, g).start()
        return carry

    def far_dot(j, carry):
        head_dot(order(j), 1 - x)
        return carry

    def x_copy(k, parity, which):
        return pltpu.make_async_remote_copy(
            src_ref=sec.at[block_rows(k, parity), :],
            dst_ref=xo.at[kept_rows(k), pair_lanes(which)],
            send_sem=x_send.at[k],
            recv_sem=x_recv.at[k],
            device_id=across,
            device_id_type=MESH,
        )

    def slot_rows(i):
        return pl.ds(pl.multiple_of(i * owned, 16), owned)

    def xz_copy(i, side, device):
        return pltpu.make_async_remote_copy(
            src_ref=xo.at[slot_rows(i), :],
            dst_ref=xh.at[side, slot_rows(i), :],
            send_sem=xz_send.at[side, i],
            recv_sem=xz_recv.at[side, i],
            device_id=(g, device, t),
            device_id_type=MESH,
        )

    def t_copy(to, slot):
        return pltpu.make_async_remote_copy(
            src_ref=tile,
            dst_ref=tt.at[slot],
            send_sem=t_send.at[to],
            recv_sem=t_recv.at[slot],
            device_id=(g, to * CROSS + z % CROSS, t),
            device_id_type=MESH,
        )

    own_w.wait()
    head_dot(z, x)

    tile[...] = jnp.zeros((8, 128), jnp.float32)
    tile[0:3, 0:owned] = taps[...]
    tile[3:4, 0:owned] = level[...].astype(jnp.float32)

    @pl.when(z == 0)
    def _():
        xh[0] = jnp.zeros(xh.shape[1:], jnp.bfloat16)
        gh[0] = jnp.zeros(gh.shape[1:], jnp.bfloat16)

    @pl.when(z == chain - 1)
    def _():
        xh[1] = jnp.zeros(xh.shape[1:], jnp.bfloat16)
        gh[1] = jnp.zeros(gh.shape[1:], jnp.bfloat16)

    for i in range(slots):
        sums[i] = jnp.zeros((128, 128), jnp.float32)

    lax.fori_loop(0, (steps - 1) * PARTS, w_relay, 0)
    first = jnp.where(is_end, 2, 1)
    lax.fori_loop(1, first, near_dot, 0)
    lax.fori_loop((steps - 1) * PARTS, steps * PARTS, w_relay, 0)
    for k in range(blocks):
        x_copy(k, 1 - x, x).start()
    early_p = jnp.where(is_end, 1, steps)
    lax.fori_loop(0, early_p * P_PARTS, p_relay, 0)
    lax.fori_loop(first, steps, near_dot, 0)
    for c in range(ADJ_PARTS):
        a_copy(c, 1 - x).wait_recv()
    lax.fori_loop(0, steps, far_dot, 0)
    later_p = jnp.where(is_end, steps - 1, steps)
    lax.fori_loop(early_p * P_PARTS, later_p * P_PARTS, p_relay, 0)
    last = order(steps)
    wait_swaps(last)
    head_dot(last, x)
    head_dot(last, 1 - x)
    lax.fori_loop(later_p * P_PARTS, steps * P_PARTS, p_relay, 0)

    for k in range(blocks):
        own_x[k].wait()
        x_copy(k, x, 1 - x).wait_recv()

    def xz_start(i, carry):
        @pl.when(has_up)
        def _():
            xz_copy(i, 0, s + CROSS).start()

        @pl.when(has_down)
        def _():
            xz_copy(i, 1, s - CROSS).start()

        return carry

    lax.fori_loop(0, slots, xz_start, 0)

    my_slot = (z // CROSS) * CROSS + x
    in_column = z % CROSS == x

    def t_start(to, carry):
        @pl.when((to != z) | jnp.logical_not(in_column))
        def _():
            t_copy(to, my_slot).start()

        return carry

    lax.fori_loop(0, chain, t_start, 0)

    @pl.when(in_column)
    def _():
        tt[my_slot] = tile[...]

    def core_sum(j, carry):
        shard = order(j)
        rows = shard_rows(shard)
        for xs in range(CROSS):
            g_copy(shard, xs).wait_recv()
            ob[rows, xs * own_rows : (xs + 1) * own_rows] = (gp[xs, rows, :] + gr[xs, rows, :]).astype(
                jnp.bfloat16
            )
        return carry

    lax.fori_loop(0, chain, core_sum, 0)

    own_p.wait()

    def p_wait(j, carry):
        for c in range(P_PARTS):
            p_swap(order(j), c, 1 - g).wait_recv()
        return carry

    lax.fori_loop(1, steps + 1, p_wait, 0)

    per_block = head_rows // small
    chunks = blocks * per_block

    def c_copy(ch):
        k = ch // per_block
        begin = (1 - x) * head_rows + (ch % per_block) * small
        return pltpu.make_async_remote_copy(
            src_ref=hs.at[k, pl.ds(pl.multiple_of(begin, 16), small), :],
            dst_ref=hx.at[pl.ds(pl.multiple_of(ch * small, 16), small), :],
            send_sem=c_send.at[ch],
            recv_sem=c_recv.at[ch],
            device_id=across,
            device_id_type=MESH,
        )

    wide = CROSS * head_rows

    def h_step(k, carry):
        lanes = pl.ds(pl.multiple_of(k * wide, 128), wide)
        total = jnp.zeros((wide, pair_rows), jnp.float32)
        for shard in range(chain):
            total = total + lax.dot_general(
                pb[shard, :, lanes],
                ob[shard * head_rows : (shard + 1) * head_rows, :],
                (((0,), (0,)), ((), ())),
                preferred_element_type=jnp.float32,
            )
        hs[k] = total.astype(jnp.bfloat16)
        hf[k] = total

        def c_start(u, inner):
            c_copy(k * per_block + u).start()
            return inner

        lax.fori_loop(0, per_block, c_start, 0)
        return carry

    lax.fori_loop(0, blocks, h_step, 0)

    norm = 1.0 / math.sqrt(length)

    def t_wait(i, carry):
        @pl.when(jnp.logical_not(in_column) | (i != my_slot))
        def _():
            t_copy(0, i).wait_recv()

        padded = jnp.concatenate([tt[i], jnp.zeros((120, 128), jnp.float32)], axis=0)
        cols[i] = jnp.transpose(padded)
        return carry

    lax.fori_loop(0, slots, t_wait, 0)

    def moved(left, here, right, lev, sign):
        result = None
        for k in range(DILATION_COUNT):
            reach = BASE_DILATION * 2**k
            if sign < 0:
                if reach % 128 == 0:
                    value = (
                        left
                        if reach == pair_rows
                        else jnp.concatenate([left[:, pair_rows - reach :], here[:, : pair_rows - reach]], axis=1)
                    )
                else:
                    joined = jnp.concatenate([left[:, pair_rows - 128 :], here], axis=1)
                    value = pltpu.roll(joined, reach, 1)[:, 128:]
            else:
                if reach % 128 == 0:
                    value = (
                        right
                        if reach == pair_rows
                        else jnp.concatenate([here[:, reach:], right[:, :reach]], axis=1)
                    )
                else:
                    joined = jnp.concatenate([here, right[:, :128]], axis=1)
                    value = pltpu.roll(joined, pair_rows + 128 - reach, 1)[:, :pair_rows]
            result = value if result is None else jnp.where(lev == float(k), value, result)
        return result

    def gz_copy(ch, side, device):
        rows = pl.ds(pl.multiple_of(ch * small, 16), small)
        return pltpu.make_async_remote_copy(
            src_ref=gs.at[rows, :],
            dst_ref=gh.at[side, rows, :],
            send_sem=gz_send.at[side, ch],
            recv_sem=gz_recv.at[side, ch],
            device_id=(g, device, t),
            device_id_type=MESH,
        )

    def conv_rows(row):
        i = row // owned
        rows = pl.ds(pl.multiple_of(row, STEP), STEP)
        within = pl.ds(pl.multiple_of(row % owned, STEP), STEP)
        lev = cols[i, within, 3:4]
        tap = cols[i, within, 0:3]
        left = xh[0, rows, :].astype(jnp.float32)
        center = xo[rows, :].astype(jnp.float32)
        right = xh[1, rows, :].astype(jnp.float32)
        minus = moved(left, center, right, lev, -1)
        plus = moved(left, center, right, lev, 1)
        pre_act = tap[:, 0:1] * minus + tap[:, 1:2] * center + tap[:, 2:3] * plus
        mine = pl.ds(pl.multiple_of(x * head_rows + row % head_rows, STEP), STEP)
        hidden = (hf[row // head_rows, mine, :] + hx[rows, :].astype(jnp.float32)).astype(jnp.bfloat16)
        pre_grad = hidden.astype(jnp.float32) * gelu_slope(pre_act)
        go[rows, :] = pre_grad
        gs[rows, :] = pre_grad.astype(jnp.bfloat16)
        sums[i, within, 0:1] = jnp.sum(pre_grad * minus, axis=1, keepdims=True)
        sums[i, within, 1:2] = jnp.sum(pre_grad * center, axis=1, keepdims=True)
        sums[i, within, 2:3] = jnp.sum(pre_grad * plus, axis=1, keepdims=True)

    def conv_chunk(ch, carry):
        c_copy(ch).wait_recv()

        @pl.when((ch % CHUNKS == 0) & has_down)
        def _():
            xz_copy(ch // CHUNKS, 0, s).wait_recv()

        @pl.when((ch % CHUNKS == 0) & has_up)
        def _():
            xz_copy(ch // CHUNKS, 1, s).wait_recv()

        def one(i, inner):
            conv_rows(ch * small + i * STEP)
            return inner

        lax.fori_loop(0, small // STEP, one, 0)

        @pl.when(has_up)
        def _():
            gz_copy(ch, 0, s + CROSS).start()

        @pl.when(has_down)
        def _():
            gz_copy(ch, 1, s - CROSS).start()

        return carry

    lax.fori_loop(0, chunks, conv_chunk, 0)

    def s_copy(i, frm):
        return pltpu.make_async_remote_copy(
            src_ref=su.at[i],
            dst_ref=sv.at[frm],
            send_sem=s_send.at[i],
            recv_sem=s_recv.at[frm],
            device_id=(g, (i // CROSS * CROSS + x) * CROSS + i % CROSS, t),
            device_id_type=MESH,
        )

    def s_mine(i):
        return in_column & (i == my_slot)

    def s_start(i, carry):
        su[i] = jnp.transpose(sums[i])[0:8]

        @pl.when(jnp.logical_not(s_mine(i)))
        def _():
            s_copy(i, z).start()

        return carry

    lax.fori_loop(0, slots, s_start, 0)

    @pl.when(in_column)
    def _():
        sv[z] = su[my_slot]

    def out_rows(ch):
        begin = (ch // per_block * CROSS + x) * head_rows + ch % per_block * small
        return pl.ds(pl.multiple_of(begin, 16), small)

    def f_copy(ch, rows):
        return pltpu.make_async_remote_copy(
            src_ref=fs.at[pl.ds(pl.multiple_of(ch * small, 16), small), :],
            dst_ref=out.at[rows, :],
            send_sem=f_send.at[ch],
            recv_sem=f_recv.at[ch],
            device_id=across,
            device_id_type=MESH,
        )

    def final_rows(row):
        i = row // owned
        k = row // head_rows
        rows = pl.ds(pl.multiple_of(row, STEP), STEP)
        within = pl.ds(pl.multiple_of(row % owned, STEP), STEP)
        lev = cols[i, within, 3:4]
        tap = cols[i, within, 0:3]
        left = gh[0, rows, :].astype(jnp.float32)
        here = go[rows, :]
        right = gh[1, rows, :].astype(jnp.float32)
        part = (
            tap[:, 0:1] * moved(left, here, right, lev, 1)
            + tap[:, 1:2] * here
            + tap[:, 2:3] * moved(left, here, right, lev, -1)
        )
        begin = (t * blocks + k) * head_rows + row % head_rows
        up = pl.ds(pl.multiple_of(begin, STEP), STEP)
        whole = jnp.concatenate([gp[xs, up, :] + gr[xs, up, :] for xs in range(CROSS)], axis=1)
        value = (whole + part).astype(jnp.bfloat16)
        begin = (k * CROSS + x) * head_rows + row % head_rows
        low, high = value[:, :own_rows], value[:, own_rows:]

        @pl.when(x == 0)
        def _():
            out[pl.ds(pl.multiple_of(begin, STEP), STEP), :] = low
            fs[rows, :] = high

        @pl.when(x != 0)
        def _():
            out[pl.ds(pl.multiple_of(begin, STEP), STEP), :] = high
            fs[rows, :] = low

    def final_chunk(ch, carry):
        @pl.when(has_down)
        def _():
            gz_copy(ch, 0, s).wait_recv()

        @pl.when(has_up)
        def _():
            gz_copy(ch, 1, s).wait_recv()

        def one(i, inner):
            final_rows(ch * small + i * STEP)
            return inner

        lax.fori_loop(0, small // STEP, one, 0)
        f_copy(ch, out_rows(ch)).start()
        return carry

    lax.fori_loop(0, chunks, final_chunk, 0)

    def s_wait(frm, carry):
        @pl.when(jnp.logical_not(in_column) | (frm != z))
        def _():
            s_copy(0, frm).wait_recv()

        return carry

    lax.fori_loop(0, chain, s_wait, 0)
    total = sv[0]
    for frm in range(1, chain):
        total = total + sv[frm]
    tg[...] = total[0:3, 0:owned] * norm

    def w_done(shard, carry):
        def one(c, inner):
            block = wb.at[w_rows(shard, c, g), :]

            @pl.when((shard <= z) & has_up)
            def _():
                w_hop(shard, c, block, z, 0).wait_send()

            @pl.when((shard >= z) & has_down)
            def _():
                w_hop(shard, c, block, z, 1).wait_send()

            @pl.when(shard != z)
            def _():
                w_swap(shard, c, g).wait_send()

            return inner

        lax.fori_loop(0, PARTS, one, 0)

        def p_one(c, inner):
            block = pb.at[shard, p_rows(c, g), :]

            @pl.when((shard <= z) & has_up)
            def _():
                p_hop(shard, c, block, z, 0).wait_send()

            @pl.when((shard >= z) & has_down)
            def _():
                p_hop(shard, c, block, z, 1).wait_send()

            @pl.when(shard != z)
            def _():
                p_swap(shard, c, g).wait_send()

            return inner

        lax.fori_loop(0, P_PARTS, p_one, 0)
        for xs in range(CROSS):
            g_copy(shard, xs).wait_send()

        @pl.when((shard != z) | jnp.logical_not(in_column))
        def _():
            t_copy(shard, 0).wait_send()

        return carry

    lax.fori_loop(0, chain, w_done, 0)

    for c in range(ADJ_PARTS):
        a_copy(c, x).wait_send()
    for k in range(blocks):
        x_copy(k, 1 - x, x).wait_send()

    def slot_done(i, carry):
        @pl.when(has_up)
        def _():
            xz_copy(i, 0, s).wait_send()

        @pl.when(has_down)
        def _():
            xz_copy(i, 1, s).wait_send()

        @pl.when(jnp.logical_not(s_mine(i)))
        def _():
            s_copy(i, z).wait_send()

        return carry

    lax.fori_loop(0, slots, slot_done, 0)

    def chunk_done(ch, carry):
        c_copy(ch).wait_send()

        @pl.when(has_up)
        def _():
            gz_copy(ch, 0, s).wait_send()

        @pl.when(has_down)
        def _():
            gz_copy(ch, 1, s).wait_send()

        f_copy(ch, out_rows(ch)).wait()
        return carry

    lax.fori_loop(0, chunks, chunk_done, 0)


def fused(
    chain,
    section_input,
    conv_taps,
    dilation_level,
    pointwise_matrix,
    head_weight,
    pred_error,
    tail_mask,
    track_scale,
):
    own, own_rows = section_input.shape
    owned = own // (chain * CROSS)
    head_rows, tracks = head_weight.shape
    pair_rows = CROSS * own_rows
    cols = pointwise_matrix.shape[1]
    blocks = chain // CROSS
    slots = blocks * CROSS
    chunks = slots * CHUNKS
    kept = blocks * head_rows
    bf16, f32 = jnp.bfloat16, jnp.float32
    dma = pltpu.SemaphoreType.DMA
    anywhere = pl.BlockSpec(memory_space=pltpu.HBM)
    vmem = pl.BlockSpec(memory_space=pltpu.VMEM)
    input_grad, taps_grad = pl.pallas_call(
        functools.partial(fused_kernel, chain),
        out_shape=(
            jax.ShapeDtypeStruct((own, own_rows), bf16),
            jax.ShapeDtypeStruct((3, owned), f32),
        ),
        in_specs=[anywhere, vmem, vmem, anywhere, anywhere, anywhere, anywhere, vmem],
        out_specs=(vmem, vmem),
        scratch_shapes=[
            pltpu.VMEM((chain * head_rows, tracks), bf16),
            pltpu.VMEM((CROSS, tracks, own_rows), bf16),
            pltpu.VMEM((tracks, own_rows), bf16),
            pltpu.VMEM((tracks, own_rows), jnp.int32),
            pltpu.VMEM((chain, cols, own), bf16),
            pltpu.VMEM((CROSS, chain * head_rows, own_rows), f32),
            pltpu.VMEM((CROSS, chain * head_rows, own_rows), f32),
            pltpu.VMEM((chain * head_rows, pair_rows), bf16),
            pltpu.VMEM((blocks, CROSS * head_rows, pair_rows), bf16),
            pltpu.VMEM((blocks, CROSS * head_rows, pair_rows), f32),
            pltpu.VMEM((kept, pair_rows), bf16),
            pltpu.VMEM((kept, pair_rows), bf16),
            pltpu.VMEM((2, kept, pair_rows), bf16),
            pltpu.VMEM((kept, pair_rows), f32),
            pltpu.VMEM((kept, pair_rows), bf16),
            pltpu.VMEM((2, kept, pair_rows), bf16),
            pltpu.VMEM((kept, own_rows), bf16),
            pltpu.VMEM((8, 128), f32),
            pltpu.VMEM((slots, 8, 128), f32),
            pltpu.VMEM((slots, 128, 128), f32),
            pltpu.VMEM((slots, 128, 128), f32),
            pltpu.VMEM((slots, 8, 128), f32),
            pltpu.VMEM((chain, 8, 128), f32),
            dma((2 + blocks + 2 * ADJ_PARTS,)),
            dma((2, chain * PARTS)),
            dma((chain * PARTS,)),
            dma((chain * PARTS,)),
            dma((chain * PARTS,)),
            dma((2, chain * P_PARTS)),
            dma((chain * P_PARTS,)),
            dma((chain * P_PARTS,)),
            dma((chain * P_PARTS,)),
            dma((ADJ_PARTS,)),
            dma((ADJ_PARTS,)),
            dma((chain, CROSS)),
            dma((chain, CROSS)),
            dma((blocks,)),
            dma((blocks,)),
            dma((2, slots)),
            dma((2, slots)),
            dma((chain,)),
            dma((slots,)),
            dma((chunks,)),
            dma((chunks,)),
            dma((2, chunks)),
            dma((2, chunks)),
            dma((slots,)),
            dma((chain,)),
            dma((chunks,)),
            dma((chunks,)),
        ],
        compiler_params=pltpu.CompilerParams(
            collective_id=0, has_side_effects=True, vmem_limit_bytes=63 * 1024 * 1024
        ),
        name="fused_section",
    )(
        section_input,
        conv_taps.T,
        dilation_level[None, :],
        pointwise_matrix.T,
        head_weight,
        pred_error.T,
        tail_mask.T,
        track_scale,
    )
    return input_grad, taps_grad.T


def local_or_fused(sizes, *args):
    section_input, head_weight, pred_error = args[0], args[4], args[5]
    seq = sizes["seq"]
    own, own_rows = section_input.shape
    fits = (
        sizes["groups"] == 2
        and sizes["track"] == 2
        and seq == 8
        and head_weight.shape[0] % (2 * PARTS * 16) == 0
        and own % (seq * 16 * CHUNKS) == 0
        and own_rows % 128 == 0
        and CROSS * own_rows == BASE_DILATION * 2 ** (DILATION_COUNT - 1)
        and pred_error.shape[1] % 16 == 0
        and pred_error.shape[1] >= 128 * ADJ_PARTS
        and args[3].shape[1] % (2 * P_PARTS * 16) == 0
        and own // seq <= 128
        and head_weight.shape[0] * 4 == own
        and own // 2 % 128 == 0
    )
    if fits:
        return fused(seq // CROSS, *args)
    return local(*args)


def solution(mesh):
    in_specs = (
        P("track", ("groups", "seq")),
        P(("track", "seq"), None),
        P(("track", "seq")),
        P("track", "seq"),
        P("seq", "track"),
        P(("groups", "seq"), "track"),
        P(("groups", "seq"), "track"),
        P("track"),
    )
    sizes = dict(mesh.shape)
    body = functools.partial(local_or_fused, sizes)
    out_specs = (P("track", ("groups", "seq")), P(("groups", "track", "seq"), None))
    return jax.shard_map(body, mesh=mesh, in_specs=in_specs, out_specs=out_specs, check_vma=False)
```

```python
import functools
import math

import jax
import jax.numpy as jnp
from jax import lax
from jax.experimental import pallas as pl
from jax.experimental.pallas import tpu as pltpu
from jax.sharding import PartitionSpec as P

DILATION_COUNT = 5
BASE_DILATION = 32


root_half = 0.7071067811865476
norm_const = 0.3989422804014327


def gelu_slope(value):
    return 0.5 * (1.0 + jax.scipy.special.erf(value * root_half)) + value * norm_const * jnp.exp(
        -0.5 * value * value
    )


def taps_at(buffer, onehot, margin, sign):
    width_own = buffer.shape[1] - 2 * margin
    result = jnp.zeros((buffer.shape[0], width_own), jnp.float32)
    for level_index in range(onehot.shape[1]):
        receptive_span = BASE_DILATION * 2**level_index
        begin = margin + sign * receptive_span
        result = (
            result + onehot[:, level_index : level_index + 1] * buffer[:, begin : begin + width_own]
        )
    return result


def spread(values, onehot, margin, sign):
    result = jnp.zeros((values.shape[0], values.shape[1] + 2 * margin), jnp.float32)
    for level_index in range(onehot.shape[1]):
        receptive_span = BASE_DILATION * 2**level_index
        placed = onehot[:, level_index : level_index + 1] * values
        result = result + jnp.pad(
            placed, ((0, 0), (margin + sign * receptive_span, margin - sign * receptive_span))
        )
    return result


def channel_grads(buffer, hidden_grad, taps, onehot, margin):
    width_own = buffer.shape[1] - 2 * margin
    minus_side = taps_at(buffer, onehot, margin, -1)
    center = buffer[:, margin : margin + width_own]
    plus_side = taps_at(buffer, onehot, margin, 1)
    pre_act = taps[:, 0:1] * minus_side + taps[:, 1:2] * center + taps[:, 2:3] * plus_side
    pre_grad = hidden_grad.astype(jnp.float32) * gelu_slope(pre_act)
    taps_part = jnp.stack(
        [
            jnp.sum(pre_grad * minus_side, axis=1),
            jnp.sum(pre_grad * center, axis=1),
            jnp.sum(pre_grad * plus_side, axis=1),
        ],
        axis=1,
    )
    contrib = spread(taps[:, 0:1] * pre_grad, onehot, margin, -1) + spread(
        taps[:, 2:3] * pre_grad, onehot, margin, 1
    )
    contrib = contrib + jnp.pad(taps[:, 1:2] * pre_grad, ((0, 0), (margin, margin)))
    return (contrib, taps_part)


def local(
    section_input,
    conv_taps,
    dilation_level,
    pointwise_matrix,
    head_weight,
    pred_error,
    tail_mask,
    track_scale,
):
    own_channels = section_input.shape[0]
    own_rows = section_input.shape[1]
    adjoint = (
        tail_mask.astype(jnp.float32) * track_scale[None, :] * pred_error.astype(jnp.float32)
    ).astype(jnp.bfloat16)
    full_grad = lax.dot_general(
        lax.all_gather(head_weight, "seq", axis=0, tiled=True),
        adjoint,
        (((1,), (1,)), ((), ())),
        preferred_element_type=jnp.float32,
    )
    total = lax.psum(full_grad, "track")
    out_grad_b = total.astype(jnp.bfloat16)
    out_grad = lax.dynamic_slice_in_dim(
        total, lax.axis_index("track") * own_channels, own_channels, 0
    )
    hidden_grad = jnp.dot(
        lax.all_gather(pointwise_matrix, "seq", axis=1, tiled=True),
        out_grad_b,
        preferred_element_type=jnp.float32,
    ).astype(jnp.bfloat16)
    largest_span = BASE_DILATION * 2 ** (DILATION_COUNT - 1)
    scale = 1.0 / math.sqrt(own_rows * lax.axis_size("seq"))
    onehot = (
        dilation_level[:, None] == jnp.arange(DILATION_COUNT, dtype=jnp.int32)[None, :]
    ).astype(jnp.float32)
    owned_input, owned_grad = (
        lax.all_to_all(section_input, "seq", split_axis=0, concat_axis=1, tiled=True),
        lax.all_to_all(hidden_grad, "seq", split_axis=0, concat_axis=1, tiled=True),
    )
    padded = jnp.pad(owned_input.astype(jnp.float32), ((0, 0), (largest_span, largest_span)))
    contrib, taps_part = channel_grads(padded, owned_grad, conv_taps, onehot, largest_span)
    window = contrib[:, largest_span : largest_span + owned_input.shape[1]]
    conv_part = lax.all_to_all(window, "seq", split_axis=1, concat_axis=0, tiled=True)
    taps_grad = taps_part * scale
    input_grad = (out_grad + conv_part).astype(jnp.bfloat16)
    return (input_grad, taps_grad)


MESH = pl.DeviceIdType.MESH
CROSS = 2
PARTS = 6
ADJ_PARTS = 4
EARLY_PARTS = 2
STEP = 16
CHUNKS = 2


def fused_kernel(
    chain,
    sec,
    taps,
    level,
    pw,
    hw,
    err,
    mask,
    scale,
    out,
    tg,
    wb,
    ab,
    ev,
    mv,
    pb,
    gp,
    gr,
    ob,
    hs,
    hf,
    hx,
    xo,
    xh,
    go,
    gs,
    gh,
    fs,
    tile,
    tt,
    cols,
    sums,
    su,
    sv,
    ld_sem,
    w_send,
    w_recv,
    wy_send,
    wy_recv,
    p_send,
    p_recv,
    py_send,
    py_recv,
    a_send,
    a_recv,
    g_send,
    g_recv,
    x_send,
    x_recv,
    xz_send,
    xz_recv,
    u_send,
    u_recv,
    t_send,
    t_recv,
    c_send,
    c_recv,
    gz_send,
    gz_recv,
    s_send,
    s_recv,
    f_send,
    f_recv,
):
    g = lax.axis_index("groups")
    s = lax.axis_index("seq")
    t = lax.axis_index("track")
    z = s // CROSS
    x = s % CROSS
    head_rows = hw.shape[0]
    half = head_rows // 2
    piece = half // PARTS
    tracks, own_rows = err.shape
    own = sec.shape[0]
    owned = own // (chain * CROSS)
    phalf = pw.shape[0] // 2
    step = tracks // ADJ_PARTS // 128 * 128
    cuts = [c * step for c in range(ADJ_PARTS)] + [tracks]
    pair_rows = CROSS * own_rows
    length = chain * pair_rows
    steps = chain - 1
    blocks = chain // CROSS
    slots = blocks * CROSS
    small = owned // CHUNKS

    sibling = (g, s, 1 - t)
    twin = (1 - g, s, t)
    across = (g, z * CROSS + 1 - x, t)
    has_up = z < chain - 1
    has_down = z > 0
    is_end = (z == 0) | (z == chain - 1)

    barrier = pltpu.get_barrier_semaphore()
    for device in (sibling, twin, across):
        pl.semaphore_signal(barrier, inc=1, device_id=device, device_id_type=MESH)

    @pl.when(has_up)
    def _():
        pl.semaphore_signal(barrier, inc=1, device_id=(g, s + CROSS, t), device_id_type=MESH)

    @pl.when(has_down)
    def _():
        pl.semaphore_signal(barrier, inc=1, device_id=(g, s - CROSS, t), device_id_type=MESH)

    own_w = pltpu.make_async_copy(
        hw, wb.at[pl.ds(pl.multiple_of(z * head_rows, 16), head_rows), :], ld_sem.at[0]
    )
    own_p = pltpu.make_async_copy(pw, pb.at[z], ld_sem.at[1])

    def block_rows(k, parity):
        return pl.ds(pl.multiple_of((CROSS * k + parity) * head_rows, 16), head_rows)

    def pair_lanes(which):
        return pl.ds(pl.multiple_of(which * own_rows, 128), own_rows)

    def kept_rows(k):
        return pl.ds(k * head_rows, head_rows)

    own_x = [
        pltpu.make_async_copy(
            sec.at[block_rows(k, x), :], xo.at[kept_rows(k), pair_lanes(x)], ld_sem.at[2 + k]
        )
        for k in range(blocks)
    ]
    loads = []
    for c in range(ADJ_PARTS):
        rows = pl.ds(cuts[c], cuts[c + 1] - cuts[c])
        at = 2 + blocks + 2 * c
        loads.append(
            (
                pltpu.make_async_copy(err.at[rows, :], ev.at[rows, :], ld_sem.at[at]),
                pltpu.make_async_copy(mask.at[rows, :], mv.at[rows, :], ld_sem.at[at + 1]),
            )
        )
    for first, second in loads:
        first.start()
        second.start()
    own_w.start()
    own_p.start()
    for k in range(blocks):
        own_x[k].start()

    def fill_part(c):
        loads[c][0].wait()
        loads[c][1].wait()

        def fill(begin, count):
            rows = pl.ds(begin, count)
            line = scale[rows].reshape(1, count)
            if count < 128:
                line = jnp.concatenate([line, jnp.zeros((1, 128 - count), jnp.float32)], axis=1)
            column = jnp.transpose(jnp.broadcast_to(line, (128, 128)))[:count]
            column = jnp.concatenate([column] * (own_rows // 128), axis=1)
            value = mv[rows, :].astype(jnp.float32) * column * ev[rows, :].astype(jnp.float32)
            ab[x, rows, :] = value.astype(jnp.bfloat16)

        def fill_step(i, carry):
            fill(pl.multiple_of(cuts[c] + i * 128, 128), 128)
            return carry

        whole, rest = divmod(cuts[c + 1] - cuts[c], 128)
        lax.fori_loop(0, whole, fill_step, 0)
        if rest:
            fill(cuts[c] + whole * 128, rest)

    for c in range(EARLY_PARTS):
        fill_part(c)

    pl.semaphore_wait(barrier, jnp.where(is_end, 4, 5))

    def w_rows(shard, c, which):
        return pl.ds(pl.multiple_of(shard * head_rows + which * half + c * piece, 16), piece)

    def w_hop(shard, c, src, toward, direction):
        slot = shard * PARTS + c
        return pltpu.make_async_remote_copy(
            src_ref=src,
            dst_ref=wb.at[w_rows(shard, c, g), :],
            send_sem=w_send.at[direction, slot],
            recv_sem=w_recv.at[slot],
            device_id=(g, toward * CROSS + x, t),
            device_id_type=MESH,
        )

    def w_swap(shard, c, which):
        slot = shard * PARTS + c
        block = wb.at[w_rows(shard, c, which), :]
        return pltpu.make_async_remote_copy(
            src_ref=block,
            dst_ref=block,
            send_sem=wy_send.at[slot],
            recv_sem=wy_recv.at[slot],
            device_id=twin,
            device_id_type=MESH,
        )

    p_parts = blocks
    wide = CROSS * head_rows

    def p_part(shard, c, which):
        rows = pl.ds(pl.multiple_of(which * phalf, 16), phalf)
        return pb.at[shard, rows, pl.ds(pl.multiple_of(c * wide, 128), wide)]

    def p_hop(shard, c, src, toward, direction):
        slot = shard * p_parts + c
        return pltpu.make_async_remote_copy(
            src_ref=src,
            dst_ref=p_part(shard, c, g),
            send_sem=p_send.at[direction, slot],
            recv_sem=p_recv.at[slot],
            device_id=(g, toward * CROSS + x, t),
            device_id_type=MESH,
        )

    def p_swap(shard, c, which):
        slot = shard * p_parts + c
        block = p_part(shard, c, which)
        return pltpu.make_async_remote_copy(
            src_ref=block,
            dst_ref=block,
            send_sem=py_send.at[slot],
            recv_sem=py_recv.at[slot],
            device_id=twin,
            device_id_type=MESH,
        )

    def own_piece(c):
        return hw.at[pl.ds(pl.multiple_of(g * half + c * piece, 16), piece), :]

    def a_copy(c, which):
        block = ab.at[which, pl.ds(cuts[c], cuts[c + 1] - cuts[c]), :]
        return pltpu.make_async_remote_copy(
            src_ref=block,
            dst_ref=block,
            send_sem=a_send.at[c],
            recv_sem=a_recv.at[c],
            device_id=across,
            device_id_type=MESH,
        )

    @pl.when(has_up)
    def _():
        for c in range(PARTS):
            w_hop(z, c, own_piece(c), z + 1, 0).start()

    @pl.when(has_down)
    def _():
        for c in range(PARTS):
            w_hop(z, c, own_piece(c), z - 1, 1).start()

    for c in range(EARLY_PARTS):
        a_copy(c, x).start()
    for c in range(EARLY_PARTS, ADJ_PARTS):
        fill_part(c)
        a_copy(c, x).start()

    def own_p_part(c):
        return pw.at[pl.ds(pl.multiple_of(g * phalf, 16), phalf), pl.ds(c * wide, wide)]

    def p_send_own(c):
        @pl.when(has_up)
        def _():
            p_hop(z, c, own_p_part(c), z + 1, 0).start()

        @pl.when(has_down)
        def _():
            p_hop(z, c, own_p_part(c), z - 1, 1).start()

    for c in range(p_parts):
        p_send_own(c)

    below = z
    above = chain - 1 - z
    near = jnp.minimum(below, above)

    def order(j):
        jump = (j + 1) // 2
        alternate = jnp.where(j % 2 == 1, z - jump, z + jump)
        one_sided = jnp.where(above > below, z + (j - near), z - (j - near))
        return jnp.where(j <= 2 * near, alternate, one_sided)

    def shard_rows(shard):
        return pl.ds(pl.multiple_of(shard * head_rows, 16), head_rows)

    def g_copy(shard, xs):
        return pltpu.make_async_remote_copy(
            src_ref=gp.at[xs, shard_rows(shard), :],
            dst_ref=gr.at[xs, shard_rows(shard), :],
            send_sem=g_send.at[shard, xs],
            recv_sem=g_recv.at[shard, xs],
            device_id=sibling,
            device_id_type=MESH,
        )

    def head_dot(shard, xs):
        rows = shard_rows(shard)
        gp[xs, rows, :] = lax.dot_general(
            wb[rows, :],
            ab[xs],
            (((1,), (0,)), ((), ())),
            preferred_element_type=jnp.float32,
        )
        g_copy(shard, xs).start()

    def w_relay(e, carry):
        paired = (near >= 1) & (e < 2 * PARTS)
        j = jnp.where(paired, 1 + e % 2, e // PARTS + 1)
        c = jnp.where(paired, e // 2, e % PARTS)
        shard = order(j)
        block = wb.at[w_rows(shard, c, g), :]
        w_hop(shard, c, block, z, 0).wait_recv()

        @pl.when((shard < z) & has_up)
        def _():
            w_hop(shard, c, block, z + 1, 0).start()

        @pl.when((shard > z) & has_down)
        def _():
            w_hop(shard, c, block, z - 1, 1).start()

        w_swap(shard, c, g).start()
        return carry

    def wait_swaps(shard):
        def one(c, carry):
            w_swap(shard, c, 1 - g).wait_recv()
            return carry

        lax.fori_loop(0, PARTS, one, 0)

    def near_dot(j, carry):
        shard = order(j)
        wait_swaps(shard)
        head_dot(shard, x)
        return carry

    def p_relay(e, carry):
        shard = order(e % steps + 1)
        c = e // steps
        block = p_part(shard, c, g)
        p_hop(shard, c, block, z, 0).wait_recv()

        @pl.when((shard < z) & has_up)
        def _():
            p_hop(shard, c, block, z + 1, 0).start()

        @pl.when((shard > z) & has_down)
        def _():
            p_hop(shard, c, block, z - 1, 1).start()

        p_swap(shard, c, g).start()
        return carry

    def far_dot(j, carry):
        head_dot(order(j), 1 - x)
        return carry

    def x_copy(k, parity, which):
        return pltpu.make_async_remote_copy(
            src_ref=sec.at[block_rows(k, parity), :],
            dst_ref=xo.at[kept_rows(k), pair_lanes(which)],
            send_sem=x_send.at[k],
            recv_sem=x_recv.at[k],
            device_id=across,
            device_id_type=MESH,
        )

    def slot_rows(i):
        return pl.ds(pl.multiple_of(i * owned, 16), owned)

    def xz_copy(i, side, device):
        return pltpu.make_async_remote_copy(
            src_ref=xo.at[slot_rows(i), :],
            dst_ref=xh.at[side, slot_rows(i), :],
            send_sem=xz_send.at[side, i],
            recv_sem=xz_recv.at[side, i],
            device_id=(g, device, t),
            device_id_type=MESH,
        )

    my_slot = (z // CROSS) * CROSS + x
    in_column = z % CROSS == x

    def u_copy(slot):
        return pltpu.make_async_remote_copy(
            src_ref=tile,
            dst_ref=tt.at[slot],
            send_sem=u_send,
            recv_sem=u_recv,
            device_id=across,
            device_id_type=MESH,
        )

    def t_copy(to, frm):
        pair = tt.at[pl.ds(frm // CROSS * CROSS, CROSS)]
        return pltpu.make_async_remote_copy(
            src_ref=pair,
            dst_ref=pair,
            send_sem=t_send.at[to],
            recv_sem=t_recv.at[frm],
            device_id=(g, to * CROSS + x, t),
            device_id_type=MESH,
        )

    own_w.wait()
    head_dot(z, x)

    tile[...] = jnp.zeros((8, 128), jnp.float32)
    tile[0:3, 0:owned] = taps[...]
    tile[3:4, 0:owned] = level[...].astype(jnp.float32)

    @pl.when(jnp.logical_not(in_column))
    def _():
        u_copy(my_slot).start()

    @pl.when(in_column)
    def _():
        tt[my_slot] = tile[...]

    @pl.when(z == 0)
    def _():
        xh[0] = jnp.zeros(xh.shape[1:], jnp.bfloat16)
        gh[0] = jnp.zeros(gh.shape[1:], jnp.bfloat16)

    @pl.when(z == chain - 1)
    def _():
        xh[1] = jnp.zeros(xh.shape[1:], jnp.bfloat16)
        gh[1] = jnp.zeros(gh.shape[1:], jnp.bfloat16)

    for i in range(slots):
        sums[i] = jnp.zeros((128, 128), jnp.float32)

    def end_relay(begin, end):
        lax.fori_loop(begin, jnp.where(is_end, end, begin), p_relay, 0)

    lax.fori_loop(0, PARTS, w_relay, 0)
    for c in range(p_parts):
        end_relay(c * steps, c * steps + 1)
    lax.fori_loop(PARTS, (steps - 1) * PARTS, w_relay, 0)
    first = jnp.where(is_end, 2, 1)
    lax.fori_loop(1, first, near_dot, 0)
    lax.fori_loop((steps - 1) * PARTS, steps * PARTS, w_relay, 0)

    @pl.when(in_column)
    def _():
        u_copy(my_slot).wait_recv()

        def t_start(j, carry):
            t_copy(order(j), z).start()
            return carry

        lax.fori_loop(1, chain, t_start, 0)

    for k in range(blocks):
        x_copy(k, 1 - x, x).start()

    lax.fori_loop(0, jnp.where(is_end, 0, p_parts * steps), p_relay, 0)
    lax.fori_loop(first, steps, near_dot, 0)
    for c in range(ADJ_PARTS):
        a_copy(c, 1 - x).wait_recv()
    lax.fori_loop(0, steps, far_dot, 0)
    end_relay(1, 2)
    last = order(steps)
    wait_swaps(last)
    head_dot(last, x)
    head_dot(last, 1 - x)
    end_relay(2, steps)

    for k in range(blocks):
        own_x[k].wait()
        x_copy(k, x, 1 - x).wait_recv()

    def xz_start(i, carry):
        @pl.when(has_up)
        def _():
            xz_copy(i, 0, s + CROSS).start()

        @pl.when(has_down)
        def _():
            xz_copy(i, 1, s - CROSS).start()

        return carry

    lax.fori_loop(0, slots, xz_start, 0)

    def core_sum(j, carry):
        shard = order(j)
        rows = shard_rows(shard)
        for xs in range(CROSS):
            g_copy(shard, xs).wait_recv()
            ob[rows, xs * own_rows : (xs + 1) * own_rows] = (gp[xs, rows, :] + gr[xs, rows, :]).astype(
                jnp.bfloat16
            )
        return carry

    lax.fori_loop(0, chain, core_sum, 0)

    own_p.wait()

    def p_wait(c):
        def one(j, carry):
            p_swap(order(j), c, 1 - g).wait_recv()
            return carry

        lax.fori_loop(1, steps + 1, one, 0)

    per_block = head_rows // small
    chunks = blocks * per_block

    def c_copy(ch):
        k = ch // per_block
        begin = (1 - x) * head_rows + (ch % per_block) * small
        return pltpu.make_async_remote_copy(
            src_ref=hs.at[k, pl.ds(pl.multiple_of(begin, 16), small), :],
            dst_ref=hx.at[pl.ds(pl.multiple_of(ch * small, 16), small), :],
            send_sem=c_send.at[ch],
            recv_sem=c_recv.at[ch],
            device_id=across,
            device_id_type=MESH,
        )

    def h_step(k, carry):
        lanes = pl.ds(pl.multiple_of(k * wide, 128), wide)
        total = jnp.zeros((wide, pair_rows), jnp.float32)
        for shard in range(chain):
            total = total + lax.dot_general(
                pb[shard, :, lanes],
                ob[shard * head_rows : (shard + 1) * head_rows, :],
                (((0,), (0,)), ((), ())),
                preferred_element_type=jnp.float32,
            )
        hs[k] = total.astype(jnp.bfloat16)
        hf[k] = total

        def c_start(u, inner):
            c_copy(k * per_block + u).start()
            return inner

        lax.fori_loop(0, per_block, c_start, 0)
        return carry

    end_relay(steps + 1, steps + 2)
    p_wait(0)
    h_step(0, 0)
    end_relay(steps + 2, blocks * steps)
    p_wait(1)
    h_step(1, 0)

    norm = 1.0 / math.sqrt(length)

    def t_wait(frm, carry):
        @pl.when((frm % CROSS == x) & (frm != z))
        def _():
            t_copy(0, frm).wait_recv()

        return carry

    lax.fori_loop(0, chain, t_wait, 0)
    for i in range(slots):
        padded = jnp.concatenate([tt[i], jnp.zeros((120, 128), jnp.float32)], axis=0)
        cols[i] = jnp.transpose(padded)

    def moved(left, here, right, lev, sign):
        result = None
        for k in range(DILATION_COUNT):
            reach = BASE_DILATION * 2**k
            if sign < 0:
                if reach % 128 == 0:
                    value = (
                        left
                        if reach == pair_rows
                        else jnp.concatenate([left[:, pair_rows - reach :], here[:, : pair_rows - reach]], axis=1)
                    )
                else:
                    joined = jnp.concatenate([left[:, pair_rows - 128 :], here], axis=1)
                    value = pltpu.roll(joined, reach, 1)[:, 128:]
            else:
                if reach % 128 == 0:
                    value = (
                        right
                        if reach == pair_rows
                        else jnp.concatenate([here[:, reach:], right[:, :reach]], axis=1)
                    )
                else:
                    joined = jnp.concatenate([here, right[:, :128]], axis=1)
                    value = pltpu.roll(joined, pair_rows + 128 - reach, 1)[:, :pair_rows]
            result = value if result is None else jnp.where(lev == float(k), value, result)
        return result

    def gz_copy(ch, side, device):
        rows = pl.ds(pl.multiple_of(ch * small, 16), small)
        return pltpu.make_async_remote_copy(
            src_ref=gs.at[rows, :],
            dst_ref=gh.at[side, rows, :],
            send_sem=gz_send.at[side, ch],
            recv_sem=gz_recv.at[side, ch],
            device_id=(g, device, t),
            device_id_type=MESH,
        )

    def conv_rows(row):
        i = row // owned
        rows = pl.ds(pl.multiple_of(row, STEP), STEP)
        within = pl.ds(pl.multiple_of(row % owned, STEP), STEP)
        lev = cols[i, within, 3:4]
        tap = cols[i, within, 0:3]
        left = xh[0, rows, :].astype(jnp.float32)
        center = xo[rows, :].astype(jnp.float32)
        right = xh[1, rows, :].astype(jnp.float32)
        minus = moved(left, center, right, lev, -1)
        plus = moved(left, center, right, lev, 1)
        pre_act = tap[:, 0:1] * minus + tap[:, 1:2] * center + tap[:, 2:3] * plus
        mine = pl.ds(pl.multiple_of(x * head_rows + row % head_rows, STEP), STEP)
        hidden = (hf[row // head_rows, mine, :] + hx[rows, :].astype(jnp.float32)).astype(jnp.bfloat16)
        pre_grad = hidden.astype(jnp.float32) * gelu_slope(pre_act)
        go[rows, :] = pre_grad
        gs[rows, :] = pre_grad.astype(jnp.bfloat16)
        sums[i, within, 0:1] = jnp.sum(pre_grad * minus, axis=1, keepdims=True)
        sums[i, within, 1:2] = jnp.sum(pre_grad * center, axis=1, keepdims=True)
        sums[i, within, 2:3] = jnp.sum(pre_grad * plus, axis=1, keepdims=True)

    def conv_chunk(ch, carry):
        c_copy(ch).wait_recv()

        @pl.when((ch % CHUNKS == 0) & has_down)
        def _():
            xz_copy(ch // CHUNKS, 0, s).wait_recv()

        @pl.when((ch % CHUNKS == 0) & has_up)
        def _():
            xz_copy(ch // CHUNKS, 1, s).wait_recv()

        def one(i, inner):
            conv_rows(ch * small + i * STEP)
            return inner

        lax.fori_loop(0, small // STEP, one, 0)

        @pl.when(has_up)
        def _():
            gz_copy(ch, 0, s + CROSS).start()

        @pl.when(has_down)
        def _():
            gz_copy(ch, 1, s - CROSS).start()

        return carry

    lax.fori_loop(0, chunks, conv_chunk, 0)

    def s_copy(i, frm):
        return pltpu.make_async_remote_copy(
            src_ref=su.at[i],
            dst_ref=sv.at[frm],
            send_sem=s_send.at[i],
            recv_sem=s_recv.at[frm],
            device_id=(g, (i // CROSS * CROSS + x) * CROSS + i % CROSS, t),
            device_id_type=MESH,
        )

    def s_mine(i):
        return in_column & (i == my_slot)

    def s_start(i, carry):
        su[i] = jnp.transpose(sums[i])[0:8]

        @pl.when(jnp.logical_not(s_mine(i)))
        def _():
            s_copy(i, z).start()

        return carry

    lax.fori_loop(0, slots, s_start, 0)

    @pl.when(in_column)
    def _():
        sv[z] = su[my_slot]

    def out_rows(ch):
        begin = (ch // per_block * CROSS + x) * head_rows + ch % per_block * small
        return pl.ds(pl.multiple_of(begin, 16), small)

    def f_copy(ch, rows):
        return pltpu.make_async_remote_copy(
            src_ref=fs.at[pl.ds(pl.multiple_of(ch * small, 16), small), :],
            dst_ref=out.at[rows, :],
            send_sem=f_send.at[ch],
            recv_sem=f_recv.at[ch],
            device_id=across,
            device_id_type=MESH,
        )

    def final_rows(row):
        i = row // owned
        k = row // head_rows
        rows = pl.ds(pl.multiple_of(row, STEP), STEP)
        within = pl.ds(pl.multiple_of(row % owned, STEP), STEP)
        lev = cols[i, within, 3:4]
        tap = cols[i, within, 0:3]
        left = gh[0, rows, :].astype(jnp.float32)
        here = go[rows, :]
        right = gh[1, rows, :].astype(jnp.float32)
        part = (
            tap[:, 0:1] * moved(left, here, right, lev, 1)
            + tap[:, 1:2] * here
            + tap[:, 2:3] * moved(left, here, right, lev, -1)
        )
        begin = (t * blocks + k) * head_rows + row % head_rows
        up = pl.ds(pl.multiple_of(begin, STEP), STEP)
        whole = jnp.concatenate([gp[xs, up, :] + gr[xs, up, :] for xs in range(CROSS)], axis=1)
        value = (whole + part).astype(jnp.bfloat16)
        begin = (k * CROSS + x) * head_rows + row % head_rows
        low, high = value[:, :own_rows], value[:, own_rows:]

        @pl.when(x == 0)
        def _():
            out[pl.ds(pl.multiple_of(begin, STEP), STEP), :] = low
            fs[rows, :] = high

        @pl.when(x != 0)
        def _():
            out[pl.ds(pl.multiple_of(begin, STEP), STEP), :] = high
            fs[rows, :] = low

    def final_chunk(ch, carry):
        @pl.when(has_down)
        def _():
            gz_copy(ch, 0, s).wait_recv()

        @pl.when(has_up)
        def _():
            gz_copy(ch, 1, s).wait_recv()

        def one(i, inner):
            final_rows(ch * small + i * STEP)
            return inner

        lax.fori_loop(0, small // STEP, one, 0)
        f_copy(ch, out_rows(ch)).start()
        return carry

    lax.fori_loop(0, chunks, final_chunk, 0)

    def s_wait(frm, carry):
        @pl.when(jnp.logical_not(in_column) | (frm != z))
        def _():
            s_copy(0, frm).wait_recv()

        return carry

    lax.fori_loop(0, chain, s_wait, 0)
    total = sv[0]
    for frm in range(1, chain):
        total = total + sv[frm]
    tg[...] = total[0:3, 0:owned] * norm

    def w_done(shard, carry):
        def one(c, inner):
            block = wb.at[w_rows(shard, c, g), :]

            @pl.when((shard <= z) & has_up)
            def _():
                w_hop(shard, c, block, z, 0).wait_send()

            @pl.when((shard >= z) & has_down)
            def _():
                w_hop(shard, c, block, z, 1).wait_send()

            @pl.when(shard != z)
            def _():
                w_swap(shard, c, g).wait_send()

            return inner

        lax.fori_loop(0, PARTS, one, 0)

        def p_one(c, inner):
            block = p_part(shard, c, g)

            @pl.when((shard <= z) & has_up)
            def _():
                p_hop(shard, c, block, z, 0).wait_send()

            @pl.when((shard >= z) & has_down)
            def _():
                p_hop(shard, c, block, z, 1).wait_send()

            @pl.when(shard != z)
            def _():
                p_swap(shard, c, g).wait_send()

            return inner

        lax.fori_loop(0, p_parts, p_one, 0)
        for xs in range(CROSS):
            g_copy(shard, xs).wait_send()

        @pl.when((shard != z) & in_column)
        def _():
            t_copy(shard, z).wait_send()

        return carry

    lax.fori_loop(0, chain, w_done, 0)

    @pl.when(jnp.logical_not(in_column))
    def _():
        u_copy(my_slot).wait_send()

    for c in range(ADJ_PARTS):
        a_copy(c, x).wait_send()
    for k in range(blocks):
        x_copy(k, 1 - x, x).wait_send()

    def slot_done(i, carry):
        @pl.when(has_up)
        def _():
            xz_copy(i, 0, s).wait_send()

        @pl.when(has_down)
        def _():
            xz_copy(i, 1, s).wait_send()

        @pl.when(jnp.logical_not(s_mine(i)))
        def _():
            s_copy(i, z).wait_send()

        return carry

    lax.fori_loop(0, slots, slot_done, 0)

    def chunk_done(ch, carry):
        c_copy(ch).wait_send()

        @pl.when(has_up)
        def _():
            gz_copy(ch, 0, s).wait_send()

        @pl.when(has_down)
        def _():
            gz_copy(ch, 1, s).wait_send()

        f_copy(ch, out_rows(ch)).wait()
        return carry

    lax.fori_loop(0, chunks, chunk_done, 0)


def hand_over(grad, taps, grad_out, taps_out):
    grad_out[...] = grad[...]
    taps_out[...] = taps[...]


def fused(
    chain,
    section_input,
    conv_taps,
    dilation_level,
    pointwise_matrix,
    head_weight,
    pred_error,
    tail_mask,
    track_scale,
):
    own, own_rows = section_input.shape
    owned = own // (chain * CROSS)
    head_rows, tracks = head_weight.shape
    pair_rows = CROSS * own_rows
    cols = pointwise_matrix.shape[1]
    blocks = chain // CROSS
    slots = blocks * CROSS
    chunks = slots * CHUNKS
    kept = blocks * head_rows
    bf16, f32 = jnp.bfloat16, jnp.float32
    dma = pltpu.SemaphoreType.DMA
    anywhere = pl.BlockSpec(memory_space=pltpu.HBM)
    vmem = pl.BlockSpec(memory_space=pltpu.VMEM)
    input_grad, taps_grad = pl.pallas_call(
        functools.partial(fused_kernel, chain),
        out_shape=(
            jax.ShapeDtypeStruct((own, own_rows), bf16),
            jax.ShapeDtypeStruct((3, owned), f32),
        ),
        in_specs=[anywhere, vmem, vmem, anywhere, anywhere, anywhere, anywhere, vmem],
        out_specs=(vmem, vmem),
        scratch_shapes=[
            pltpu.VMEM((chain * head_rows, tracks), bf16),
            pltpu.VMEM((CROSS, tracks, own_rows), bf16),
            pltpu.VMEM((tracks, own_rows), bf16),
            pltpu.VMEM((tracks, own_rows), jnp.int32),
            pltpu.VMEM((chain, cols, own), bf16),
            pltpu.VMEM((CROSS, chain * head_rows, own_rows), f32),
            pltpu.VMEM((CROSS, chain * head_rows, own_rows), f32),
            pltpu.VMEM((chain * head_rows, pair_rows), bf16),
            pltpu.VMEM((blocks, CROSS * head_rows, pair_rows), bf16),
            pltpu.VMEM((blocks, CROSS * head_rows, pair_rows), f32),
            pltpu.VMEM((kept, pair_rows), bf16),
            pltpu.VMEM((kept, pair_rows), bf16),
            pltpu.VMEM((2, kept, pair_rows), bf16),
            pltpu.VMEM((kept, pair_rows), f32),
            pltpu.VMEM((kept, pair_rows), bf16),
            pltpu.VMEM((2, kept, pair_rows), bf16),
            pltpu.VMEM((kept, own_rows), bf16),
            pltpu.VMEM((8, 128), f32),
            pltpu.VMEM((slots, 8, 128), f32),
            pltpu.VMEM((slots, 128, 128), f32),
            pltpu.VMEM((slots, 128, 128), f32),
            pltpu.VMEM((slots, 8, 128), f32),
            pltpu.VMEM((chain, 8, 128), f32),
            dma((2 + blocks + 2 * ADJ_PARTS,)),
            dma((2, chain * PARTS)),
            dma((chain * PARTS,)),
            dma((chain * PARTS,)),
            dma((chain * PARTS,)),
            dma((2, chain * blocks)),
            dma((chain * blocks,)),
            dma((chain * blocks,)),
            dma((chain * blocks,)),
            dma((ADJ_PARTS,)),
            dma((ADJ_PARTS,)),
            dma((chain, CROSS)),
            dma((chain, CROSS)),
            dma((blocks,)),
            dma((blocks,)),
            dma((2, slots)),
            dma((2, slots)),
            dma,
            dma,
            dma((chain,)),
            dma((chain,)),
            dma((chunks,)),
            dma((chunks,)),
            dma((2, chunks)),
            dma((2, chunks)),
            dma((slots,)),
            dma((chain,)),
            dma((chunks,)),
            dma((chunks,)),
        ],
        compiler_params=pltpu.CompilerParams(
            collective_id=0, has_side_effects=True, vmem_limit_bytes=63 * 1024 * 1024
        ),
        name="fused_section",
    )(
        section_input,
        conv_taps.T,
        dilation_level[None, :],
        pointwise_matrix.T,
        head_weight,
        pred_error.T,
        tail_mask.T,
        track_scale,
    )
    input_grad, taps_grad = pl.pallas_call(
        hand_over,
        out_shape=(
            jax.ShapeDtypeStruct((own, own_rows), bf16),
            jax.ShapeDtypeStruct((3, owned), f32),
        ),
        in_specs=[vmem, vmem],
        out_specs=(vmem, vmem),
        name="hand_over",
    )(input_grad, taps_grad)
    return input_grad, taps_grad.T


def local_or_fused(sizes, *args):
    section_input, head_weight, pred_error = args[0], args[4], args[5]
    seq = sizes["seq"]
    own, own_rows = section_input.shape
    fits = (
        sizes["groups"] == 2
        and sizes["track"] == 2
        and seq == 8
        and head_weight.shape[0] % (2 * PARTS * 16) == 0
        and own % (seq * 16 * CHUNKS) == 0
        and own_rows % 128 == 0
        and CROSS * own_rows == BASE_DILATION * 2 ** (DILATION_COUNT - 1)
        and pred_error.shape[1] % 16 == 0
        and pred_error.shape[1] >= 128 * ADJ_PARTS
        and args[3].shape[1] % 32 == 0
        and own // seq <= 128
        and head_weight.shape[0] * 4 == own
        and own // 2 % 128 == 0
    )
    if fits:
        return fused(seq // CROSS, *args)
    return local(*args)


def solution(mesh):
    in_specs = (
        P("track", ("groups", "seq")),
        P(("track", "seq"), None),
        P(("track", "seq")),
        P("track", "seq"),
        P("seq", "track"),
        P(("groups", "seq"), "track"),
        P(("groups", "seq"), "track"),
        P("track"),
    )
    sizes = dict(mesh.shape)
    body = functools.partial(local_or_fused, sizes)
    out_specs = (P("track", ("groups", "seq")), P(("groups", "track", "seq"), None))
    return jax.shard_map(body, mesh=mesh, in_specs=in_specs, out_specs=out_specs, check_vma=False)
```

```python
import functools
import math

import jax
import jax.numpy as jnp
from jax import lax
from jax.experimental import pallas as pl
from jax.experimental.pallas import tpu as pltpu
from jax.sharding import PartitionSpec as P

DILATION_COUNT = 5
BASE_DILATION = 32


root_half = 0.7071067811865476
norm_const = 0.3989422804014327


def gelu_slope(value):
    return 0.5 * (1.0 + jax.scipy.special.erf(value * root_half)) + value * norm_const * jnp.exp(
        -0.5 * value * value
    )


def taps_at(buffer, onehot, margin, sign):
    width_own = buffer.shape[1] - 2 * margin
    result = jnp.zeros((buffer.shape[0], width_own), jnp.float32)
    for level_index in range(onehot.shape[1]):
        receptive_span = BASE_DILATION * 2**level_index
        begin = margin + sign * receptive_span
        result = (
            result + onehot[:, level_index : level_index + 1] * buffer[:, begin : begin + width_own]
        )
    return result


def spread(values, onehot, margin, sign):
    result = jnp.zeros((values.shape[0], values.shape[1] + 2 * margin), jnp.float32)
    for level_index in range(onehot.shape[1]):
        receptive_span = BASE_DILATION * 2**level_index
        placed = onehot[:, level_index : level_index + 1] * values
        result = result + jnp.pad(
            placed, ((0, 0), (margin + sign * receptive_span, margin - sign * receptive_span))
        )
    return result


def channel_grads(buffer, hidden_grad, taps, onehot, margin):
    width_own = buffer.shape[1] - 2 * margin
    minus_side = taps_at(buffer, onehot, margin, -1)
    center = buffer[:, margin : margin + width_own]
    plus_side = taps_at(buffer, onehot, margin, 1)
    pre_act = taps[:, 0:1] * minus_side + taps[:, 1:2] * center + taps[:, 2:3] * plus_side
    pre_grad = hidden_grad.astype(jnp.float32) * gelu_slope(pre_act)
    taps_part = jnp.stack(
        [
            jnp.sum(pre_grad * minus_side, axis=1),
            jnp.sum(pre_grad * center, axis=1),
            jnp.sum(pre_grad * plus_side, axis=1),
        ],
        axis=1,
    )
    contrib = spread(taps[:, 0:1] * pre_grad, onehot, margin, -1) + spread(
        taps[:, 2:3] * pre_grad, onehot, margin, 1
    )
    contrib = contrib + jnp.pad(taps[:, 1:2] * pre_grad, ((0, 0), (margin, margin)))
    return (contrib, taps_part)


def local(
    section_input,
    conv_taps,
    dilation_level,
    pointwise_matrix,
    head_weight,
    pred_error,
    tail_mask,
    track_scale,
):
    own_channels = section_input.shape[0]
    own_rows = section_input.shape[1]
    adjoint = (
        tail_mask.astype(jnp.float32) * track_scale[None, :] * pred_error.astype(jnp.float32)
    ).astype(jnp.bfloat16)
    full_grad = lax.dot_general(
        lax.all_gather(head_weight, "seq", axis=0, tiled=True),
        adjoint,
        (((1,), (1,)), ((), ())),
        preferred_element_type=jnp.float32,
    )
    total = lax.psum(full_grad, "track")
    out_grad_b = total.astype(jnp.bfloat16)
    out_grad = lax.dynamic_slice_in_dim(
        total, lax.axis_index("track") * own_channels, own_channels, 0
    )
    hidden_grad = jnp.dot(
        lax.all_gather(pointwise_matrix, "seq", axis=1, tiled=True),
        out_grad_b,
        preferred_element_type=jnp.float32,
    ).astype(jnp.bfloat16)
    largest_span = BASE_DILATION * 2 ** (DILATION_COUNT - 1)
    scale = 1.0 / math.sqrt(own_rows * lax.axis_size("seq"))
    onehot = (
        dilation_level[:, None] == jnp.arange(DILATION_COUNT, dtype=jnp.int32)[None, :]
    ).astype(jnp.float32)
    owned_input, owned_grad = (
        lax.all_to_all(section_input, "seq", split_axis=0, concat_axis=1, tiled=True),
        lax.all_to_all(hidden_grad, "seq", split_axis=0, concat_axis=1, tiled=True),
    )
    padded = jnp.pad(owned_input.astype(jnp.float32), ((0, 0), (largest_span, largest_span)))
    contrib, taps_part = channel_grads(padded, owned_grad, conv_taps, onehot, largest_span)
    window = contrib[:, largest_span : largest_span + owned_input.shape[1]]
    conv_part = lax.all_to_all(window, "seq", split_axis=1, concat_axis=0, tiled=True)
    taps_grad = taps_part * scale
    input_grad = (out_grad + conv_part).astype(jnp.bfloat16)
    return (input_grad, taps_grad)


MESH = pl.DeviceIdType.MESH
CROSS = 2
PARTS = 6
ADJ_PARTS = 4
EARLY_PARTS = 2
STEP = 16
CHUNKS = 2


def fused_kernel(
    chain,
    sec,
    taps,
    level,
    pw,
    hw,
    err,
    mask,
    scale,
    out,
    tg,
    wb,
    ab,
    ev,
    mv,
    pb,
    gp,
    gr,
    ob,
    hs,
    hf,
    hx,
    xo,
    xh,
    go,
    gs,
    gh,
    fs,
    tile,
    tt,
    cols,
    sums,
    su,
    sv,
    ld_sem,
    w_send,
    w_recv,
    wy_send,
    wy_recv,
    p_send,
    p_recv,
    py_send,
    py_recv,
    a_send,
    a_recv,
    g_send,
    g_recv,
    x_send,
    x_recv,
    xz_send,
    xz_recv,
    u_send,
    u_recv,
    t_send,
    t_recv,
    c_send,
    c_recv,
    gz_send,
    gz_recv,
    s_send,
    s_recv,
    f_send,
    f_recv,
):
    g = lax.axis_index("groups")
    s = lax.axis_index("seq")
    t = lax.axis_index("track")
    z = s // CROSS
    x = s % CROSS
    head_rows = hw.shape[0]
    half = head_rows // 2
    piece = half // PARTS
    tracks, own_rows = err.shape
    own = sec.shape[0]
    owned = own // (chain * CROSS)
    phalf = pw.shape[0] // 2
    step = tracks // ADJ_PARTS // 128 * 128
    cuts = [c * step for c in range(ADJ_PARTS)] + [tracks]
    pair_rows = CROSS * own_rows
    length = chain * pair_rows
    steps = chain - 1
    blocks = chain // CROSS
    slots = blocks * CROSS
    small = owned // CHUNKS

    sibling = (g, s, 1 - t)
    twin = (1 - g, s, t)
    across = (g, z * CROSS + 1 - x, t)
    has_up = z < chain - 1
    has_down = z > 0
    is_end = (z == 0) | (z == chain - 1)

    barrier = pltpu.get_barrier_semaphore()
    for device in (sibling, twin, across):
        pl.semaphore_signal(barrier, inc=1, device_id=device, device_id_type=MESH)

    @pl.when(has_up)
    def _():
        pl.semaphore_signal(barrier, inc=1, device_id=(g, s + CROSS, t), device_id_type=MESH)

    @pl.when(has_down)
    def _():
        pl.semaphore_signal(barrier, inc=1, device_id=(g, s - CROSS, t), device_id_type=MESH)

    own_w = pltpu.make_async_copy(
        hw, wb.at[pl.ds(pl.multiple_of(z * head_rows, 16), head_rows), :], ld_sem.at[0]
    )
    own_p = pltpu.make_async_copy(pw, pb.at[z], ld_sem.at[1])

    def block_rows(k, parity):
        return pl.ds(pl.multiple_of((CROSS * k + parity) * head_rows, 16), head_rows)

    def pair_lanes(which):
        return pl.ds(pl.multiple_of(which * own_rows, 128), own_rows)

    def kept_rows(k):
        return pl.ds(k * head_rows, head_rows)

    own_x = [
        pltpu.make_async_copy(
            sec.at[block_rows(k, x), :], xo.at[kept_rows(k), pair_lanes(x)], ld_sem.at[2 + k]
        )
        for k in range(blocks)
    ]
    loads = []
    for c in range(ADJ_PARTS):
        rows = pl.ds(cuts[c], cuts[c + 1] - cuts[c])
        at = 2 + blocks + 2 * c
        loads.append(
            (
                pltpu.make_async_copy(err.at[rows, :], ev.at[rows, :], ld_sem.at[at]),
                pltpu.make_async_copy(mask.at[rows, :], mv.at[rows, :], ld_sem.at[at + 1]),
            )
        )
    for first, second in loads:
        first.start()
        second.start()
    own_w.start()
    own_p.start()
    for k in range(blocks):
        own_x[k].start()

    def fill_part(c):
        loads[c][0].wait()
        loads[c][1].wait()

        def fill(begin, count):
            rows = pl.ds(begin, count)
            line = scale[rows].reshape(1, count)
            if count < 128:
                line = jnp.concatenate([line, jnp.zeros((1, 128 - count), jnp.float32)], axis=1)
            column = jnp.transpose(jnp.broadcast_to(line, (128, 128)))[:count]
            column = jnp.concatenate([column] * (own_rows // 128), axis=1)
            value = mv[rows, :].astype(jnp.float32) * column * ev[rows, :].astype(jnp.float32)
            ab[x, rows, :] = value.astype(jnp.bfloat16)

        def fill_step(i, carry):
            fill(pl.multiple_of(cuts[c] + i * 128, 128), 128)
            return carry

        whole, rest = divmod(cuts[c + 1] - cuts[c], 128)
        lax.fori_loop(0, whole, fill_step, 0)
        if rest:
            fill(cuts[c] + whole * 128, rest)

    for c in range(EARLY_PARTS):
        fill_part(c)

    pl.semaphore_wait(barrier, jnp.where(is_end, 4, 5))

    def w_rows(shard, c, which):
        return pl.ds(pl.multiple_of(shard * head_rows + which * half + c * piece, 16), piece)

    def w_hop(shard, c, src, toward, direction):
        slot = shard * PARTS + c
        return pltpu.make_async_remote_copy(
            src_ref=src,
            dst_ref=wb.at[w_rows(shard, c, g), :],
            send_sem=w_send.at[direction, slot],
            recv_sem=w_recv.at[slot],
            device_id=(g, toward * CROSS + x, t),
            device_id_type=MESH,
        )

    def w_swap(shard, c, which):
        slot = shard * PARTS + c
        block = wb.at[w_rows(shard, c, which), :]
        return pltpu.make_async_remote_copy(
            src_ref=block,
            dst_ref=block,
            send_sem=wy_send.at[slot],
            recv_sem=wy_recv.at[slot],
            device_id=twin,
            device_id_type=MESH,
        )

    p_parts = blocks
    wide = CROSS * head_rows

    def p_part(shard, c, which):
        rows = pl.ds(pl.multiple_of(which * phalf, 16), phalf)
        return pb.at[shard, rows, pl.ds(pl.multiple_of(c * wide, 128), wide)]

    def p_hop(shard, c, src, toward, direction):
        slot = shard * p_parts + c
        return pltpu.make_async_remote_copy(
            src_ref=src,
            dst_ref=p_part(shard, c, g),
            send_sem=p_send.at[direction, slot],
            recv_sem=p_recv.at[slot],
            device_id=(g, toward * CROSS + x, t),
            device_id_type=MESH,
        )

    def p_swap(shard, c, which):
        slot = shard * p_parts + c
        block = p_part(shard, c, which)
        return pltpu.make_async_remote_copy(
            src_ref=block,
            dst_ref=block,
            send_sem=py_send.at[slot],
            recv_sem=py_recv.at[slot],
            device_id=twin,
            device_id_type=MESH,
        )

    def own_piece(c):
        return hw.at[pl.ds(pl.multiple_of(g * half + c * piece, 16), piece), :]

    def a_copy(c, which):
        block = ab.at[which, pl.ds(cuts[c], cuts[c + 1] - cuts[c]), :]
        return pltpu.make_async_remote_copy(
            src_ref=block,
            dst_ref=block,
            send_sem=a_send.at[c],
            recv_sem=a_recv.at[c],
            device_id=across,
            device_id_type=MESH,
        )

    @pl.when(has_up)
    def _():
        for c in range(PARTS):
            w_hop(z, c, own_piece(c), z + 1, 0).start()

    @pl.when(has_down)
    def _():
        for c in range(PARTS):
            w_hop(z, c, own_piece(c), z - 1, 1).start()

    for c in range(EARLY_PARTS):
        a_copy(c, x).start()
    for c in range(EARLY_PARTS, ADJ_PARTS):
        fill_part(c)
        a_copy(c, x).start()

    def own_p_part(c):
        return pw.at[pl.ds(pl.multiple_of(g * phalf, 16), phalf), pl.ds(c * wide, wide)]

    def p_send_own(c):
        @pl.when(has_up)
        def _():
            p_hop(z, c, own_p_part(c), z + 1, 0).start()

        @pl.when(has_down)
        def _():
            p_hop(z, c, own_p_part(c), z - 1, 1).start()

    for c in range(p_parts):
        p_send_own(c)

    below = z
    above = chain - 1 - z
    near = jnp.minimum(below, above)

    def order(j):
        jump = (j + 1) // 2
        alternate = jnp.where(j % 2 == 1, z - jump, z + jump)
        one_sided = jnp.where(above > below, z + (j - near), z - (j - near))
        return jnp.where(j <= 2 * near, alternate, one_sided)

    def shard_rows(shard):
        return pl.ds(pl.multiple_of(shard * head_rows, 16), head_rows)

    def g_copy(shard, xs):
        return pltpu.make_async_remote_copy(
            src_ref=gp.at[xs, shard_rows(shard), :],
            dst_ref=gr.at[xs, shard_rows(shard), :],
            send_sem=g_send.at[shard, xs],
            recv_sem=g_recv.at[shard, xs],
            device_id=sibling,
            device_id_type=MESH,
        )

    def head_dot(shard, xs):
        rows = shard_rows(shard)
        gp[xs, rows, :] = lax.dot_general(
            wb[rows, :],
            ab[xs],
            (((1,), (0,)), ((), ())),
            preferred_element_type=jnp.float32,
        )
        g_copy(shard, xs).start()

    def w_relay(e, carry):
        paired = (near >= 1) & (e < 2 * PARTS)
        j = jnp.where(paired, 1 + e % 2, e // PARTS + 1)
        c = jnp.where(paired, e // 2, e % PARTS)
        shard = order(j)
        block = wb.at[w_rows(shard, c, g), :]
        w_hop(shard, c, block, z, 0).wait_recv()

        @pl.when((shard < z) & has_up)
        def _():
            w_hop(shard, c, block, z + 1, 0).start()

        @pl.when((shard > z) & has_down)
        def _():
            w_hop(shard, c, block, z - 1, 1).start()

        w_swap(shard, c, g).start()
        return carry

    def wait_swaps(shard):
        def one(c, carry):
            w_swap(shard, c, 1 - g).wait_recv()
            return carry

        lax.fori_loop(0, PARTS, one, 0)

    def near_dot(j, carry):
        shard = order(j)
        wait_swaps(shard)
        head_dot(shard, x)
        return carry

    def p_relay(e, carry):
        shard = order(e % steps + 1)
        c = e // steps
        block = p_part(shard, c, g)
        p_hop(shard, c, block, z, 0).wait_recv()

        @pl.when((shard < z) & has_up)
        def _():
            p_hop(shard, c, block, z + 1, 0).start()

        @pl.when((shard > z) & has_down)
        def _():
            p_hop(shard, c, block, z - 1, 1).start()

        p_swap(shard, c, g).start()
        return carry

    def far_dot(j, carry):
        head_dot(order(j), 1 - x)
        return carry

    def x_copy(k, parity, which):
        return pltpu.make_async_remote_copy(
            src_ref=sec.at[block_rows(k, parity), :],
            dst_ref=xo.at[kept_rows(k), pair_lanes(which)],
            send_sem=x_send.at[k],
            recv_sem=x_recv.at[k],
            device_id=across,
            device_id_type=MESH,
        )

    def slot_rows(i):
        return pl.ds(pl.multiple_of(i * owned, 16), owned)

    def xz_copy(i, side, device):
        return pltpu.make_async_remote_copy(
            src_ref=xo.at[slot_rows(i), :],
            dst_ref=xh.at[side, slot_rows(i), :],
            send_sem=xz_send.at[side, i],
            recv_sem=xz_recv.at[side, i],
            device_id=(g, device, t),
            device_id_type=MESH,
        )

    my_slot = (z // CROSS) * CROSS + x
    in_column = z % CROSS == x

    def u_copy(slot):
        return pltpu.make_async_remote_copy(
            src_ref=tile,
            dst_ref=tt.at[slot],
            send_sem=u_send,
            recv_sem=u_recv,
            device_id=across,
            device_id_type=MESH,
        )

    def t_copy(to, frm):
        pair = tt.at[pl.ds(frm // CROSS * CROSS, CROSS)]
        return pltpu.make_async_remote_copy(
            src_ref=pair,
            dst_ref=pair,
            send_sem=t_send.at[to],
            recv_sem=t_recv.at[frm],
            device_id=(g, to * CROSS + x, t),
            device_id_type=MESH,
        )

    own_w.wait()
    head_dot(z, x)

    tile[...] = jnp.zeros((8, 128), jnp.float32)
    tile[0:3, 0:owned] = taps[...]
    tile[3:4, 0:owned] = level[...].astype(jnp.float32)

    @pl.when(jnp.logical_not(in_column))
    def _():
        u_copy(my_slot).start()

    @pl.when(in_column)
    def _():
        tt[my_slot] = tile[...]

    @pl.when(z == 0)
    def _():
        xh[0] = jnp.zeros(xh.shape[1:], jnp.bfloat16)
        gh[0] = jnp.zeros(gh.shape[1:], jnp.bfloat16)

    @pl.when(z == chain - 1)
    def _():
        xh[1] = jnp.zeros(xh.shape[1:], jnp.bfloat16)
        gh[1] = jnp.zeros(gh.shape[1:], jnp.bfloat16)

    for i in range(slots):
        sums[i] = jnp.zeros((128, 128), jnp.float32)

    def end_relay(begin, end):
        lax.fori_loop(begin, jnp.where(is_end, end, begin), p_relay, 0)

    lax.fori_loop(0, PARTS, w_relay, 0)
    for c in range(p_parts):
        end_relay(c * steps, c * steps + 1)
    lax.fori_loop(PARTS, (steps - 1) * PARTS, w_relay, 0)
    first = jnp.where(is_end, 2, 1)
    lax.fori_loop(1, first, near_dot, 0)
    lax.fori_loop((steps - 1) * PARTS, steps * PARTS, w_relay, 0)

    @pl.when(in_column)
    def _():
        u_copy(my_slot).wait_recv()

        def t_start(j, carry):
            t_copy(order(j), z).start()
            return carry

        lax.fori_loop(1, chain, t_start, 0)

    for k in range(blocks):
        x_copy(k, 1 - x, x).start()

    lax.fori_loop(0, jnp.where(is_end, 0, p_parts * steps), p_relay, 0)
    lax.fori_loop(first, steps, near_dot, 0)
    for c in range(ADJ_PARTS):
        a_copy(c, 1 - x).wait_recv()
    lax.fori_loop(0, steps, far_dot, 0)
    end_relay(1, 2)
    last = order(steps)
    wait_swaps(last)
    head_dot(last, x)
    head_dot(last, 1 - x)
    end_relay(2, steps)

    for k in range(blocks):
        own_x[k].wait()
        x_copy(k, x, 1 - x).wait_recv()

    def xz_start(i, carry):
        @pl.when(has_up)
        def _():
            xz_copy(i, 0, s + CROSS).start()

        @pl.when(has_down)
        def _():
            xz_copy(i, 1, s - CROSS).start()

        return carry

    lax.fori_loop(0, slots, xz_start, 0)

    def core_sum(j, carry):
        shard = order(j)
        rows = shard_rows(shard)
        for xs in range(CROSS):
            g_copy(shard, xs).wait_recv()
            ob[rows, xs * own_rows : (xs + 1) * own_rows] = (gp[xs, rows, :] + gr[xs, rows, :]).astype(
                jnp.bfloat16
            )
        return carry

    lax.fori_loop(0, chain, core_sum, 0)

    own_p.wait()

    def p_wait(c):
        def one(j, carry):
            p_swap(order(j), c, 1 - g).wait_recv()
            return carry

        lax.fori_loop(1, steps + 1, one, 0)

    per_block = head_rows // small
    chunks = blocks * per_block

    def c_copy(ch):
        k = ch // per_block
        begin = (1 - x) * head_rows + (ch % per_block) * small
        return pltpu.make_async_remote_copy(
            src_ref=hs.at[k, pl.ds(pl.multiple_of(begin, 16), small), :],
            dst_ref=hx.at[pl.ds(pl.multiple_of(ch * small, 16), small), :],
            send_sem=c_send.at[ch],
            recv_sem=c_recv.at[ch],
            device_id=across,
            device_id_type=MESH,
        )

    def h_step(k, carry):
        lanes = pl.ds(pl.multiple_of(k * wide, 128), wide)
        total = jnp.zeros((wide, pair_rows), jnp.float32)
        for shard in range(chain):
            total = total + lax.dot_general(
                pb[shard, :, lanes],
                ob[shard * head_rows : (shard + 1) * head_rows, :],
                (((0,), (0,)), ((), ())),
                preferred_element_type=jnp.float32,
            )
        hs[k] = total.astype(jnp.bfloat16)
        hf[k] = total

        def c_start(u, inner):
            c_copy(k * per_block + u).start()
            return inner

        lax.fori_loop(0, per_block, c_start, 0)
        return carry

    end_relay(steps + 1, blocks * steps)
    p_wait(0)
    h_step(0, 0)
    p_wait(1)
    h_step(1, 0)

    norm = 1.0 / math.sqrt(length)

    def t_wait(frm, carry):
        @pl.when((frm % CROSS == x) & (frm != z))
        def _():
            t_copy(0, frm).wait_recv()

        return carry

    lax.fori_loop(0, chain, t_wait, 0)
    for i in range(slots):
        padded = jnp.concatenate([tt[i], jnp.zeros((120, 128), jnp.float32)], axis=0)
        cols[i] = jnp.transpose(padded)

    def moved(left, here, right, lev, sign):
        result = None
        for k in range(DILATION_COUNT):
            reach = BASE_DILATION * 2**k
            if sign < 0:
                if reach % 128 == 0:
                    value = (
                        left
                        if reach == pair_rows
                        else jnp.concatenate([left[:, pair_rows - reach :], here[:, : pair_rows - reach]], axis=1)
                    )
                else:
                    joined = jnp.concatenate([left[:, pair_rows - 128 :], here], axis=1)
                    value = pltpu.roll(joined, reach, 1)[:, 128:]
            else:
                if reach % 128 == 0:
                    value = (
                        right
                        if reach == pair_rows
                        else jnp.concatenate([here[:, reach:], right[:, :reach]], axis=1)
                    )
                else:
                    joined = jnp.concatenate([here, right[:, :128]], axis=1)
                    value = pltpu.roll(joined, pair_rows + 128 - reach, 1)[:, :pair_rows]
            result = value if result is None else jnp.where(lev == float(k), value, result)
        return result

    def gz_copy(ch, side, device):
        rows = pl.ds(pl.multiple_of(ch * small, 16), small)
        return pltpu.make_async_remote_copy(
            src_ref=gs.at[rows, :],
            dst_ref=gh.at[side, rows, :],
            send_sem=gz_send.at[side, ch],
            recv_sem=gz_recv.at[side, ch],
            device_id=(g, device, t),
            device_id_type=MESH,
        )

    def conv_rows(row):
        i = row // owned
        rows = pl.ds(pl.multiple_of(row, STEP), STEP)
        within = pl.ds(pl.multiple_of(row % owned, STEP), STEP)
        lev = cols[i, within, 3:4]
        tap = cols[i, within, 0:3]
        left = xh[0, rows, :].astype(jnp.float32)
        center = xo[rows, :].astype(jnp.float32)
        right = xh[1, rows, :].astype(jnp.float32)
        minus = moved(left, center, right, lev, -1)
        plus = moved(left, center, right, lev, 1)
        pre_act = tap[:, 0:1] * minus + tap[:, 1:2] * center + tap[:, 2:3] * plus
        mine = pl.ds(pl.multiple_of(x * head_rows + row % head_rows, STEP), STEP)
        hidden = (hf[row // head_rows, mine, :] + hx[rows, :].astype(jnp.float32)).astype(jnp.bfloat16)
        pre_grad = hidden.astype(jnp.float32) * gelu_slope(pre_act)
        go[rows, :] = pre_grad
        gs[rows, :] = pre_grad.astype(jnp.bfloat16)
        sums[i, within, 0:1] = jnp.sum(pre_grad * minus, axis=1, keepdims=True)
        sums[i, within, 1:2] = jnp.sum(pre_grad * center, axis=1, keepdims=True)
        sums[i, within, 2:3] = jnp.sum(pre_grad * plus, axis=1, keepdims=True)

    def conv_chunk(ch, carry):
        c_copy(ch).wait_recv()

        @pl.when((ch % CHUNKS == 0) & has_down)
        def _():
            xz_copy(ch // CHUNKS, 0, s).wait_recv()

        @pl.when((ch % CHUNKS == 0) & has_up)
        def _():
            xz_copy(ch // CHUNKS, 1, s).wait_recv()

        def one(i, inner):
            conv_rows(ch * small + i * STEP)
            return inner

        lax.fori_loop(0, small // STEP, one, 0)

        @pl.when(has_up)
        def _():
            gz_copy(ch, 0, s + CROSS).start()

        @pl.when(has_down)
        def _():
            gz_copy(ch, 1, s - CROSS).start()

        return carry

    lax.fori_loop(0, chunks, conv_chunk, 0)

    def s_copy(i, frm):
        return pltpu.make_async_remote_copy(
            src_ref=su.at[i],
            dst_ref=sv.at[frm],
            send_sem=s_send.at[i],
            recv_sem=s_recv.at[frm],
            device_id=(g, (i // CROSS * CROSS + x) * CROSS + i % CROSS, t),
            device_id_type=MESH,
        )

    def s_mine(i):
        return in_column & (i == my_slot)

    def s_start(i, carry):
        su[i] = jnp.transpose(sums[i])[0:8]

        @pl.when(jnp.logical_not(s_mine(i)))
        def _():
            s_copy(i, z).start()

        return carry

    lax.fori_loop(0, slots, s_start, 0)

    @pl.when(in_column)
    def _():
        sv[z] = su[my_slot]

    def out_rows(ch):
        begin = (ch // per_block * CROSS + x) * head_rows + ch % per_block * small
        return pl.ds(pl.multiple_of(begin, 16), small)

    def f_copy(ch, rows):
        return pltpu.make_async_remote_copy(
            src_ref=fs.at[pl.ds(pl.multiple_of(ch * small, 16), small), :],
            dst_ref=out.at[rows, :],
            send_sem=f_send.at[ch],
            recv_sem=f_recv.at[ch],
            device_id=across,
            device_id_type=MESH,
        )

    def final_rows(row):
        i = row // owned
        k = row // head_rows
        rows = pl.ds(pl.multiple_of(row, STEP), STEP)
        within = pl.ds(pl.multiple_of(row % owned, STEP), STEP)
        lev = cols[i, within, 3:4]
        tap = cols[i, within, 0:3]
        left = gh[0, rows, :].astype(jnp.float32)
        here = go[rows, :]
        right = gh[1, rows, :].astype(jnp.float32)
        part = (
            tap[:, 0:1] * moved(left, here, right, lev, 1)
            + tap[:, 1:2] * here
            + tap[:, 2:3] * moved(left, here, right, lev, -1)
        )
        begin = (t * blocks + k) * head_rows + row % head_rows
        up = pl.ds(pl.multiple_of(begin, STEP), STEP)
        whole = jnp.concatenate([gp[xs, up, :] + gr[xs, up, :] for xs in range(CROSS)], axis=1)
        value = (whole + part).astype(jnp.bfloat16)
        begin = (k * CROSS + x) * head_rows + row % head_rows
        low, high = value[:, :own_rows], value[:, own_rows:]

        @pl.when(x == 0)
        def _():
            out[pl.ds(pl.multiple_of(begin, STEP), STEP), :] = low
            fs[rows, :] = high

        @pl.when(x != 0)
        def _():
            out[pl.ds(pl.multiple_of(begin, STEP), STEP), :] = high
            fs[rows, :] = low

    def final_chunk(ch, carry):
        @pl.when(has_down)
        def _():
            gz_copy(ch, 0, s).wait_recv()

        @pl.when(has_up)
        def _():
            gz_copy(ch, 1, s).wait_recv()

        def one(i, inner):
            final_rows(ch * small + i * STEP)
            return inner

        lax.fori_loop(0, small // STEP, one, 0)
        f_copy(ch, out_rows(ch)).start()
        return carry

    lax.fori_loop(0, chunks, final_chunk, 0)

    def s_wait(frm, carry):
        @pl.when(jnp.logical_not(in_column) | (frm != z))
        def _():
            s_copy(0, frm).wait_recv()

        return carry

    lax.fori_loop(0, chain, s_wait, 0)
    total = sv[0]
    for frm in range(1, chain):
        total = total + sv[frm]
    tg[...] = total[0:3, 0:owned] * norm

    def w_done(shard, carry):
        def one(c, inner):
            block = wb.at[w_rows(shard, c, g), :]

            @pl.when((shard <= z) & has_up)
            def _():
                w_hop(shard, c, block, z, 0).wait_send()

            @pl.when((shard >= z) & has_down)
            def _():
                w_hop(shard, c, block, z, 1).wait_send()

            @pl.when(shard != z)
            def _():
                w_swap(shard, c, g).wait_send()

            return inner

        lax.fori_loop(0, PARTS, one, 0)

        def p_one(c, inner):
            block = p_part(shard, c, g)

            @pl.when((shard <= z) & has_up)
            def _():
                p_hop(shard, c, block, z, 0).wait_send()

            @pl.when((shard >= z) & has_down)
            def _():
                p_hop(shard, c, block, z, 1).wait_send()

            @pl.when(shard != z)
            def _():
                p_swap(shard, c, g).wait_send()

            return inner

        lax.fori_loop(0, p_parts, p_one, 0)
        for xs in range(CROSS):
            g_copy(shard, xs).wait_send()

        @pl.when((shard != z) & in_column)
        def _():
            t_copy(shard, z).wait_send()

        return carry

    lax.fori_loop(0, chain, w_done, 0)

    @pl.when(jnp.logical_not(in_column))
    def _():
        u_copy(my_slot).wait_send()

    for c in range(ADJ_PARTS):
        a_copy(c, x).wait_send()
    for k in range(blocks):
        x_copy(k, 1 - x, x).wait_send()

    def slot_done(i, carry):
        @pl.when(has_up)
        def _():
            xz_copy(i, 0, s).wait_send()

        @pl.when(has_down)
        def _():
            xz_copy(i, 1, s).wait_send()

        @pl.when(jnp.logical_not(s_mine(i)))
        def _():
            s_copy(i, z).wait_send()

        return carry

    lax.fori_loop(0, slots, slot_done, 0)

    def chunk_done(ch, carry):
        c_copy(ch).wait_send()

        @pl.when(has_up)
        def _():
            gz_copy(ch, 0, s).wait_send()

        @pl.when(has_down)
        def _():
            gz_copy(ch, 1, s).wait_send()

        f_copy(ch, out_rows(ch)).wait()
        return carry

    lax.fori_loop(0, chunks, chunk_done, 0)


def hand_over(grad, taps, grad_out, taps_out):
    grad_out[...] = grad[...]
    taps_out[...] = taps[...]


def fused(
    chain,
    section_input,
    conv_taps,
    dilation_level,
    pointwise_matrix,
    head_weight,
    pred_error,
    tail_mask,
    track_scale,
):
    own, own_rows = section_input.shape
    owned = own // (chain * CROSS)
    head_rows, tracks = head_weight.shape
    pair_rows = CROSS * own_rows
    cols = pointwise_matrix.shape[1]
    blocks = chain // CROSS
    slots = blocks * CROSS
    chunks = slots * CHUNKS
    kept = blocks * head_rows
    bf16, f32 = jnp.bfloat16, jnp.float32
    dma = pltpu.SemaphoreType.DMA
    anywhere = pl.BlockSpec(memory_space=pltpu.HBM)
    vmem = pl.BlockSpec(memory_space=pltpu.VMEM)
    input_grad, taps_grad = pl.pallas_call(
        functools.partial(fused_kernel, chain),
        out_shape=(
            pltpu.VMEM((own, own_rows), bf16),
            pltpu.VMEM((3, owned), f32),
        ),
        in_specs=[anywhere, vmem, vmem, anywhere, anywhere, anywhere, anywhere, vmem],
        out_specs=(vmem, vmem),
        scratch_shapes=[
            pltpu.VMEM((chain * head_rows, tracks), bf16),
            pltpu.VMEM((CROSS, tracks, own_rows), bf16),
            pltpu.VMEM((tracks, own_rows), bf16),
            pltpu.VMEM((tracks, own_rows), jnp.int32),
            pltpu.VMEM((chain, cols, own), bf16),
            pltpu.VMEM((CROSS, chain * head_rows, own_rows), f32),
            pltpu.VMEM((CROSS, chain * head_rows, own_rows), f32),
            pltpu.VMEM((chain * head_rows, pair_rows), bf16),
            pltpu.VMEM((blocks, CROSS * head_rows, pair_rows), bf16),
            pltpu.VMEM((blocks, CROSS * head_rows, pair_rows), f32),
            pltpu.VMEM((kept, pair_rows), bf16),
            pltpu.VMEM((kept, pair_rows), bf16),
            pltpu.VMEM((2, kept, pair_rows), bf16),
            pltpu.VMEM((kept, pair_rows), f32),
            pltpu.VMEM((kept, pair_rows), bf16),
            pltpu.VMEM((2, kept, pair_rows), bf16),
            pltpu.VMEM((kept, own_rows), bf16),
            pltpu.VMEM((8, 128), f32),
            pltpu.VMEM((slots, 8, 128), f32),
            pltpu.VMEM((slots, 128, 128), f32),
            pltpu.VMEM((slots, 128, 128), f32),
            pltpu.VMEM((slots, 8, 128), f32),
            pltpu.VMEM((chain, 8, 128), f32),
            dma((2 + blocks + 2 * ADJ_PARTS,)),
            dma((2, chain * PARTS)),
            dma((chain * PARTS,)),
            dma((chain * PARTS,)),
            dma((chain * PARTS,)),
            dma((2, chain * blocks)),
            dma((chain * blocks,)),
            dma((chain * blocks,)),
            dma((chain * blocks,)),
            dma((ADJ_PARTS,)),
            dma((ADJ_PARTS,)),
            dma((chain, CROSS)),
            dma((chain, CROSS)),
            dma((blocks,)),
            dma((blocks,)),
            dma((2, slots)),
            dma((2, slots)),
            dma,
            dma,
            dma((chain,)),
            dma((chain,)),
            dma((chunks,)),
            dma((chunks,)),
            dma((2, chunks)),
            dma((2, chunks)),
            dma((slots,)),
            dma((chain,)),
            dma((chunks,)),
            dma((chunks,)),
        ],
        compiler_params=pltpu.CompilerParams(
            collective_id=0, has_side_effects=True, vmem_limit_bytes=63 * 1024 * 1024
        ),
        name="fused_section",
    )(
        section_input,
        conv_taps.T,
        dilation_level[None, :],
        pointwise_matrix.T,
        head_weight,
        pred_error.T,
        tail_mask.T,
        track_scale,
    )
    return input_grad, taps_grad.T


def local_or_fused(sizes, *args):
    section_input, head_weight, pred_error = args[0], args[4], args[5]
    seq = sizes["seq"]
    own, own_rows = section_input.shape
    fits = (
        sizes["groups"] == 2
        and sizes["track"] == 2
        and seq == 8
        and head_weight.shape[0] % (2 * PARTS * 16) == 0
        and own % (seq * 16 * CHUNKS) == 0
        and own_rows % 128 == 0
        and CROSS * own_rows == BASE_DILATION * 2 ** (DILATION_COUNT - 1)
        and pred_error.shape[1] % 16 == 0
        and pred_error.shape[1] >= 128 * ADJ_PARTS
        and args[3].shape[1] % 32 == 0
        and own // seq <= 128
        and head_weight.shape[0] * 4 == own
        and own // 2 % 128 == 0
    )
    if fits:
        return fused(seq // CROSS, *args)
    return local(*args)


def solution(mesh):
    in_specs = (
        P("track", ("groups", "seq")),
        P(("track", "seq"), None),
        P(("track", "seq")),
        P("track", "seq"),
        P("seq", "track"),
        P(("groups", "seq"), "track"),
        P(("groups", "seq"), "track"),
        P("track"),
    )
    sizes = dict(mesh.shape)
    body = functools.partial(local_or_fused, sizes)
    out_specs = (P("track", ("groups", "seq")), P(("groups", "track", "seq"), None))
    return jax.shard_map(body, mesh=mesh, in_specs=in_specs, out_specs=out_specs, check_vma=False)
```

```python
import functools
import math

import jax
import jax.numpy as jnp
from jax import lax
from jax.experimental import pallas as pl
from jax.experimental.pallas import tpu as pltpu
from jax.sharding import PartitionSpec as P

DILATION_COUNT = 5
BASE_DILATION = 32


root_half = 0.7071067811865476
norm_const = 0.3989422804014327


def gelu_slope(value):
    return 0.5 * (1.0 + jax.scipy.special.erf(value * root_half)) + value * norm_const * jnp.exp(
        -0.5 * value * value
    )


def taps_at(buffer, onehot, margin, sign):
    width_own = buffer.shape[1] - 2 * margin
    result = jnp.zeros((buffer.shape[0], width_own), jnp.float32)
    for level_index in range(onehot.shape[1]):
        receptive_span = BASE_DILATION * 2**level_index
        begin = margin + sign * receptive_span
        result = (
            result + onehot[:, level_index : level_index + 1] * buffer[:, begin : begin + width_own]
        )
    return result


def spread(values, onehot, margin, sign):
    result = jnp.zeros((values.shape[0], values.shape[1] + 2 * margin), jnp.float32)
    for level_index in range(onehot.shape[1]):
        receptive_span = BASE_DILATION * 2**level_index
        placed = onehot[:, level_index : level_index + 1] * values
        result = result + jnp.pad(
            placed, ((0, 0), (margin + sign * receptive_span, margin - sign * receptive_span))
        )
    return result


def channel_grads(buffer, hidden_grad, taps, onehot, margin):
    width_own = buffer.shape[1] - 2 * margin
    minus_side = taps_at(buffer, onehot, margin, -1)
    center = buffer[:, margin : margin + width_own]
    plus_side = taps_at(buffer, onehot, margin, 1)
    pre_act = taps[:, 0:1] * minus_side + taps[:, 1:2] * center + taps[:, 2:3] * plus_side
    pre_grad = hidden_grad.astype(jnp.float32) * gelu_slope(pre_act)
    taps_part = jnp.stack(
        [
            jnp.sum(pre_grad * minus_side, axis=1),
            jnp.sum(pre_grad * center, axis=1),
            jnp.sum(pre_grad * plus_side, axis=1),
        ],
        axis=1,
    )
    contrib = spread(taps[:, 0:1] * pre_grad, onehot, margin, -1) + spread(
        taps[:, 2:3] * pre_grad, onehot, margin, 1
    )
    contrib = contrib + jnp.pad(taps[:, 1:2] * pre_grad, ((0, 0), (margin, margin)))
    return (contrib, taps_part)


def local(
    section_input,
    conv_taps,
    dilation_level,
    pointwise_matrix,
    head_weight,
    pred_error,
    tail_mask,
    track_scale,
):
    own_channels = section_input.shape[0]
    own_rows = section_input.shape[1]
    adjoint = (
        tail_mask.astype(jnp.float32) * track_scale[None, :] * pred_error.astype(jnp.float32)
    ).astype(jnp.bfloat16)
    full_grad = lax.dot_general(
        lax.all_gather(head_weight, "seq", axis=0, tiled=True),
        adjoint,
        (((1,), (1,)), ((), ())),
        preferred_element_type=jnp.float32,
    )
    total = lax.psum(full_grad, "track")
    out_grad_b = total.astype(jnp.bfloat16)
    out_grad = lax.dynamic_slice_in_dim(
        total, lax.axis_index("track") * own_channels, own_channels, 0
    )
    hidden_grad = jnp.dot(
        lax.all_gather(pointwise_matrix, "seq", axis=1, tiled=True),
        out_grad_b,
        preferred_element_type=jnp.float32,
    ).astype(jnp.bfloat16)
    largest_span = BASE_DILATION * 2 ** (DILATION_COUNT - 1)
    scale = 1.0 / math.sqrt(own_rows * lax.axis_size("seq"))
    onehot = (
        dilation_level[:, None] == jnp.arange(DILATION_COUNT, dtype=jnp.int32)[None, :]
    ).astype(jnp.float32)
    owned_input, owned_grad = (
        lax.all_to_all(section_input, "seq", split_axis=0, concat_axis=1, tiled=True),
        lax.all_to_all(hidden_grad, "seq", split_axis=0, concat_axis=1, tiled=True),
    )
    padded = jnp.pad(owned_input.astype(jnp.float32), ((0, 0), (largest_span, largest_span)))
    contrib, taps_part = channel_grads(padded, owned_grad, conv_taps, onehot, largest_span)
    window = contrib[:, largest_span : largest_span + owned_input.shape[1]]
    conv_part = lax.all_to_all(window, "seq", split_axis=1, concat_axis=0, tiled=True)
    taps_grad = taps_part * scale
    input_grad = (out_grad + conv_part).astype(jnp.bfloat16)
    return (input_grad, taps_grad)


MESH = pl.DeviceIdType.MESH
CROSS = 2
PARTS = 6
ADJ_PARTS = 4
STEP = 16
CHUNKS = 2


def fused_kernel(
    chain,
    sec,
    taps_in,
    level_in,
    pw,
    hw,
    err,
    mask,
    scale_in,
    out,
    tg,
    taps,
    level,
    scale,
    wb,
    ab,
    ev,
    mv,
    pb,
    gp,
    gr,
    ob,
    hs,
    hf,
    hx,
    xo,
    xh,
    go,
    gs,
    gh,
    fs,
    tile,
    tt,
    cols,
    sums,
    su,
    sv,
    table_sem,
    ld_sem,
    w_send,
    w_recv,
    wy_send,
    wy_recv,
    p_send,
    p_recv,
    py_send,
    py_recv,
    a_send,
    a_recv,
    g_send,
    g_recv,
    x_send,
    x_recv,
    xz_send,
    xz_recv,
    u_send,
    u_recv,
    t_send,
    t_recv,
    c_send,
    c_recv,
    gz_send,
    gz_recv,
    s_send,
    s_recv,
    f_send,
    f_recv,
):
    g = lax.axis_index("groups")
    s = lax.axis_index("seq")
    t = lax.axis_index("track")
    z = s // CROSS
    x = s % CROSS
    head_rows = hw.shape[0]
    half = head_rows // 2
    piece = half // PARTS
    tracks, own_rows = err.shape
    own = sec.shape[0]
    owned = own // (chain * CROSS)
    phalf = pw.shape[0] // 2
    step = tracks // ADJ_PARTS // 128 * 128
    cuts = [c * step for c in range(ADJ_PARTS)] + [tracks]
    pair_rows = CROSS * own_rows
    length = chain * pair_rows
    steps = chain - 1
    blocks = chain // CROSS
    slots = blocks * CROSS
    small = owned // CHUNKS

    sibling = (g, s, 1 - t)
    twin = (1 - g, s, t)
    across = (g, z * CROSS + 1 - x, t)
    has_up = z < chain - 1
    has_down = z > 0
    is_end = (z == 0) | (z == chain - 1)

    barrier = pltpu.get_barrier_semaphore()
    for device in (sibling, twin, across):
        pl.semaphore_signal(barrier, inc=1, device_id=device, device_id_type=MESH)

    @pl.when(has_up)
    def _():
        pl.semaphore_signal(barrier, inc=1, device_id=(g, s + CROSS, t), device_id_type=MESH)

    @pl.when(has_down)
    def _():
        pl.semaphore_signal(barrier, inc=1, device_id=(g, s - CROSS, t), device_id_type=MESH)

    own_w = pltpu.make_async_copy(
        hw, wb.at[pl.ds(pl.multiple_of(z * head_rows, 16), head_rows), :], ld_sem.at[0]
    )
    own_p = pltpu.make_async_copy(pw, pb.at[z], ld_sem.at[1])

    def block_rows(k, parity):
        return pl.ds(pl.multiple_of((CROSS * k + parity) * head_rows, 16), head_rows)

    def pair_lanes(which):
        return pl.ds(pl.multiple_of(which * own_rows, 128), own_rows)

    def kept_rows(k):
        return pl.ds(k * head_rows, head_rows)

    own_x = [
        pltpu.make_async_copy(
            sec.at[block_rows(k, x), :], xo.at[kept_rows(k), pair_lanes(x)], ld_sem.at[2 + k]
        )
        for k in range(blocks)
    ]
    loads = []
    for c in range(ADJ_PARTS):
        rows = pl.ds(cuts[c], cuts[c + 1] - cuts[c])
        at = 2 + blocks + 2 * c
        loads.append(
            (
                pltpu.make_async_copy(err.at[rows, :], ev.at[rows, :], ld_sem.at[at]),
                pltpu.make_async_copy(mask.at[rows, :], mv.at[rows, :], ld_sem.at[at + 1]),
            )
        )
    tables = [
        pltpu.make_async_copy(src, dst, table_sem.at[k])
        for k, (src, dst) in enumerate([(scale_in, scale), (taps_in, taps), (level_in, level)])
    ]
    tables[0].start()
    for first, second in loads:
        first.start()
        second.start()
    tables[1].start()
    tables[2].start()

    def fill_part(c):
        loads[c][0].wait()
        loads[c][1].wait()

        def fill(begin, count):
            rows = pl.ds(begin, count)
            line = scale[rows].reshape(1, count)
            if count < 128:
                line = jnp.concatenate([line, jnp.zeros((1, 128 - count), jnp.float32)], axis=1)
            column = jnp.transpose(jnp.broadcast_to(line, (128, 128)))[:count]
            column = jnp.concatenate([column] * (own_rows // 128), axis=1)
            value = mv[rows, :].astype(jnp.float32) * column * ev[rows, :].astype(jnp.float32)
            ab[x, rows, :] = value.astype(jnp.bfloat16)

        def fill_step(i, carry):
            fill(pl.multiple_of(cuts[c] + i * 128, 128), 128)
            return carry

        whole, rest = divmod(cuts[c + 1] - cuts[c], 128)
        lax.fori_loop(0, whole, fill_step, 0)
        if rest:
            fill(cuts[c] + whole * 128, rest)

    pl.semaphore_wait(barrier, jnp.where(is_end, 4, 5))

    def w_rows(shard, c, which):
        return pl.ds(pl.multiple_of(shard * head_rows + which * half + c * piece, 16), piece)

    def w_hop(shard, c, src, toward, direction):
        slot = shard * PARTS + c
        return pltpu.make_async_remote_copy(
            src_ref=src,
            dst_ref=wb.at[w_rows(shard, c, g), :],
            send_sem=w_send.at[direction, slot],
            recv_sem=w_recv.at[slot],
            device_id=(g, toward * CROSS + x, t),
            device_id_type=MESH,
        )

    def w_swap(shard, c, which):
        slot = shard * PARTS + c
        block = wb.at[w_rows(shard, c, which), :]
        return pltpu.make_async_remote_copy(
            src_ref=block,
            dst_ref=block,
            send_sem=wy_send.at[slot],
            recv_sem=wy_recv.at[slot],
            device_id=twin,
            device_id_type=MESH,
        )

    p_parts = blocks
    wide = CROSS * head_rows

    def p_part(shard, c, which):
        rows = pl.ds(pl.multiple_of(which * phalf, 16), phalf)
        return pb.at[shard, rows, pl.ds(pl.multiple_of(c * wide, 128), wide)]

    def p_hop(shard, c, src, toward, direction):
        slot = shard * p_parts + c
        return pltpu.make_async_remote_copy(
            src_ref=src,
            dst_ref=p_part(shard, c, g),
            send_sem=p_send.at[direction, slot],
            recv_sem=p_recv.at[slot],
            device_id=(g, toward * CROSS + x, t),
            device_id_type=MESH,
        )

    def p_swap(shard, c, which):
        slot = shard * p_parts + c
        block = p_part(shard, c, which)
        return pltpu.make_async_remote_copy(
            src_ref=block,
            dst_ref=block,
            send_sem=py_send.at[slot],
            recv_sem=py_recv.at[slot],
            device_id=twin,
            device_id_type=MESH,
        )

    def own_piece(c):
        return hw.at[pl.ds(pl.multiple_of(g * half + c * piece, 16), piece), :]

    def a_copy(c, which):
        block = ab.at[which, pl.ds(cuts[c], cuts[c + 1] - cuts[c]), :]
        return pltpu.make_async_remote_copy(
            src_ref=block,
            dst_ref=block,
            send_sem=a_send.at[c],
            recv_sem=a_recv.at[c],
            device_id=across,
            device_id_type=MESH,
        )

    @pl.when(has_up)
    def _():
        for c in range(PARTS):
            w_hop(z, c, own_piece(c), z + 1, 0).start()

    @pl.when(has_down)
    def _():
        for c in range(PARTS):
            w_hop(z, c, own_piece(c), z - 1, 1).start()

    own_w.start()
    own_p.start()
    for k in range(blocks):
        own_x[k].start()
    tables[0].wait()
    for c in range(ADJ_PARTS):
        fill_part(c)
        a_copy(c, x).start()

    def own_p_part(c):
        return pw.at[pl.ds(pl.multiple_of(g * phalf, 16), phalf), pl.ds(c * wide, wide)]

    def p_send_own(c):
        @pl.when(has_up)
        def _():
            p_hop(z, c, own_p_part(c), z + 1, 0).start()

        @pl.when(has_down)
        def _():
            p_hop(z, c, own_p_part(c), z - 1, 1).start()

    for c in range(p_parts):
        p_send_own(c)

    below = z
    above = chain - 1 - z
    near = jnp.minimum(below, above)

    def order(j):
        jump = (j + 1) // 2
        alternate = jnp.where(j % 2 == 1, z - jump, z + jump)
        one_sided = jnp.where(above > below, z + (j - near), z - (j - near))
        return jnp.where(j <= 2 * near, alternate, one_sided)

    def shard_rows(shard):
        return pl.ds(pl.multiple_of(shard * head_rows, 16), head_rows)

    def g_copy(shard, xs):
        return pltpu.make_async_remote_copy(
            src_ref=gp.at[xs, shard_rows(shard), :],
            dst_ref=gr.at[xs, shard_rows(shard), :],
            send_sem=g_send.at[shard, xs],
            recv_sem=g_recv.at[shard, xs],
            device_id=sibling,
            device_id_type=MESH,
        )

    def head_dot(shard, xs):
        rows = shard_rows(shard)
        gp[xs, rows, :] = lax.dot_general(
            wb[rows, :],
            ab[xs],
            (((1,), (0,)), ((), ())),
            preferred_element_type=jnp.float32,
        )
        g_copy(shard, xs).start()

    def w_relay(e, carry):
        paired = (near >= 1) & (e < 2 * PARTS)
        j = jnp.where(paired, 1 + e % 2, e // PARTS + 1)
        c = jnp.where(paired, e // 2, e % PARTS)
        shard = order(j)
        block = wb.at[w_rows(shard, c, g), :]
        w_hop(shard, c, block, z, 0).wait_recv()

        @pl.when((shard < z) & has_up)
        def _():
            w_hop(shard, c, block, z + 1, 0).start()

        @pl.when((shard > z) & has_down)
        def _():
            w_hop(shard, c, block, z - 1, 1).start()

        w_swap(shard, c, g).start()
        return carry

    def wait_swaps(shard):
        def one(c, carry):
            w_swap(shard, c, 1 - g).wait_recv()
            return carry

        lax.fori_loop(0, PARTS, one, 0)

    def near_dot(j, carry):
        shard = order(j)
        wait_swaps(shard)
        head_dot(shard, x)
        return carry

    def p_relay(e, carry):
        shard = order(e % steps + 1)
        c = e // steps
        block = p_part(shard, c, g)
        p_hop(shard, c, block, z, 0).wait_recv()

        @pl.when((shard < z) & has_up)
        def _():
            p_hop(shard, c, block, z + 1, 0).start()

        @pl.when((shard > z) & has_down)
        def _():
            p_hop(shard, c, block, z - 1, 1).start()

        p_swap(shard, c, g).start()
        return carry

    def far_dot(j, carry):
        head_dot(order(j), 1 - x)
        return carry

    def x_copy(k, parity, which):
        return pltpu.make_async_remote_copy(
            src_ref=sec.at[block_rows(k, parity), :],
            dst_ref=xo.at[kept_rows(k), pair_lanes(which)],
            send_sem=x_send.at[k],
            recv_sem=x_recv.at[k],
            device_id=across,
            device_id_type=MESH,
        )

    def slot_rows(i):
        return pl.ds(pl.multiple_of(i * owned, 16), owned)

    def xz_copy(i, side, device):
        return pltpu.make_async_remote_copy(
            src_ref=xo.at[slot_rows(i), :],
            dst_ref=xh.at[side, slot_rows(i), :],
            send_sem=xz_send.at[side, i],
            recv_sem=xz_recv.at[side, i],
            device_id=(g, device, t),
            device_id_type=MESH,
        )

    my_slot = (z // CROSS) * CROSS + x
    in_column = z % CROSS == x

    def u_copy(slot):
        return pltpu.make_async_remote_copy(
            src_ref=tile,
            dst_ref=tt.at[slot],
            send_sem=u_send,
            recv_sem=u_recv,
            device_id=across,
            device_id_type=MESH,
        )

    def t_copy(to, frm):
        pair = tt.at[pl.ds(frm // CROSS * CROSS, CROSS)]
        return pltpu.make_async_remote_copy(
            src_ref=pair,
            dst_ref=pair,
            send_sem=t_send.at[to],
            recv_sem=t_recv.at[frm],
            device_id=(g, to * CROSS + x, t),
            device_id_type=MESH,
        )

    own_w.wait()
    head_dot(z, x)

    tables[1].wait()
    tables[2].wait()
    tile[...] = jnp.zeros((8, 128), jnp.float32)
    tile[0:3, 0:owned] = taps[...]
    tile[3:4, 0:owned] = level[...].astype(jnp.float32)

    @pl.when(jnp.logical_not(in_column))
    def _():
        u_copy(my_slot).start()

    @pl.when(in_column)
    def _():
        tt[my_slot] = tile[...]

    @pl.when(z == 0)
    def _():
        xh[0] = jnp.zeros(xh.shape[1:], jnp.bfloat16)
        gh[0] = jnp.zeros(gh.shape[1:], jnp.bfloat16)

    @pl.when(z == chain - 1)
    def _():
        xh[1] = jnp.zeros(xh.shape[1:], jnp.bfloat16)
        gh[1] = jnp.zeros(gh.shape[1:], jnp.bfloat16)

    for i in range(slots):
        sums[i] = jnp.zeros((128, 128), jnp.float32)

    def end_relay(begin, end):
        lax.fori_loop(begin, jnp.where(is_end, end, begin), p_relay, 0)

    lax.fori_loop(0, PARTS, w_relay, 0)
    for c in range(p_parts):
        end_relay(c * steps, c * steps + 1)
    lax.fori_loop(PARTS, (steps - 1) * PARTS, w_relay, 0)
    first = jnp.where(is_end, 2, 1)
    lax.fori_loop(1, first, near_dot, 0)
    lax.fori_loop((steps - 1) * PARTS, steps * PARTS, w_relay, 0)

    @pl.when(in_column)
    def _():
        u_copy(my_slot).wait_recv()

        def t_start(j, carry):
            t_copy(order(j), z).start()
            return carry

        lax.fori_loop(1, chain, t_start, 0)

    for k in range(blocks):
        x_copy(k, 1 - x, x).start()

    lax.fori_loop(0, jnp.where(is_end, 0, p_parts * steps), p_relay, 0)
    lax.fori_loop(first, steps, near_dot, 0)
    for c in range(ADJ_PARTS):
        a_copy(c, 1 - x).wait_recv()
    lax.fori_loop(0, steps, far_dot, 0)
    end_relay(1, 2)
    last = order(steps)
    wait_swaps(last)
    head_dot(last, x)
    head_dot(last, 1 - x)
    end_relay(2, steps)

    for k in range(blocks):
        own_x[k].wait()
        x_copy(k, x, 1 - x).wait_recv()

    def xz_start(i, carry):
        @pl.when(has_up)
        def _():
            xz_copy(i, 0, s + CROSS).start()

        @pl.when(has_down)
        def _():
            xz_copy(i, 1, s - CROSS).start()

        return carry

    lax.fori_loop(0, slots, xz_start, 0)

    def core_sum(j, carry):
        shard = order(j)
        rows = shard_rows(shard)
        for xs in range(CROSS):
            g_copy(shard, xs).wait_recv()
            ob[rows, xs * own_rows : (xs + 1) * own_rows] = (gp[xs, rows, :] + gr[xs, rows, :]).astype(
                jnp.bfloat16
            )
        return carry

    lax.fori_loop(0, chain, core_sum, 0)

    own_p.wait()

    def p_wait(c):
        def one(j, carry):
            p_swap(order(j), c, 1 - g).wait_recv()
            return carry

        lax.fori_loop(1, steps + 1, one, 0)

    per_block = head_rows // small
    chunks = blocks * per_block

    def c_copy(ch):
        k = ch // per_block
        begin = (1 - x) * head_rows + (ch % per_block) * small
        return pltpu.make_async_remote_copy(
            src_ref=hs.at[k, pl.ds(pl.multiple_of(begin, 16), small), :],
            dst_ref=hx.at[pl.ds(pl.multiple_of(ch * small, 16), small), :],
            send_sem=c_send.at[ch],
            recv_sem=c_recv.at[ch],
            device_id=across,
            device_id_type=MESH,
        )

    def h_step(k, carry):
        lanes = pl.ds(pl.multiple_of(k * wide, 128), wide)
        total = jnp.zeros((wide, pair_rows), jnp.float32)
        for shard in range(chain):
            total = total + lax.dot_general(
                pb[shard, :, lanes],
                ob[shard * head_rows : (shard + 1) * head_rows, :],
                (((0,), (0,)), ((), ())),
                preferred_element_type=jnp.float32,
            )
        hs[k] = total.astype(jnp.bfloat16)
        hf[k] = total

        def c_start(u, inner):
            c_copy(k * per_block + u).start()
            return inner

        lax.fori_loop(0, per_block, c_start, 0)
        return carry

    end_relay(steps + 1, blocks * steps)
    p_wait(0)
    h_step(0, 0)
    p_wait(1)
    h_step(1, 0)

    norm = 1.0 / math.sqrt(length)

    def t_wait(frm, carry):
        @pl.when((frm % CROSS == x) & (frm != z))
        def _():
            t_copy(0, frm).wait_recv()

        return carry

    lax.fori_loop(0, chain, t_wait, 0)
    for i in range(slots):
        padded = jnp.concatenate([tt[i], jnp.zeros((120, 128), jnp.float32)], axis=0)
        cols[i] = jnp.transpose(padded)

    def moved(left, here, right, lev, sign):
        result = None
        for k in range(DILATION_COUNT):
            reach = BASE_DILATION * 2**k
            if sign < 0:
                if reach % 128 == 0:
                    value = (
                        left
                        if reach == pair_rows
                        else jnp.concatenate([left[:, pair_rows - reach :], here[:, : pair_rows - reach]], axis=1)
                    )
                else:
                    joined = jnp.concatenate([left[:, pair_rows - 128 :], here], axis=1)
                    value = pltpu.roll(joined, reach, 1)[:, 128:]
            else:
                if reach % 128 == 0:
                    value = (
                        right
                        if reach == pair_rows
                        else jnp.concatenate([here[:, reach:], right[:, :reach]], axis=1)
                    )
                else:
                    joined = jnp.concatenate([here, right[:, :128]], axis=1)
                    value = pltpu.roll(joined, pair_rows + 128 - reach, 1)[:, :pair_rows]
            result = value if result is None else jnp.where(lev == float(k), value, result)
        return result

    def gz_copy(ch, side, device):
        rows = pl.ds(pl.multiple_of(ch * small, 16), small)
        return pltpu.make_async_remote_copy(
            src_ref=gs.at[rows, :],
            dst_ref=gh.at[side, rows, :],
            send_sem=gz_send.at[side, ch],
            recv_sem=gz_recv.at[side, ch],
            device_id=(g, device, t),
            device_id_type=MESH,
        )

    def conv_rows(row):
        i = row // owned
        rows = pl.ds(pl.multiple_of(row, STEP), STEP)
        within = pl.ds(pl.multiple_of(row % owned, STEP), STEP)
        lev = cols[i, within, 3:4]
        tap = cols[i, within, 0:3]
        left = xh[0, rows, :].astype(jnp.float32)
        center = xo[rows, :].astype(jnp.float32)
        right = xh[1, rows, :].astype(jnp.float32)
        minus = moved(left, center, right, lev, -1)
        plus = moved(left, center, right, lev, 1)
        pre_act = tap[:, 0:1] * minus + tap[:, 1:2] * center + tap[:, 2:3] * plus
        mine = pl.ds(pl.multiple_of(x * head_rows + row % head_rows, STEP), STEP)
        hidden = (hf[row // head_rows, mine, :] + hx[rows, :].astype(jnp.float32)).astype(jnp.bfloat16)
        pre_grad = hidden.astype(jnp.float32) * gelu_slope(pre_act)
        go[rows, :] = pre_grad
        gs[rows, :] = pre_grad.astype(jnp.bfloat16)
        sums[i, within, 0:1] = jnp.sum(pre_grad * minus, axis=1, keepdims=True)
        sums[i, within, 1:2] = jnp.sum(pre_grad * center, axis=1, keepdims=True)
        sums[i, within, 2:3] = jnp.sum(pre_grad * plus, axis=1, keepdims=True)

    def conv_chunk(ch, carry):
        c_copy(ch).wait_recv()

        @pl.when((ch % CHUNKS == 0) & has_down)
        def _():
            xz_copy(ch // CHUNKS, 0, s).wait_recv()

        @pl.when((ch % CHUNKS == 0) & has_up)
        def _():
            xz_copy(ch // CHUNKS, 1, s).wait_recv()

        def one(i, inner):
            conv_rows(ch * small + i * STEP)
            return inner

        lax.fori_loop(0, small // STEP, one, 0)

        @pl.when(has_up)
        def _():
            gz_copy(ch, 0, s + CROSS).start()

        @pl.when(has_down)
        def _():
            gz_copy(ch, 1, s - CROSS).start()

        return carry

    def conv_slot(i, carry):
        lax.fori_loop(i * CHUNKS, (i + 1) * CHUNKS, conv_chunk, 0)
        return s_start(i, carry)


    def s_copy(i, frm):
        return pltpu.make_async_remote_copy(
            src_ref=su.at[i],
            dst_ref=sv.at[frm],
            send_sem=s_send.at[i],
            recv_sem=s_recv.at[frm],
            device_id=(g, (i // CROSS * CROSS + x) * CROSS + i % CROSS, t),
            device_id_type=MESH,
        )

    def s_mine(i):
        return in_column & (i == my_slot)

    def s_start(i, carry):
        su[i] = jnp.transpose(sums[i])[0:8]

        @pl.when(jnp.logical_not(s_mine(i)))
        def _():
            s_copy(i, z).start()

        return carry

    lax.fori_loop(0, slots, conv_slot, 0)

    @pl.when(in_column)
    def _():
        sv[z] = su[my_slot]

    def out_rows(ch):
        begin = (ch // per_block * CROSS + x) * head_rows + ch % per_block * small
        return pl.ds(pl.multiple_of(begin, 16), small)

    def f_copy(ch, rows):
        return pltpu.make_async_remote_copy(
            src_ref=fs.at[pl.ds(pl.multiple_of(ch * small, 16), small), :],
            dst_ref=out.at[rows, :],
            send_sem=f_send.at[ch],
            recv_sem=f_recv.at[ch],
            device_id=across,
            device_id_type=MESH,
        )

    def final_rows(row):
        i = row // owned
        k = row // head_rows
        rows = pl.ds(pl.multiple_of(row, STEP), STEP)
        within = pl.ds(pl.multiple_of(row % owned, STEP), STEP)
        lev = cols[i, within, 3:4]
        tap = cols[i, within, 0:3]
        left = gh[0, rows, :].astype(jnp.float32)
        here = go[rows, :]
        right = gh[1, rows, :].astype(jnp.float32)
        part = (
            tap[:, 0:1] * moved(left, here, right, lev, 1)
            + tap[:, 1:2] * here
            + tap[:, 2:3] * moved(left, here, right, lev, -1)
        )
        begin = (t * blocks + k) * head_rows + row % head_rows
        up = pl.ds(pl.multiple_of(begin, STEP), STEP)
        whole = jnp.concatenate([gp[xs, up, :] + gr[xs, up, :] for xs in range(CROSS)], axis=1)
        value = (whole + part).astype(jnp.bfloat16)
        begin = (k * CROSS + x) * head_rows + row % head_rows
        low, high = value[:, :own_rows], value[:, own_rows:]

        @pl.when(x == 0)
        def _():
            out[pl.ds(pl.multiple_of(begin, STEP), STEP), :] = low
            fs[rows, :] = high

        @pl.when(x != 0)
        def _():
            out[pl.ds(pl.multiple_of(begin, STEP), STEP), :] = high
            fs[rows, :] = low

    def final_chunk(ch, carry):
        @pl.when(has_down)
        def _():
            gz_copy(ch, 0, s).wait_recv()

        @pl.when(has_up)
        def _():
            gz_copy(ch, 1, s).wait_recv()

        def one(i, inner):
            final_rows(ch * small + i * STEP)
            return inner

        lax.fori_loop(0, small // STEP, one, 0)
        f_copy(ch, out_rows(ch)).start()
        return carry

    lax.fori_loop(0, chunks, final_chunk, 0)

    def s_wait(frm, carry):
        @pl.when(jnp.logical_not(in_column) | (frm != z))
        def _():
            s_copy(0, frm).wait_recv()

        return carry

    lax.fori_loop(0, chain, s_wait, 0)
    total = sv[0]
    for frm in range(1, chain):
        total = total + sv[frm]
    tg[...] = total[0:3, 0:owned] * norm

    def w_done(shard, carry):
        def one(c, inner):
            block = wb.at[w_rows(shard, c, g), :]

            @pl.when((shard <= z) & has_up)
            def _():
                w_hop(shard, c, block, z, 0).wait_send()

            @pl.when((shard >= z) & has_down)
            def _():
                w_hop(shard, c, block, z, 1).wait_send()

            @pl.when(shard != z)
            def _():
                w_swap(shard, c, g).wait_send()

            return inner

        lax.fori_loop(0, PARTS, one, 0)

        def p_one(c, inner):
            block = p_part(shard, c, g)

            @pl.when((shard <= z) & has_up)
            def _():
                p_hop(shard, c, block, z, 0).wait_send()

            @pl.when((shard >= z) & has_down)
            def _():
                p_hop(shard, c, block, z, 1).wait_send()

            @pl.when(shard != z)
            def _():
                p_swap(shard, c, g).wait_send()

            return inner

        lax.fori_loop(0, p_parts, p_one, 0)
        for xs in range(CROSS):
            g_copy(shard, xs).wait_send()

        @pl.when((shard != z) & in_column)
        def _():
            t_copy(shard, z).wait_send()

        return carry

    lax.fori_loop(0, chain, w_done, 0)

    @pl.when(jnp.logical_not(in_column))
    def _():
        u_copy(my_slot).wait_send()

    for c in range(ADJ_PARTS):
        a_copy(c, x).wait_send()
    for k in range(blocks):
        x_copy(k, 1 - x, x).wait_send()

    def slot_done(i, carry):
        @pl.when(has_up)
        def _():
            xz_copy(i, 0, s).wait_send()

        @pl.when(has_down)
        def _():
            xz_copy(i, 1, s).wait_send()

        @pl.when(jnp.logical_not(s_mine(i)))
        def _():
            s_copy(i, z).wait_send()

        return carry

    lax.fori_loop(0, slots, slot_done, 0)

    def chunk_done(ch, carry):
        c_copy(ch).wait_send()

        @pl.when(has_up)
        def _():
            gz_copy(ch, 0, s).wait_send()

        @pl.when(has_down)
        def _():
            gz_copy(ch, 1, s).wait_send()

        f_copy(ch, out_rows(ch)).wait()
        return carry

    lax.fori_loop(0, chunks, chunk_done, 0)


def hand_over(grad, taps, grad_out, taps_out):
    grad_out[...] = grad[...]
    taps_out[...] = taps[...]


def fused(
    chain,
    section_input,
    conv_taps,
    dilation_level,
    pointwise_matrix,
    head_weight,
    pred_error,
    tail_mask,
    track_scale,
):
    own, own_rows = section_input.shape
    owned = own // (chain * CROSS)
    head_rows, tracks = head_weight.shape
    pair_rows = CROSS * own_rows
    cols = pointwise_matrix.shape[1]
    blocks = chain // CROSS
    slots = blocks * CROSS
    chunks = slots * CHUNKS
    kept = blocks * head_rows
    bf16, f32 = jnp.bfloat16, jnp.float32
    dma = pltpu.SemaphoreType.DMA
    anywhere = pl.BlockSpec(memory_space=pltpu.HBM)
    vmem = pl.BlockSpec(memory_space=pltpu.VMEM)
    input_grad, taps_grad = pl.pallas_call(
        functools.partial(fused_kernel, chain),
        out_shape=(
            pltpu.VMEM((own, own_rows), bf16),
            pltpu.VMEM((3, owned), f32),
        ),
        in_specs=[anywhere] * 8,
        out_specs=(vmem, vmem),
        scratch_shapes=[
            pltpu.VMEM((3, owned), f32),
            pltpu.VMEM((1, owned), jnp.int32),
            pltpu.VMEM((tracks,), f32),
            pltpu.VMEM((chain * head_rows, tracks), bf16),
            pltpu.VMEM((CROSS, tracks, own_rows), bf16),
            pltpu.VMEM((tracks, own_rows), bf16),
            pltpu.VMEM((tracks, own_rows), jnp.int32),
            pltpu.VMEM((chain, cols, own), bf16),
            pltpu.VMEM((CROSS, chain * head_rows, own_rows), f32),
            pltpu.VMEM((CROSS, chain * head_rows, own_rows), f32),
            pltpu.VMEM((chain * head_rows, pair_rows), bf16),
            pltpu.VMEM((blocks, CROSS * head_rows, pair_rows), bf16),
            pltpu.VMEM((blocks, CROSS * head_rows, pair_rows), f32),
            pltpu.VMEM((kept, pair_rows), bf16),
            pltpu.VMEM((kept, pair_rows), bf16),
            pltpu.VMEM((2, kept, pair_rows), bf16),
            pltpu.VMEM((kept, pair_rows), f32),
            pltpu.VMEM((kept, pair_rows), bf16),
            pltpu.VMEM((2, kept, pair_rows), bf16),
            pltpu.VMEM((kept, own_rows), bf16),
            pltpu.VMEM((8, 128), f32),
            pltpu.VMEM((slots, 8, 128), f32),
            pltpu.VMEM((slots, 128, 128), f32),
            pltpu.VMEM((slots, 128, 128), f32),
            pltpu.VMEM((slots, 8, 128), f32),
            pltpu.VMEM((chain, 8, 128), f32),
            dma((3,)),
            dma((2 + blocks + 2 * ADJ_PARTS,)),
            dma((2, chain * PARTS)),
            dma((chain * PARTS,)),
            dma((chain * PARTS,)),
            dma((chain * PARTS,)),
            dma((2, chain * blocks)),
            dma((chain * blocks,)),
            dma((chain * blocks,)),
            dma((chain * blocks,)),
            dma((ADJ_PARTS,)),
            dma((ADJ_PARTS,)),
            dma((chain, CROSS)),
            dma((chain, CROSS)),
            dma((blocks,)),
            dma((blocks,)),
            dma((2, slots)),
            dma((2, slots)),
            dma,
            dma,
            dma((chain,)),
            dma((chain,)),
            dma((chunks,)),
            dma((chunks,)),
            dma((2, chunks)),
            dma((2, chunks)),
            dma((slots,)),
            dma((chain,)),
            dma((chunks,)),
            dma((chunks,)),
        ],
        compiler_params=pltpu.CompilerParams(
            collective_id=0, has_side_effects=True, vmem_limit_bytes=63 * 1024 * 1024
        ),
        name="fused_section",
    )(
        section_input,
        conv_taps.T,
        dilation_level[None, :],
        pointwise_matrix.T,
        head_weight,
        pred_error.T,
        tail_mask.T,
        track_scale,
    )
    return input_grad, taps_grad.T


def local_or_fused(sizes, *args):
    section_input, head_weight, pred_error = args[0], args[4], args[5]
    seq = sizes["seq"]
    own, own_rows = section_input.shape
    fits = (
        sizes["groups"] == 2
        and sizes["track"] == 2
        and seq == 8
        and head_weight.shape[0] % (2 * PARTS * 16) == 0
        and own % (seq * 16 * CHUNKS) == 0
        and own_rows % 128 == 0
        and CROSS * own_rows == BASE_DILATION * 2 ** (DILATION_COUNT - 1)
        and pred_error.shape[1] % 16 == 0
        and pred_error.shape[1] >= 128 * ADJ_PARTS
        and args[3].shape[1] % 32 == 0
        and own // seq <= 128
        and head_weight.shape[0] * 4 == own
        and own // 2 % 128 == 0
    )
    if fits:
        return fused(seq // CROSS, *args)
    return local(*args)


def solution(mesh):
    in_specs = (
        P("track", ("groups", "seq")),
        P(("track", "seq"), None),
        P(("track", "seq")),
        P("track", "seq"),
        P("seq", "track"),
        P(("groups", "seq"), "track"),
        P(("groups", "seq"), "track"),
        P("track"),
    )
    sizes = dict(mesh.shape)
    body = functools.partial(local_or_fused, sizes)
    out_specs = (P("track", ("groups", "seq")), P(("groups", "track", "seq"), None))
    return jax.shard_map(body, mesh=mesh, in_specs=in_specs, out_specs=out_specs, check_vma=False)
```

```python
import functools
import math

import jax
import jax.numpy as jnp
from jax import lax
from jax.experimental import pallas as pl
from jax.experimental.pallas import tpu as pltpu
from jax.sharding import PartitionSpec as P

DILATION_COUNT = 5
BASE_DILATION = 32


root_half = 0.7071067811865476
norm_const = 0.3989422804014327


def gelu_slope(value):
    return 0.5 * (1.0 + jax.scipy.special.erf(value * root_half)) + value * norm_const * jnp.exp(
        -0.5 * value * value
    )


def taps_at(buffer, onehot, margin, sign):
    width_own = buffer.shape[1] - 2 * margin
    result = jnp.zeros((buffer.shape[0], width_own), jnp.float32)
    for level_index in range(onehot.shape[1]):
        receptive_span = BASE_DILATION * 2**level_index
        begin = margin + sign * receptive_span
        result = (
            result + onehot[:, level_index : level_index + 1] * buffer[:, begin : begin + width_own]
        )
    return result


def spread(values, onehot, margin, sign):
    result = jnp.zeros((values.shape[0], values.shape[1] + 2 * margin), jnp.float32)
    for level_index in range(onehot.shape[1]):
        receptive_span = BASE_DILATION * 2**level_index
        placed = onehot[:, level_index : level_index + 1] * values
        result = result + jnp.pad(
            placed, ((0, 0), (margin + sign * receptive_span, margin - sign * receptive_span))
        )
    return result


def channel_grads(buffer, hidden_grad, taps, onehot, margin):
    width_own = buffer.shape[1] - 2 * margin
    minus_side = taps_at(buffer, onehot, margin, -1)
    center = buffer[:, margin : margin + width_own]
    plus_side = taps_at(buffer, onehot, margin, 1)
    pre_act = taps[:, 0:1] * minus_side + taps[:, 1:2] * center + taps[:, 2:3] * plus_side
    pre_grad = hidden_grad.astype(jnp.float32) * gelu_slope(pre_act)
    taps_part = jnp.stack(
        [
            jnp.sum(pre_grad * minus_side, axis=1),
            jnp.sum(pre_grad * center, axis=1),
            jnp.sum(pre_grad * plus_side, axis=1),
        ],
        axis=1,
    )
    contrib = spread(taps[:, 0:1] * pre_grad, onehot, margin, -1) + spread(
        taps[:, 2:3] * pre_grad, onehot, margin, 1
    )
    contrib = contrib + jnp.pad(taps[:, 1:2] * pre_grad, ((0, 0), (margin, margin)))
    return (contrib, taps_part)


def local(
    section_input,
    conv_taps,
    dilation_level,
    pointwise_matrix,
    head_weight,
    pred_error,
    tail_mask,
    track_scale,
):
    own_channels = section_input.shape[0]
    own_rows = section_input.shape[1]
    adjoint = (
        tail_mask.astype(jnp.float32) * track_scale[None, :] * pred_error.astype(jnp.float32)
    ).astype(jnp.bfloat16)
    full_grad = lax.dot_general(
        lax.all_gather(head_weight, "seq", axis=0, tiled=True),
        adjoint,
        (((1,), (1,)), ((), ())),
        preferred_element_type=jnp.float32,
    )
    total = lax.psum(full_grad, "track")
    out_grad_b = total.astype(jnp.bfloat16)
    out_grad = lax.dynamic_slice_in_dim(
        total, lax.axis_index("track") * own_channels, own_channels, 0
    )
    hidden_grad = jnp.dot(
        lax.all_gather(pointwise_matrix, "seq", axis=1, tiled=True),
        out_grad_b,
        preferred_element_type=jnp.float32,
    ).astype(jnp.bfloat16)
    largest_span = BASE_DILATION * 2 ** (DILATION_COUNT - 1)
    scale = 1.0 / math.sqrt(own_rows * lax.axis_size("seq"))
    onehot = (
        dilation_level[:, None] == jnp.arange(DILATION_COUNT, dtype=jnp.int32)[None, :]
    ).astype(jnp.float32)
    owned_input, owned_grad = (
        lax.all_to_all(section_input, "seq", split_axis=0, concat_axis=1, tiled=True),
        lax.all_to_all(hidden_grad, "seq", split_axis=0, concat_axis=1, tiled=True),
    )
    padded = jnp.pad(owned_input.astype(jnp.float32), ((0, 0), (largest_span, largest_span)))
    contrib, taps_part = channel_grads(padded, owned_grad, conv_taps, onehot, largest_span)
    window = contrib[:, largest_span : largest_span + owned_input.shape[1]]
    conv_part = lax.all_to_all(window, "seq", split_axis=1, concat_axis=0, tiled=True)
    taps_grad = taps_part * scale
    input_grad = (out_grad + conv_part).astype(jnp.bfloat16)
    return (input_grad, taps_grad)


MESH = pl.DeviceIdType.MESH
CROSS = 2
PARTS = 6
ADJ_PARTS = 4
STEP = 16
CHUNKS = 2


def fused_kernel(
    chain,
    sec,
    taps_in,
    level_in,
    pw,
    hw,
    err,
    mask,
    scale_in,
    out,
    tg,
    taps,
    level,
    scale,
    wb,
    ab,
    ev,
    mv,
    pb,
    gp,
    gr,
    ob,
    hs,
    hf,
    hx,
    xo,
    xh,
    go,
    gs,
    gh,
    fs,
    tile,
    tt,
    cols,
    sums,
    su,
    sv,
    table_sem,
    ld_sem,
    w_send,
    w_recv,
    wy_send,
    wy_recv,
    p_send,
    p_recv,
    py_send,
    py_recv,
    a_send,
    a_recv,
    g_send,
    g_recv,
    x_send,
    x_recv,
    xz_send,
    xz_recv,
    u_send,
    u_recv,
    t_send,
    t_recv,
    c_send,
    c_recv,
    gz_send,
    gz_recv,
    s_send,
    s_recv,
    f_send,
    f_recv,
):
    g = lax.axis_index("groups")
    s = lax.axis_index("seq")
    t = lax.axis_index("track")
    z = s // CROSS
    x = s % CROSS
    head_rows = hw.shape[0]
    half = head_rows // 2
    piece = half // PARTS
    tracks, own_rows = err.shape
    own = sec.shape[0]
    owned = own // (chain * CROSS)
    phalf = pw.shape[0] // 2
    step = tracks // ADJ_PARTS // 128 * 128
    cuts = [c * step for c in range(ADJ_PARTS)] + [tracks]
    pair_rows = CROSS * own_rows
    length = chain * pair_rows
    steps = chain - 1
    blocks = chain // CROSS
    slots = blocks * CROSS
    small = owned // CHUNKS

    sibling = (g, s, 1 - t)
    twin = (1 - g, s, t)
    across = (g, z * CROSS + 1 - x, t)
    has_up = z < chain - 1
    has_down = z > 0
    is_end = (z == 0) | (z == chain - 1)

    barrier = pltpu.get_barrier_semaphore()
    for device in (sibling, twin, across):
        pl.semaphore_signal(barrier, inc=1, device_id=device, device_id_type=MESH)

    @pl.when(has_up)
    def _():
        pl.semaphore_signal(barrier, inc=1, device_id=(g, s + CROSS, t), device_id_type=MESH)

    @pl.when(has_down)
    def _():
        pl.semaphore_signal(barrier, inc=1, device_id=(g, s - CROSS, t), device_id_type=MESH)

    own_w = pltpu.make_async_copy(
        hw, wb.at[pl.ds(pl.multiple_of(z * head_rows, 16), head_rows), :], ld_sem.at[0]
    )
    own_p = pltpu.make_async_copy(pw, pb.at[z], ld_sem.at[1])

    def block_rows(k, parity):
        return pl.ds(pl.multiple_of((CROSS * k + parity) * head_rows, 16), head_rows)

    def pair_lanes(which):
        return pl.ds(pl.multiple_of(which * own_rows, 128), own_rows)

    def kept_rows(k):
        return pl.ds(k * head_rows, head_rows)

    own_x = [
        pltpu.make_async_copy(
            sec.at[block_rows(k, x), :], xo.at[kept_rows(k), pair_lanes(x)], ld_sem.at[2 + k]
        )
        for k in range(blocks)
    ]
    loads = []
    for c in range(ADJ_PARTS):
        rows = pl.ds(cuts[c], cuts[c + 1] - cuts[c])
        at = 2 + blocks + 2 * c
        loads.append(
            (
                pltpu.make_async_copy(err.at[rows, :], ev.at[rows, :], ld_sem.at[at]),
                pltpu.make_async_copy(mask.at[rows, :], mv.at[rows, :], ld_sem.at[at + 1]),
            )
        )
    tables = [
        pltpu.make_async_copy(src, dst, table_sem.at[k])
        for k, (src, dst) in enumerate([(scale_in, scale), (taps_in, taps), (level_in, level)])
    ]
    tables[0].start()
    for first, second in loads:
        first.start()
        second.start()
    tables[1].start()
    tables[2].start()

    def fill_part(c):
        loads[c][0].wait()
        loads[c][1].wait()

        def fill(begin, count):
            rows = pl.ds(begin, count)
            line = scale[rows].reshape(1, count)
            if count < 128:
                line = jnp.concatenate([line, jnp.zeros((1, 128 - count), jnp.float32)], axis=1)
            column = jnp.transpose(jnp.broadcast_to(line, (128, 128)))[:count]
            column = jnp.concatenate([column] * (own_rows // 128), axis=1)
            value = mv[rows, :].astype(jnp.float32) * column * ev[rows, :].astype(jnp.float32)
            ab[x, rows, :] = value.astype(jnp.bfloat16)

        def fill_step(i, carry):
            fill(pl.multiple_of(cuts[c] + i * 128, 128), 128)
            return carry

        whole, rest = divmod(cuts[c + 1] - cuts[c], 128)
        lax.fori_loop(0, whole, fill_step, 0)
        if rest:
            fill(cuts[c] + whole * 128, rest)

    pl.semaphore_wait(barrier, jnp.where(is_end, 4, 5))

    def w_rows(shard, c, which):
        return pl.ds(pl.multiple_of(shard * head_rows + which * half + c * piece, 16), piece)

    def w_hop(shard, c, src, toward, direction):
        slot = shard * PARTS + c
        return pltpu.make_async_remote_copy(
            src_ref=src,
            dst_ref=wb.at[w_rows(shard, c, g), :],
            send_sem=w_send.at[direction, slot],
            recv_sem=w_recv.at[slot],
            device_id=(g, toward * CROSS + x, t),
            device_id_type=MESH,
        )

    def w_swap(shard, c, which):
        slot = shard * PARTS + c
        block = wb.at[w_rows(shard, c, which), :]
        return pltpu.make_async_remote_copy(
            src_ref=block,
            dst_ref=block,
            send_sem=wy_send.at[slot],
            recv_sem=wy_recv.at[slot],
            device_id=twin,
            device_id_type=MESH,
        )

    p_parts = blocks
    wide = CROSS * head_rows

    def p_part(shard, c, which):
        rows = pl.ds(pl.multiple_of(which * phalf, 16), phalf)
        return pb.at[shard, rows, pl.ds(pl.multiple_of(c * wide, 128), wide)]

    def p_hop(shard, c, src, toward, direction):
        slot = shard * p_parts + c
        return pltpu.make_async_remote_copy(
            src_ref=src,
            dst_ref=p_part(shard, c, g),
            send_sem=p_send.at[direction, slot],
            recv_sem=p_recv.at[slot],
            device_id=(g, toward * CROSS + x, t),
            device_id_type=MESH,
        )

    def p_swap(shard, c, which):
        slot = shard * p_parts + c
        block = p_part(shard, c, which)
        return pltpu.make_async_remote_copy(
            src_ref=block,
            dst_ref=block,
            send_sem=py_send.at[slot],
            recv_sem=py_recv.at[slot],
            device_id=twin,
            device_id_type=MESH,
        )

    def own_piece(c):
        return hw.at[pl.ds(pl.multiple_of(g * half + c * piece, 16), piece), :]

    def a_copy(c, which):
        block = ab.at[which, pl.ds(cuts[c], cuts[c + 1] - cuts[c]), :]
        return pltpu.make_async_remote_copy(
            src_ref=block,
            dst_ref=block,
            send_sem=a_send.at[c],
            recv_sem=a_recv.at[c],
            device_id=across,
            device_id_type=MESH,
        )

    @pl.when(has_up)
    def _():
        for c in range(PARTS):
            w_hop(z, c, own_piece(c), z + 1, 0).start()

    @pl.when(has_down)
    def _():
        for c in range(PARTS):
            w_hop(z, c, own_piece(c), z - 1, 1).start()

    own_w.start()
    own_p.start()
    for k in range(blocks):
        own_x[k].start()
    tables[0].wait()
    for c in range(ADJ_PARTS):
        fill_part(c)
        a_copy(c, x).start()

    def own_p_part(c):
        return pw.at[pl.ds(pl.multiple_of(g * phalf, 16), phalf), pl.ds(c * wide, wide)]

    def p_send_own(c):
        @pl.when(has_up)
        def _():
            p_hop(z, c, own_p_part(c), z + 1, 0).start()

        @pl.when(has_down)
        def _():
            p_hop(z, c, own_p_part(c), z - 1, 1).start()

    for c in range(p_parts):
        p_send_own(c)

    below = z
    above = chain - 1 - z
    near = jnp.minimum(below, above)

    def order(j):
        jump = (j + 1) // 2
        alternate = jnp.where(j % 2 == 1, z - jump, z + jump)
        one_sided = jnp.where(above > below, z + (j - near), z - (j - near))
        return jnp.where(j <= 2 * near, alternate, one_sided)

    def shard_rows(shard):
        return pl.ds(pl.multiple_of(shard * head_rows, 16), head_rows)

    def g_copy(shard, xs):
        return pltpu.make_async_remote_copy(
            src_ref=gp.at[xs, shard_rows(shard), :],
            dst_ref=gr.at[xs, shard_rows(shard), :],
            send_sem=g_send.at[shard, xs],
            recv_sem=g_recv.at[shard, xs],
            device_id=sibling,
            device_id_type=MESH,
        )

    def head_dot(shard, xs):
        rows = shard_rows(shard)
        gp[xs, rows, :] = lax.dot_general(
            wb[rows, :],
            ab[xs],
            (((1,), (0,)), ((), ())),
            preferred_element_type=jnp.float32,
        )
        g_copy(shard, xs).start()

    def w_relay(e, carry):
        paired = (near >= 1) & (e < 2 * PARTS)
        j = jnp.where(paired, 1 + e % 2, e // PARTS + 1)
        c = jnp.where(paired, e // 2, e % PARTS)
        shard = order(j)
        block = wb.at[w_rows(shard, c, g), :]
        w_hop(shard, c, block, z, 0).wait_recv()

        @pl.when((shard < z) & has_up)
        def _():
            w_hop(shard, c, block, z + 1, 0).start()

        @pl.when((shard > z) & has_down)
        def _():
            w_hop(shard, c, block, z - 1, 1).start()

        w_swap(shard, c, g).start()
        return carry

    def wait_swaps(shard):
        def one(c, carry):
            w_swap(shard, c, 1 - g).wait_recv()
            return carry

        lax.fori_loop(0, PARTS, one, 0)

    def near_dot(j, carry):
        shard = order(j)
        wait_swaps(shard)
        head_dot(shard, x)
        return carry

    def p_relay(e, carry):
        shard = order(e % steps + 1)
        c = e // steps
        block = p_part(shard, c, g)
        p_hop(shard, c, block, z, 0).wait_recv()

        @pl.when((shard < z) & has_up)
        def _():
            p_hop(shard, c, block, z + 1, 0).start()

        @pl.when((shard > z) & has_down)
        def _():
            p_hop(shard, c, block, z - 1, 1).start()

        p_swap(shard, c, g).start()
        return carry

    def far_dot(j, carry):
        head_dot(order(j), 1 - x)
        return carry

    def x_copy(k, parity, which):
        return pltpu.make_async_remote_copy(
            src_ref=sec.at[block_rows(k, parity), :],
            dst_ref=xo.at[kept_rows(k), pair_lanes(which)],
            send_sem=x_send.at[k],
            recv_sem=x_recv.at[k],
            device_id=across,
            device_id_type=MESH,
        )

    def slot_rows(i):
        return pl.ds(pl.multiple_of(i * owned, 16), owned)

    def xz_copy(i, side, device):
        return pltpu.make_async_remote_copy(
            src_ref=xo.at[slot_rows(i), :],
            dst_ref=xh.at[side, slot_rows(i), :],
            send_sem=xz_send.at[side, i],
            recv_sem=xz_recv.at[side, i],
            device_id=(g, device, t),
            device_id_type=MESH,
        )

    my_slot = (z // CROSS) * CROSS + x
    in_column = z % CROSS == x

    def u_copy(slot):
        return pltpu.make_async_remote_copy(
            src_ref=tile,
            dst_ref=tt.at[slot],
            send_sem=u_send,
            recv_sem=u_recv,
            device_id=across,
            device_id_type=MESH,
        )

    def t_copy(to, frm):
        pair = tt.at[pl.ds(frm // CROSS * CROSS, CROSS)]
        return pltpu.make_async_remote_copy(
            src_ref=pair,
            dst_ref=pair,
            send_sem=t_send.at[to],
            recv_sem=t_recv.at[frm],
            device_id=(g, to * CROSS + x, t),
            device_id_type=MESH,
        )

    own_w.wait()
    head_dot(z, x)

    tables[1].wait()
    tables[2].wait()
    tile[...] = jnp.zeros((8, 128), jnp.float32)
    tile[0:3, 0:owned] = taps[...]
    tile[3:4, 0:owned] = level[...].astype(jnp.float32)

    @pl.when(jnp.logical_not(in_column))
    def _():
        u_copy(my_slot).start()

    @pl.when(in_column)
    def _():
        tt[my_slot] = tile[...]

    @pl.when(z == 0)
    def _():
        xh[0] = jnp.zeros(xh.shape[1:], jnp.bfloat16)
        gh[0] = jnp.zeros(gh.shape[1:], jnp.bfloat16)

    @pl.when(z == chain - 1)
    def _():
        xh[1] = jnp.zeros(xh.shape[1:], jnp.bfloat16)
        gh[1] = jnp.zeros(gh.shape[1:], jnp.bfloat16)

    for i in range(slots):
        sums[i] = jnp.zeros((128, 128), jnp.float32)

    def end_relay(begin, end):
        lax.fori_loop(begin, jnp.where(is_end, end, begin), p_relay, 0)

    lax.fori_loop(0, PARTS, w_relay, 0)
    for c in range(p_parts):
        end_relay(c * steps, c * steps + 1)
    lax.fori_loop(PARTS, (steps - 1) * PARTS, w_relay, 0)
    first = jnp.where(is_end, 2, 1)
    lax.fori_loop(1, first, near_dot, 0)
    lax.fori_loop((steps - 1) * PARTS, steps * PARTS, w_relay, 0)

    @pl.when(in_column)
    def _():
        u_copy(my_slot).wait_recv()

        def t_start(j, carry):
            t_copy(order(j), z).start()
            return carry

        lax.fori_loop(1, chain, t_start, 0)

    for k in range(blocks):
        x_copy(k, 1 - x, x).start()

    lax.fori_loop(0, jnp.where(is_end, 0, p_parts * steps), p_relay, 0)
    lax.fori_loop(first, steps, near_dot, 0)
    for c in range(ADJ_PARTS):
        a_copy(c, 1 - x).wait_recv()
    lax.fori_loop(0, steps, far_dot, 0)
    end_relay(1, 2)
    last = order(steps)
    wait_swaps(last)
    head_dot(last, x)
    head_dot(last, 1 - x)
    end_relay(2, steps)

    for k in range(blocks):
        own_x[k].wait()
        x_copy(k, x, 1 - x).wait_recv()

    def xz_start(i, carry):
        @pl.when(has_up)
        def _():
            xz_copy(i, 0, s + CROSS).start()

        @pl.when(has_down)
        def _():
            xz_copy(i, 1, s - CROSS).start()

        return carry

    lax.fori_loop(0, slots, xz_start, 0)

    def core_sum(j, carry):
        shard = order(j)
        rows = shard_rows(shard)
        for xs in range(CROSS):
            g_copy(shard, xs).wait_recv()
            ob[rows, xs * own_rows : (xs + 1) * own_rows] = (gp[xs, rows, :] + gr[xs, rows, :]).astype(
                jnp.bfloat16
            )
        return carry

    lax.fori_loop(0, chain, core_sum, 0)

    own_p.wait()

    def p_wait(c):
        def one(j, carry):
            p_swap(order(j), c, 1 - g).wait_recv()
            return carry

        lax.fori_loop(1, steps + 1, one, 0)

    per_block = head_rows // small
    chunks = blocks * per_block

    def c_copy(ch):
        k = ch // per_block
        begin = (1 - x) * head_rows + (ch % per_block) * small
        return pltpu.make_async_remote_copy(
            src_ref=hs.at[k, pl.ds(pl.multiple_of(begin, 16), small), :],
            dst_ref=hx.at[pl.ds(pl.multiple_of(ch * small, 16), small), :],
            send_sem=c_send.at[ch],
            recv_sem=c_recv.at[ch],
            device_id=across,
            device_id_type=MESH,
        )

    def h_step(k, carry):
        lanes = pl.ds(pl.multiple_of(k * wide, 128), wide)
        total = jnp.zeros((wide, pair_rows), jnp.float32)
        for shard in range(chain):
            total = total + lax.dot_general(
                pb[shard, :, lanes],
                ob[shard * head_rows : (shard + 1) * head_rows, :],
                (((0,), (0,)), ((), ())),
                preferred_element_type=jnp.float32,
            )
        hs[k] = total.astype(jnp.bfloat16)
        hf[k] = total

        def c_start(u, inner):
            c_copy(k * per_block + u).start()
            return inner

        lax.fori_loop(0, per_block, c_start, 0)
        return carry

    end_relay(steps + 1, blocks * steps)
    p_wait(0)
    h_step(0, 0)
    p_wait(1)
    h_step(1, 0)

    norm = 1.0 / math.sqrt(length)

    def t_wait(frm, carry):
        @pl.when((frm % CROSS == x) & (frm != z))
        def _():
            t_copy(0, frm).wait_recv()

        return carry

    lax.fori_loop(0, chain, t_wait, 0)
    for i in range(slots):
        padded = jnp.concatenate([tt[i], jnp.zeros((120, 128), jnp.float32)], axis=0)
        cols[i] = jnp.transpose(padded)

    def moved(left, here, right, lev, sign):
        result = None
        for k in range(DILATION_COUNT):
            reach = BASE_DILATION * 2**k
            if sign < 0:
                if reach % 128 == 0:
                    value = (
                        left
                        if reach == pair_rows
                        else jnp.concatenate([left[:, pair_rows - reach :], here[:, : pair_rows - reach]], axis=1)
                    )
                else:
                    joined = jnp.concatenate([left[:, pair_rows - 128 :], here], axis=1)
                    value = pltpu.roll(joined, reach, 1)[:, 128:]
            else:
                if reach % 128 == 0:
                    value = (
                        right
                        if reach == pair_rows
                        else jnp.concatenate([here[:, reach:], right[:, :reach]], axis=1)
                    )
                else:
                    joined = jnp.concatenate([here, right[:, :128]], axis=1)
                    value = pltpu.roll(joined, pair_rows + 128 - reach, 1)[:, :pair_rows]
            result = value if result is None else jnp.where(lev == float(k), value, result)
        return result

    def gz_copy(ch, side, device):
        rows = pl.ds(pl.multiple_of(ch * small, 16), small)
        return pltpu.make_async_remote_copy(
            src_ref=gs.at[rows, :],
            dst_ref=gh.at[side, rows, :],
            send_sem=gz_send.at[side, ch],
            recv_sem=gz_recv.at[side, ch],
            device_id=(g, device, t),
            device_id_type=MESH,
        )

    def conv_rows(row):
        i = row // owned
        rows = pl.ds(pl.multiple_of(row, STEP), STEP)
        within = pl.ds(pl.multiple_of(row % owned, STEP), STEP)
        lev = cols[i, within, 3:4]
        tap = cols[i, within, 0:3]
        left = xh[0, rows, :].astype(jnp.float32)
        center = xo[rows, :].astype(jnp.float32)
        right = xh[1, rows, :].astype(jnp.float32)
        minus = moved(left, center, right, lev, -1)
        plus = moved(left, center, right, lev, 1)
        pre_act = tap[:, 0:1] * minus + tap[:, 1:2] * center + tap[:, 2:3] * plus
        mine = pl.ds(pl.multiple_of(x * head_rows + row % head_rows, STEP), STEP)
        hidden = (hf[row // head_rows, mine, :] + hx[rows, :].astype(jnp.float32)).astype(jnp.bfloat16)
        pre_grad = hidden.astype(jnp.float32) * gelu_slope(pre_act)
        go[rows, :] = pre_grad
        gs[rows, :] = pre_grad.astype(jnp.bfloat16)
        sums[i, within, 0:1] = jnp.sum(pre_grad * minus, axis=1, keepdims=True)
        sums[i, within, 1:2] = jnp.sum(pre_grad * center, axis=1, keepdims=True)
        sums[i, within, 2:3] = jnp.sum(pre_grad * plus, axis=1, keepdims=True)

    def conv_chunk(ch, carry):
        c_copy(ch).wait_recv()

        @pl.when((ch % CHUNKS == 0) & has_down)
        def _():
            xz_copy(ch // CHUNKS, 0, s).wait_recv()

        @pl.when((ch % CHUNKS == 0) & has_up)
        def _():
            xz_copy(ch // CHUNKS, 1, s).wait_recv()

        def one(i, inner):
            conv_rows(ch * small + i * STEP)
            return inner

        lax.fori_loop(0, small // STEP, one, 0)

        @pl.when(has_up)
        def _():
            gz_copy(ch, 0, s + CROSS).start()

        @pl.when(has_down)
        def _():
            gz_copy(ch, 1, s - CROSS).start()

        return carry

    def conv_slot(i, carry):
        lax.fori_loop(i * CHUNKS, (i + 1) * CHUNKS, conv_chunk, 0)
        return s_start(i, carry)


    def s_copy(i, frm):
        return pltpu.make_async_remote_copy(
            src_ref=su.at[i],
            dst_ref=sv.at[frm],
            send_sem=s_send.at[i],
            recv_sem=s_recv.at[frm],
            device_id=(g, (i // CROSS * CROSS + x) * CROSS + i % CROSS, t),
            device_id_type=MESH,
        )

    def s_mine(i):
        return in_column & (i == my_slot)

    def s_start(i, carry):
        su[i] = jnp.transpose(sums[i])[0:8]

        @pl.when(jnp.logical_not(s_mine(i)))
        def _():
            s_copy(i, z).start()

        return carry

    lax.fori_loop(0, slots, conv_slot, 0)

    @pl.when(in_column)
    def _():
        sv[z] = su[my_slot]

    def out_rows(ch):
        begin = (ch // per_block * CROSS + x) * head_rows + ch % per_block * small
        return pl.ds(pl.multiple_of(begin, 16), small)

    def f_copy(ch, rows):
        return pltpu.make_async_remote_copy(
            src_ref=fs.at[pl.ds(pl.multiple_of(ch * small, 16), small), :],
            dst_ref=out.at[rows, :],
            send_sem=f_send.at[ch],
            recv_sem=f_recv.at[ch],
            device_id=across,
            device_id_type=MESH,
        )

    def final_rows(row):
        i = row // owned
        k = row // head_rows
        rows = pl.ds(pl.multiple_of(row, STEP), STEP)
        within = pl.ds(pl.multiple_of(row % owned, STEP), STEP)
        lev = cols[i, within, 3:4]
        tap = cols[i, within, 0:3]
        left = gh[0, rows, :].astype(jnp.float32)
        here = go[rows, :]
        right = gh[1, rows, :].astype(jnp.float32)
        part = (
            tap[:, 0:1] * moved(left, here, right, lev, 1)
            + tap[:, 1:2] * here
            + tap[:, 2:3] * moved(left, here, right, lev, -1)
        )
        begin = (t * blocks + k) * head_rows + row % head_rows
        up = pl.ds(pl.multiple_of(begin, STEP), STEP)
        whole = jnp.concatenate([gp[xs, up, :] + gr[xs, up, :] for xs in range(CROSS)], axis=1)
        value = (whole + part).astype(jnp.bfloat16)
        begin = (k * CROSS + x) * head_rows + row % head_rows
        low, high = value[:, :own_rows], value[:, own_rows:]

        @pl.when(x == 0)
        def _():
            out[pl.ds(pl.multiple_of(begin, STEP), STEP), :] = low
            fs[rows, :] = high

        @pl.when(x != 0)
        def _():
            out[pl.ds(pl.multiple_of(begin, STEP), STEP), :] = high
            fs[rows, :] = low

    def final_chunk(ch, carry):
        @pl.when(has_down)
        def _():
            gz_copy(ch, 0, s).wait_recv()

        @pl.when(has_up)
        def _():
            gz_copy(ch, 1, s).wait_recv()

        def one(i, inner):
            final_rows(ch * small + i * STEP)
            return inner

        lax.fori_loop(0, small // STEP, one, 0)
        f_copy(ch, out_rows(ch)).start()
        return carry

    lax.fori_loop(0, chunks, final_chunk, 0)

    def s_wait(frm, carry):
        @pl.when(jnp.logical_not(in_column) | (frm != z))
        def _():
            s_copy(0, frm).wait_recv()

        return carry

    lax.fori_loop(0, chain, s_wait, 0)
    total = sv[0]
    for frm in range(1, chain):
        total = total + sv[frm]
    tg[...] = total[0:3, 0:owned] * norm

    def w_done(shard, carry):
        def one(c, inner):
            block = wb.at[w_rows(shard, c, g), :]

            @pl.when((shard <= z) & has_up)
            def _():
                w_hop(shard, c, block, z, 0).wait_send()

            @pl.when((shard >= z) & has_down)
            def _():
                w_hop(shard, c, block, z, 1).wait_send()

            @pl.when(shard != z)
            def _():
                w_swap(shard, c, g).wait_send()

            return inner

        lax.fori_loop(0, PARTS, one, 0)

        def p_one(c, inner):
            block = p_part(shard, c, g)

            @pl.when((shard <= z) & has_up)
            def _():
                p_hop(shard, c, block, z, 0).wait_send()

            @pl.when((shard >= z) & has_down)
            def _():
                p_hop(shard, c, block, z, 1).wait_send()

            @pl.when(shard != z)
            def _():
                p_swap(shard, c, g).wait_send()

            return inner

        lax.fori_loop(0, p_parts, p_one, 0)
        for xs in range(CROSS):
            g_copy(shard, xs).wait_send()

        @pl.when((shard != z) & in_column)
        def _():
            t_copy(shard, z).wait_send()

        return carry

    lax.fori_loop(0, chain, w_done, 0)

    @pl.when(jnp.logical_not(in_column))
    def _():
        u_copy(my_slot).wait_send()

    for c in range(ADJ_PARTS):
        a_copy(c, x).wait_send()
    for k in range(blocks):
        x_copy(k, 1 - x, x).wait_send()

    def slot_done(i, carry):
        @pl.when(has_up)
        def _():
            xz_copy(i, 0, s).wait_send()

        @pl.when(has_down)
        def _():
            xz_copy(i, 1, s).wait_send()

        @pl.when(jnp.logical_not(s_mine(i)))
        def _():
            s_copy(i, z).wait_send()

        return carry

    lax.fori_loop(0, slots, slot_done, 0)

    def chunk_done(ch, carry):
        c_copy(ch).wait_send()

        @pl.when(has_up)
        def _():
            gz_copy(ch, 0, s).wait_send()

        @pl.when(has_down)
        def _():
            gz_copy(ch, 1, s).wait_send()

        f_copy(ch, out_rows(ch)).wait()
        return carry

    lax.fori_loop(0, chunks, chunk_done, 0)


def hand_over(grad, taps, grad_out, taps_out, sem):
    copies = [
        pltpu.make_async_copy(grad, grad_out, sem.at[0]),
        pltpu.make_async_copy(taps, taps_out, sem.at[1]),
    ]
    for copy in copies:
        copy.start()
    for copy in copies:
        copy.wait()


def fused(
    chain,
    section_input,
    conv_taps,
    dilation_level,
    pointwise_matrix,
    head_weight,
    pred_error,
    tail_mask,
    track_scale,
):
    own, own_rows = section_input.shape
    owned = own // (chain * CROSS)
    head_rows, tracks = head_weight.shape
    pair_rows = CROSS * own_rows
    cols = pointwise_matrix.shape[1]
    blocks = chain // CROSS
    slots = blocks * CROSS
    chunks = slots * CHUNKS
    kept = blocks * head_rows
    bf16, f32 = jnp.bfloat16, jnp.float32
    dma = pltpu.SemaphoreType.DMA
    anywhere = pl.BlockSpec(memory_space=pltpu.HBM)
    vmem = pl.BlockSpec(memory_space=pltpu.VMEM)
    input_grad, taps_grad = pl.pallas_call(
        functools.partial(fused_kernel, chain),
        out_shape=(
            pltpu.VMEM((own, own_rows), bf16),
            pltpu.VMEM((3, owned), f32),
        ),
        in_specs=[anywhere] * 8,
        out_specs=(vmem, vmem),
        scratch_shapes=[
            pltpu.VMEM((3, owned), f32),
            pltpu.VMEM((1, owned), jnp.int32),
            pltpu.VMEM((tracks,), f32),
            pltpu.VMEM((chain * head_rows, tracks), bf16),
            pltpu.VMEM((CROSS, tracks, own_rows), bf16),
            pltpu.VMEM((tracks, own_rows), bf16),
            pltpu.VMEM((tracks, own_rows), jnp.int32),
            pltpu.VMEM((chain, cols, own), bf16),
            pltpu.VMEM((CROSS, chain * head_rows, own_rows), f32),
            pltpu.VMEM((CROSS, chain * head_rows, own_rows), f32),
            pltpu.VMEM((chain * head_rows, pair_rows), bf16),
            pltpu.VMEM((blocks, CROSS * head_rows, pair_rows), bf16),
            pltpu.VMEM((blocks, CROSS * head_rows, pair_rows), f32),
            pltpu.VMEM((kept, pair_rows), bf16),
            pltpu.VMEM((kept, pair_rows), bf16),
            pltpu.VMEM((2, kept, pair_rows), bf16),
            pltpu.VMEM((kept, pair_rows), f32),
            pltpu.VMEM((kept, pair_rows), bf16),
            pltpu.VMEM((2, kept, pair_rows), bf16),
            pltpu.VMEM((kept, own_rows), bf16),
            pltpu.VMEM((8, 128), f32),
            pltpu.VMEM((slots, 8, 128), f32),
            pltpu.VMEM((slots, 128, 128), f32),
            pltpu.VMEM((slots, 128, 128), f32),
            pltpu.VMEM((slots, 8, 128), f32),
            pltpu.VMEM((chain, 8, 128), f32),
            dma((3,)),
            dma((2 + blocks + 2 * ADJ_PARTS,)),
            dma((2, chain * PARTS)),
            dma((chain * PARTS,)),
            dma((chain * PARTS,)),
            dma((chain * PARTS,)),
            dma((2, chain * blocks)),
            dma((chain * blocks,)),
            dma((chain * blocks,)),
            dma((chain * blocks,)),
            dma((ADJ_PARTS,)),
            dma((ADJ_PARTS,)),
            dma((chain, CROSS)),
            dma((chain, CROSS)),
            dma((blocks,)),
            dma((blocks,)),
            dma((2, slots)),
            dma((2, slots)),
            dma,
            dma,
            dma((chain,)),
            dma((chain,)),
            dma((chunks,)),
            dma((chunks,)),
            dma((2, chunks)),
            dma((2, chunks)),
            dma((slots,)),
            dma((chain,)),
            dma((chunks,)),
            dma((chunks,)),
        ],
        compiler_params=pltpu.CompilerParams(
            collective_id=0, has_side_effects=True, vmem_limit_bytes=63 * 1024 * 1024
        ),
        name="fused_section",
    )(
        section_input,
        conv_taps.T,
        dilation_level[None, :],
        pointwise_matrix.T,
        head_weight,
        pred_error.T,
        tail_mask.T,
        track_scale,
    )
    input_grad, taps_grad = pl.pallas_call(
        hand_over,
        out_shape=(
            jax.ShapeDtypeStruct((own, own_rows), bf16),
            jax.ShapeDtypeStruct((3, owned), f32),
        ),
        in_specs=[vmem, vmem],
        out_specs=(anywhere, anywhere),
        scratch_shapes=[dma((2,))],
        name="hand_over",
    )(pltpu.with_memory_space_constraint(input_grad, pltpu.VMEM), pltpu.with_memory_space_constraint(taps_grad, pltpu.VMEM))
    return input_grad, taps_grad.T


def local_or_fused(sizes, *args):
    section_input, head_weight, pred_error = args[0], args[4], args[5]
    seq = sizes["seq"]
    own, own_rows = section_input.shape
    fits = (
        sizes["groups"] == 2
        and sizes["track"] == 2
        and seq == 8
        and head_weight.shape[0] % (2 * PARTS * 16) == 0
        and own % (seq * 16 * CHUNKS) == 0
        and own_rows % 128 == 0
        and CROSS * own_rows == BASE_DILATION * 2 ** (DILATION_COUNT - 1)
        and pred_error.shape[1] % 16 == 0
        and pred_error.shape[1] >= 128 * ADJ_PARTS
        and args[3].shape[1] % 32 == 0
        and own // seq <= 128
        and head_weight.shape[0] * 4 == own
        and own // 2 % 128 == 0
    )
    if fits:
        return fused(seq // CROSS, *args)
    return local(*args)


def solution(mesh):
    in_specs = (
        P("track", ("groups", "seq")),
        P(("track", "seq"), None),
        P(("track", "seq")),
        P("track", "seq"),
        P("seq", "track"),
        P(("groups", "seq"), "track"),
        P(("groups", "seq"), "track"),
        P("track"),
    )
    sizes = dict(mesh.shape)
    body = functools.partial(local_or_fused, sizes)
    out_specs = (P("track", ("groups", "seq")), P(("groups", "track", "seq"), None))
    return jax.shard_map(body, mesh=mesh, in_specs=in_specs, out_specs=out_specs, check_vma=False)
```

```python
import functools
import math

import jax
import jax.numpy as jnp
from jax import lax
from jax.experimental import pallas as pl
from jax.experimental.pallas import tpu as pltpu
from jax.sharding import PartitionSpec as P

DILATION_COUNT = 5
BASE_DILATION = 32


root_half = 0.7071067811865476
norm_const = 0.3989422804014327


def gelu_slope(value):
    return 0.5 * (1.0 + jax.scipy.special.erf(value * root_half)) + value * norm_const * jnp.exp(
        -0.5 * value * value
    )


def taps_at(buffer, onehot, margin, sign):
    width_own = buffer.shape[1] - 2 * margin
    result = jnp.zeros((buffer.shape[0], width_own), jnp.float32)
    for level_index in range(onehot.shape[1]):
        receptive_span = BASE_DILATION * 2**level_index
        begin = margin + sign * receptive_span
        result = (
            result + onehot[:, level_index : level_index + 1] * buffer[:, begin : begin + width_own]
        )
    return result


def spread(values, onehot, margin, sign):
    result = jnp.zeros((values.shape[0], values.shape[1] + 2 * margin), jnp.float32)
    for level_index in range(onehot.shape[1]):
        receptive_span = BASE_DILATION * 2**level_index
        placed = onehot[:, level_index : level_index + 1] * values
        result = result + jnp.pad(
            placed, ((0, 0), (margin + sign * receptive_span, margin - sign * receptive_span))
        )
    return result


def channel_grads(buffer, hidden_grad, taps, onehot, margin):
    width_own = buffer.shape[1] - 2 * margin
    minus_side = taps_at(buffer, onehot, margin, -1)
    center = buffer[:, margin : margin + width_own]
    plus_side = taps_at(buffer, onehot, margin, 1)
    pre_act = taps[:, 0:1] * minus_side + taps[:, 1:2] * center + taps[:, 2:3] * plus_side
    pre_grad = hidden_grad.astype(jnp.float32) * gelu_slope(pre_act)
    taps_part = jnp.stack(
        [
            jnp.sum(pre_grad * minus_side, axis=1),
            jnp.sum(pre_grad * center, axis=1),
            jnp.sum(pre_grad * plus_side, axis=1),
        ],
        axis=1,
    )
    contrib = spread(taps[:, 0:1] * pre_grad, onehot, margin, -1) + spread(
        taps[:, 2:3] * pre_grad, onehot, margin, 1
    )
    contrib = contrib + jnp.pad(taps[:, 1:2] * pre_grad, ((0, 0), (margin, margin)))
    return (contrib, taps_part)


def local(
    section_input,
    conv_taps,
    dilation_level,
    pointwise_matrix,
    head_weight,
    pred_error,
    tail_mask,
    track_scale,
):
    own_channels = section_input.shape[0]
    own_rows = section_input.shape[1]
    adjoint = (
        tail_mask.astype(jnp.float32) * track_scale[None, :] * pred_error.astype(jnp.float32)
    ).astype(jnp.bfloat16)
    full_grad = lax.dot_general(
        lax.all_gather(head_weight, "seq", axis=0, tiled=True),
        adjoint,
        (((1,), (1,)), ((), ())),
        preferred_element_type=jnp.float32,
    )
    total = lax.psum(full_grad, "track")
    out_grad_b = total.astype(jnp.bfloat16)
    out_grad = lax.dynamic_slice_in_dim(
        total, lax.axis_index("track") * own_channels, own_channels, 0
    )
    hidden_grad = jnp.dot(
        lax.all_gather(pointwise_matrix, "seq", axis=1, tiled=True),
        out_grad_b,
        preferred_element_type=jnp.float32,
    ).astype(jnp.bfloat16)
    largest_span = BASE_DILATION * 2 ** (DILATION_COUNT - 1)
    scale = 1.0 / math.sqrt(own_rows * lax.axis_size("seq"))
    onehot = (
        dilation_level[:, None] == jnp.arange(DILATION_COUNT, dtype=jnp.int32)[None, :]
    ).astype(jnp.float32)
    owned_input, owned_grad = (
        lax.all_to_all(section_input, "seq", split_axis=0, concat_axis=1, tiled=True),
        lax.all_to_all(hidden_grad, "seq", split_axis=0, concat_axis=1, tiled=True),
    )
    padded = jnp.pad(owned_input.astype(jnp.float32), ((0, 0), (largest_span, largest_span)))
    contrib, taps_part = channel_grads(padded, owned_grad, conv_taps, onehot, largest_span)
    window = contrib[:, largest_span : largest_span + owned_input.shape[1]]
    conv_part = lax.all_to_all(window, "seq", split_axis=1, concat_axis=0, tiled=True)
    taps_grad = taps_part * scale
    input_grad = (out_grad + conv_part).astype(jnp.bfloat16)
    return (input_grad, taps_grad)


MESH = pl.DeviceIdType.MESH
CROSS = 2
PARTS = 6
ADJ_PARTS = 2
STEP = 16
CHUNKS = 2


def fused_kernel(
    chain,
    sec,
    taps_in,
    level_in,
    pw,
    hw,
    err,
    mask,
    scale_in,
    out,
    tg,
    taps,
    level,
    scale,
    wb,
    ab,
    ev,
    mv,
    pb,
    gp,
    gr,
    ob,
    hs,
    hf,
    hx,
    xo,
    xh,
    go,
    gs,
    gh,
    fs,
    tile,
    tt,
    cols,
    sums,
    su,
    sv,
    table_sem,
    ld_sem,
    w_send,
    w_recv,
    wy_send,
    wy_recv,
    p_send,
    p_recv,
    py_send,
    py_recv,
    a_send,
    a_recv,
    g_send,
    g_recv,
    x_send,
    x_recv,
    xz_send,
    xz_recv,
    u_send,
    u_recv,
    t_send,
    t_recv,
    c_send,
    c_recv,
    gz_send,
    gz_recv,
    s_send,
    s_recv,
    f_send,
    f_recv,
):
    g = lax.axis_index("groups")
    s = lax.axis_index("seq")
    t = lax.axis_index("track")
    z = s // CROSS
    x = s % CROSS
    head_rows = hw.shape[0]
    half = head_rows // 2
    piece = half // PARTS
    tracks, own_rows = err.shape
    own = sec.shape[0]
    owned = own // (chain * CROSS)
    phalf = pw.shape[0] // 2
    step = tracks // ADJ_PARTS // 128 * 128
    cuts = [c * step for c in range(ADJ_PARTS)] + [tracks]
    pair_rows = CROSS * own_rows
    length = chain * pair_rows
    steps = chain - 1
    blocks = chain // CROSS
    slots = blocks * CROSS
    small = owned // CHUNKS

    sibling = (g, s, 1 - t)
    twin = (1 - g, s, t)
    across = (g, z * CROSS + 1 - x, t)
    has_up = z < chain - 1
    has_down = z > 0
    is_end = (z == 0) | (z == chain - 1)

    barrier = pltpu.get_barrier_semaphore()
    for device in (sibling, twin, across):
        pl.semaphore_signal(barrier, inc=1, device_id=device, device_id_type=MESH)

    @pl.when(has_up)
    def _():
        pl.semaphore_signal(barrier, inc=1, device_id=(g, s + CROSS, t), device_id_type=MESH)

    @pl.when(has_down)
    def _():
        pl.semaphore_signal(barrier, inc=1, device_id=(g, s - CROSS, t), device_id_type=MESH)

    own_w = pltpu.make_async_copy(
        hw, wb.at[pl.ds(pl.multiple_of(z * head_rows, 16), head_rows), :], ld_sem.at[0]
    )
    own_p = pltpu.make_async_copy(pw, pb.at[z], ld_sem.at[1])

    def block_rows(k, parity):
        return pl.ds(pl.multiple_of((CROSS * k + parity) * head_rows, 16), head_rows)

    def pair_lanes(which):
        return pl.ds(pl.multiple_of(which * own_rows, 128), own_rows)

    def kept_rows(k):
        return pl.ds(k * head_rows, head_rows)

    own_x = [
        pltpu.make_async_copy(
            sec.at[block_rows(k, x), :], xo.at[kept_rows(k), pair_lanes(x)], ld_sem.at[2 + k]
        )
        for k in range(blocks)
    ]
    loads = []
    for c in range(ADJ_PARTS):
        rows = pl.ds(cuts[c], cuts[c + 1] - cuts[c])
        at = 2 + blocks + 2 * c
        loads.append(
            (
                pltpu.make_async_copy(err.at[rows, :], ev.at[rows, :], ld_sem.at[at]),
                pltpu.make_async_copy(mask.at[rows, :], mv.at[rows, :], ld_sem.at[at + 1]),
            )
        )
    tables = [
        pltpu.make_async_copy(src, dst, table_sem.at[k])
        for k, (src, dst) in enumerate([(scale_in, scale), (taps_in, taps), (level_in, level)])
    ]
    tables[0].start()
    for first, second in loads:
        first.start()
        second.start()
    tables[1].start()
    tables[2].start()

    def fill_part(c):
        loads[c][0].wait()
        loads[c][1].wait()

        def fill(begin, count):
            rows = pl.ds(begin, count)
            line = scale[rows].reshape(1, count)
            if count < 128:
                line = jnp.concatenate([line, jnp.zeros((1, 128 - count), jnp.float32)], axis=1)
            column = jnp.transpose(jnp.broadcast_to(line, (128, 128)))[:count]
            column = jnp.concatenate([column] * (own_rows // 128), axis=1)
            value = mv[rows, :].astype(jnp.float32) * column * ev[rows, :].astype(jnp.float32)
            ab[x, rows, :] = value.astype(jnp.bfloat16)

        def fill_step(i, carry):
            fill(pl.multiple_of(cuts[c] + i * 128, 128), 128)
            return carry

        whole, rest = divmod(cuts[c + 1] - cuts[c], 128)
        lax.fori_loop(0, whole, fill_step, 0)
        if rest:
            fill(cuts[c] + whole * 128, rest)

    pl.semaphore_wait(barrier, jnp.where(is_end, 4, 5))

    def w_rows(shard, c, which):
        return pl.ds(pl.multiple_of(shard * head_rows + which * half + c * piece, 16), piece)

    def w_hop(shard, c, src, toward, direction):
        slot = shard * PARTS + c
        return pltpu.make_async_remote_copy(
            src_ref=src,
            dst_ref=wb.at[w_rows(shard, c, g), :],
            send_sem=w_send.at[direction, slot],
            recv_sem=w_recv.at[slot],
            device_id=(g, toward * CROSS + x, t),
            device_id_type=MESH,
        )

    def w_swap(shard, c, which):
        slot = shard * PARTS + c
        block = wb.at[w_rows(shard, c, which), :]
        return pltpu.make_async_remote_copy(
            src_ref=block,
            dst_ref=block,
            send_sem=wy_send.at[slot],
            recv_sem=wy_recv.at[slot],
            device_id=twin,
            device_id_type=MESH,
        )

    p_parts = blocks
    wide = CROSS * head_rows

    def p_part(shard, c, which):
        rows = pl.ds(pl.multiple_of(which * phalf, 16), phalf)
        return pb.at[shard, rows, pl.ds(pl.multiple_of(c * wide, 128), wide)]

    def p_hop(shard, c, src, toward, direction):
        slot = shard * p_parts + c
        return pltpu.make_async_remote_copy(
            src_ref=src,
            dst_ref=p_part(shard, c, g),
            send_sem=p_send.at[direction, slot],
            recv_sem=p_recv.at[slot],
            device_id=(g, toward * CROSS + x, t),
            device_id_type=MESH,
        )

    def p_swap(shard, c, which):
        slot = shard * p_parts + c
        block = p_part(shard, c, which)
        return pltpu.make_async_remote_copy(
            src_ref=block,
            dst_ref=block,
            send_sem=py_send.at[slot],
            recv_sem=py_recv.at[slot],
            device_id=twin,
            device_id_type=MESH,
        )

    def own_piece(c):
        return hw.at[pl.ds(pl.multiple_of(g * half + c * piece, 16), piece), :]

    def a_copy(c, which):
        block = ab.at[which, pl.ds(cuts[c], cuts[c + 1] - cuts[c]), :]
        return pltpu.make_async_remote_copy(
            src_ref=block,
            dst_ref=block,
            send_sem=a_send.at[c],
            recv_sem=a_recv.at[c],
            device_id=across,
            device_id_type=MESH,
        )

    lower = z < chain // 2

    def both_ways(go_up, go_down):
        @pl.when(lower)
        def _():
            pl.when(has_down)(go_down)
            pl.when(has_up)(go_up)

        @pl.when(jnp.logical_not(lower))
        def _():
            pl.when(has_up)(go_up)
            pl.when(has_down)(go_down)

    for c in range(PARTS):
        both_ways(
            lambda: w_hop(z, c, own_piece(c), z + 1, 0).start(),
            lambda: w_hop(z, c, own_piece(c), z - 1, 1).start(),
        )

    own_w.start()
    own_p.start()
    for k in range(blocks):
        own_x[k].start()
    tables[0].wait()
    for c in range(ADJ_PARTS):
        fill_part(c)
        a_copy(c, x).start()

    def own_p_part(c):
        return pw.at[pl.ds(pl.multiple_of(g * phalf, 16), phalf), pl.ds(c * wide, wide)]

    def p_send_own(c):
        both_ways(
            lambda: p_hop(z, c, own_p_part(c), z + 1, 0).start(),
            lambda: p_hop(z, c, own_p_part(c), z - 1, 1).start(),
        )

    for c in range(p_parts):
        p_send_own(c)

    below = z
    above = chain - 1 - z
    near = jnp.minimum(below, above)

    def order(j):
        jump = (j + 1) // 2
        alternate = jnp.where(j % 2 == 1, z - jump, z + jump)
        one_sided = jnp.where(above > below, z + (j - near), z - (j - near))
        return jnp.where(j <= 2 * near, alternate, one_sided)

    def shard_rows(shard):
        return pl.ds(pl.multiple_of(shard * head_rows, 16), head_rows)

    def g_copy(shard, xs):
        return pltpu.make_async_remote_copy(
            src_ref=gp.at[xs, shard_rows(shard), :],
            dst_ref=gr.at[xs, shard_rows(shard), :],
            send_sem=g_send.at[shard, xs],
            recv_sem=g_recv.at[shard, xs],
            device_id=sibling,
            device_id_type=MESH,
        )

    def head_dot(shard, xs):
        rows = shard_rows(shard)
        gp[xs, rows, :] = lax.dot_general(
            wb[rows, :],
            ab[xs],
            (((1,), (0,)), ((), ())),
            preferred_element_type=jnp.float32,
        )
        g_copy(shard, xs).start()

    def w_relay(e, carry):
        paired = (near >= 1) & (e < 2 * PARTS)
        j = jnp.where(paired, 1 + e % 2, e // PARTS + 1)
        c = jnp.where(paired, e // 2, e % PARTS)
        shard = order(j)
        block = wb.at[w_rows(shard, c, g), :]
        w_hop(shard, c, block, z, 0).wait_recv()

        @pl.when((shard < z) & has_up)
        def _():
            w_hop(shard, c, block, z + 1, 0).start()

        @pl.when((shard > z) & has_down)
        def _():
            w_hop(shard, c, block, z - 1, 1).start()

        w_swap(shard, c, g).start()
        return carry

    def wait_swaps(shard):
        def one(c, carry):
            w_swap(shard, c, 1 - g).wait_recv()
            return carry

        lax.fori_loop(0, PARTS, one, 0)

    def near_dot(j, carry):
        shard = order(j)
        wait_swaps(shard)
        head_dot(shard, x)
        return carry

    def p_relay(e, carry):
        shard = order(e % steps + 1)
        c = e // steps
        block = p_part(shard, c, g)
        p_hop(shard, c, block, z, 0).wait_recv()

        @pl.when((shard < z) & has_up)
        def _():
            p_hop(shard, c, block, z + 1, 0).start()

        @pl.when((shard > z) & has_down)
        def _():
            p_hop(shard, c, block, z - 1, 1).start()

        p_swap(shard, c, g).start()
        return carry

    def far_dot(j, carry):
        head_dot(order(j), 1 - x)
        return carry

    def x_copy(k, parity, which):
        return pltpu.make_async_remote_copy(
            src_ref=sec.at[block_rows(k, parity), :],
            dst_ref=xo.at[kept_rows(k), pair_lanes(which)],
            send_sem=x_send.at[k],
            recv_sem=x_recv.at[k],
            device_id=across,
            device_id_type=MESH,
        )

    def slot_rows(i):
        return pl.ds(pl.multiple_of(i * owned, 16), owned)

    def xz_copy(i, side, device):
        return pltpu.make_async_remote_copy(
            src_ref=xo.at[slot_rows(i), :],
            dst_ref=xh.at[side, slot_rows(i), :],
            send_sem=xz_send.at[side, i],
            recv_sem=xz_recv.at[side, i],
            device_id=(g, device, t),
            device_id_type=MESH,
        )

    my_slot = (z // CROSS) * CROSS + x
    in_column = z % CROSS == x

    def u_copy(slot):
        return pltpu.make_async_remote_copy(
            src_ref=tile,
            dst_ref=tt.at[slot],
            send_sem=u_send,
            recv_sem=u_recv,
            device_id=across,
            device_id_type=MESH,
        )

    def t_copy(to, frm):
        pair = tt.at[pl.ds(frm // CROSS * CROSS, CROSS)]
        return pltpu.make_async_remote_copy(
            src_ref=pair,
            dst_ref=pair,
            send_sem=t_send.at[to],
            recv_sem=t_recv.at[frm],
            device_id=(g, to * CROSS + x, t),
            device_id_type=MESH,
        )

    own_w.wait()
    head_dot(z, x)

    tables[1].wait()
    tables[2].wait()
    tile[...] = jnp.zeros((8, 128), jnp.float32)
    tile[0:3, 0:owned] = taps[...]
    tile[3:4, 0:owned] = level[...].astype(jnp.float32)

    @pl.when(jnp.logical_not(in_column))
    def _():
        u_copy(my_slot).start()

    @pl.when(in_column)
    def _():
        tt[my_slot] = tile[...]

    @pl.when(z == 0)
    def _():
        xh[0] = jnp.zeros(xh.shape[1:], jnp.bfloat16)
        gh[0] = jnp.zeros(gh.shape[1:], jnp.bfloat16)

    @pl.when(z == chain - 1)
    def _():
        xh[1] = jnp.zeros(xh.shape[1:], jnp.bfloat16)
        gh[1] = jnp.zeros(gh.shape[1:], jnp.bfloat16)

    for i in range(slots):
        sums[i] = jnp.zeros((128, 128), jnp.float32)

    def end_relay(begin, end):
        lax.fori_loop(begin, jnp.where(is_end, end, begin), p_relay, 0)

    lax.fori_loop(0, PARTS, w_relay, 0)
    for c in range(p_parts):
        end_relay(c * steps, c * steps + 1)
    lax.fori_loop(PARTS, (steps - 1) * PARTS, w_relay, 0)
    first = jnp.where(is_end, 2, 1)
    lax.fori_loop(1, first, near_dot, 0)
    lax.fori_loop((steps - 1) * PARTS, steps * PARTS, w_relay, 0)

    @pl.when(in_column)
    def _():
        u_copy(my_slot).wait_recv()

        def t_start(j, carry):
            t_copy(order(j), z).start()
            return carry

        lax.fori_loop(1, chain, t_start, 0)

    for k in range(blocks):
        x_copy(k, 1 - x, x).start()

    lax.fori_loop(0, jnp.where(is_end, 0, p_parts * steps), p_relay, 0)
    lax.fori_loop(first, steps, near_dot, 0)
    for c in range(ADJ_PARTS):
        a_copy(c, 1 - x).wait_recv()
    lax.fori_loop(0, steps, far_dot, 0)
    end_relay(1, 2)
    last = order(steps)
    wait_swaps(last)
    head_dot(last, x)
    head_dot(last, 1 - x)
    end_relay(2, steps)

    for k in range(blocks):
        own_x[k].wait()
        x_copy(k, x, 1 - x).wait_recv()

    def xz_start(i, carry):
        both_ways(
            lambda: xz_copy(i, 0, s + CROSS).start(), lambda: xz_copy(i, 1, s - CROSS).start()
        )

        return carry

    lax.fori_loop(0, slots, xz_start, 0)

    def core_sum(j, carry):
        shard = order(j)
        rows = shard_rows(shard)
        for xs in range(CROSS):
            g_copy(shard, xs).wait_recv()
            ob[rows, xs * own_rows : (xs + 1) * own_rows] = (gp[xs, rows, :] + gr[xs, rows, :]).astype(
                jnp.bfloat16
            )
        return carry

    lax.fori_loop(0, chain, core_sum, 0)

    own_p.wait()

    def p_wait(c):
        def one(j, carry):
            p_swap(order(j), c, 1 - g).wait_recv()
            return carry

        lax.fori_loop(1, steps + 1, one, 0)

    per_block = head_rows // small
    chunks = blocks * per_block

    def c_copy(ch):
        k = ch // per_block
        begin = (1 - x) * head_rows + (ch % per_block) * small
        return pltpu.make_async_remote_copy(
            src_ref=hs.at[k, pl.ds(pl.multiple_of(begin, 16), small), :],
            dst_ref=hx.at[pl.ds(pl.multiple_of(ch * small, 16), small), :],
            send_sem=c_send.at[ch],
            recv_sem=c_recv.at[ch],
            device_id=across,
            device_id_type=MESH,
        )

    def h_step(k, carry):
        lanes = pl.ds(pl.multiple_of(k * wide, 128), wide)
        total = jnp.zeros((wide, pair_rows), jnp.float32)
        for shard in range(chain):
            total = total + lax.dot_general(
                pb[shard, :, lanes],
                ob[shard * head_rows : (shard + 1) * head_rows, :],
                (((0,), (0,)), ((), ())),
                preferred_element_type=jnp.float32,
            )
        hs[k] = total.astype(jnp.bfloat16)
        hf[k] = total

        def c_start(u, inner):
            c_copy(k * per_block + u).start()
            return inner

        lax.fori_loop(0, per_block, c_start, 0)
        return carry

    end_relay(steps + 1, blocks * steps)
    p_wait(0)
    h_step(0, 0)
    p_wait(1)
    h_step(1, 0)

    norm = 1.0 / math.sqrt(length)

    def t_wait(frm, carry):
        @pl.when((frm % CROSS == x) & (frm != z))
        def _():
            t_copy(0, frm).wait_recv()

        return carry

    lax.fori_loop(0, chain, t_wait, 0)
    for i in range(slots):
        padded = jnp.concatenate([tt[i], jnp.zeros((120, 128), jnp.float32)], axis=0)
        cols[i] = jnp.transpose(padded)

    def moved(left, here, right, lev, sign):
        result = None
        for k in range(DILATION_COUNT):
            reach = BASE_DILATION * 2**k
            if sign < 0:
                if reach % 128 == 0:
                    value = (
                        left
                        if reach == pair_rows
                        else jnp.concatenate([left[:, pair_rows - reach :], here[:, : pair_rows - reach]], axis=1)
                    )
                else:
                    joined = jnp.concatenate([left[:, pair_rows - 128 :], here], axis=1)
                    value = pltpu.roll(joined, reach, 1)[:, 128:]
            else:
                if reach % 128 == 0:
                    value = (
                        right
                        if reach == pair_rows
                        else jnp.concatenate([here[:, reach:], right[:, :reach]], axis=1)
                    )
                else:
                    joined = jnp.concatenate([here, right[:, :128]], axis=1)
                    value = pltpu.roll(joined, pair_rows + 128 - reach, 1)[:, :pair_rows]
            result = value if result is None else jnp.where(lev == float(k), value, result)
        return result

    def gz_copy(ch, side, device):
        rows = pl.ds(pl.multiple_of(ch * small, 16), small)
        return pltpu.make_async_remote_copy(
            src_ref=gs.at[rows, :],
            dst_ref=gh.at[side, rows, :],
            send_sem=gz_send.at[side, ch],
            recv_sem=gz_recv.at[side, ch],
            device_id=(g, device, t),
            device_id_type=MESH,
        )

    def conv_rows(row):
        i = row // owned
        rows = pl.ds(pl.multiple_of(row, STEP), STEP)
        within = pl.ds(pl.multiple_of(row % owned, STEP), STEP)
        lev = cols[i, within, 3:4]
        tap = cols[i, within, 0:3]
        left = xh[0, rows, :].astype(jnp.float32)
        center = xo[rows, :].astype(jnp.float32)
        right = xh[1, rows, :].astype(jnp.float32)
        minus = moved(left, center, right, lev, -1)
        plus = moved(left, center, right, lev, 1)
        pre_act = tap[:, 0:1] * minus + tap[:, 1:2] * center + tap[:, 2:3] * plus
        mine = pl.ds(pl.multiple_of(x * head_rows + row % head_rows, STEP), STEP)
        hidden = (hf[row // head_rows, mine, :] + hx[rows, :].astype(jnp.float32)).astype(jnp.bfloat16)
        pre_grad = hidden.astype(jnp.float32) * gelu_slope(pre_act)
        go[rows, :] = pre_grad
        gs[rows, :] = pre_grad.astype(jnp.bfloat16)
        sums[i, within, 0:1] = jnp.sum(pre_grad * minus, axis=1, keepdims=True)
        sums[i, within, 1:2] = jnp.sum(pre_grad * center, axis=1, keepdims=True)
        sums[i, within, 2:3] = jnp.sum(pre_grad * plus, axis=1, keepdims=True)

    def conv_chunk(ch, carry):
        c_copy(ch).wait_recv()

        @pl.when((ch % CHUNKS == 0) & has_down)
        def _():
            xz_copy(ch // CHUNKS, 0, s).wait_recv()

        @pl.when((ch % CHUNKS == 0) & has_up)
        def _():
            xz_copy(ch // CHUNKS, 1, s).wait_recv()

        def one(i, inner):
            conv_rows(ch * small + i * STEP)
            return inner

        lax.fori_loop(0, small // STEP, one, 0)

        both_ways(
            lambda: gz_copy(ch, 0, s + CROSS).start(), lambda: gz_copy(ch, 1, s - CROSS).start()
        )

        return carry

    def conv_slot(i, carry):
        lax.fori_loop(i * CHUNKS, (i + 1) * CHUNKS, conv_chunk, 0)
        return s_start(i, carry)


    def s_copy(i, frm):
        return pltpu.make_async_remote_copy(
            src_ref=su.at[i],
            dst_ref=sv.at[frm],
            send_sem=s_send.at[i],
            recv_sem=s_recv.at[frm],
            device_id=(g, (i // CROSS * CROSS + x) * CROSS + i % CROSS, t),
            device_id_type=MESH,
        )

    def s_mine(i):
        return in_column & (i == my_slot)

    def s_start(i, carry):
        su[i] = jnp.transpose(sums[i])[0:8]

        @pl.when(jnp.logical_not(s_mine(i)))
        def _():
            s_copy(i, z).start()

        return carry

    lax.fori_loop(0, slots, conv_slot, 0)

    @pl.when(in_column)
    def _():
        sv[z] = su[my_slot]

    def out_rows(ch):
        begin = (ch // per_block * CROSS + x) * head_rows + ch % per_block * small
        return pl.ds(pl.multiple_of(begin, 16), small)

    def f_copy(ch, rows):
        return pltpu.make_async_remote_copy(
            src_ref=fs.at[pl.ds(pl.multiple_of(ch * small, 16), small), :],
            dst_ref=out.at[rows, :],
            send_sem=f_send.at[ch],
            recv_sem=f_recv.at[ch],
            device_id=across,
            device_id_type=MESH,
        )

    def final_rows(row):
        i = row // owned
        k = row // head_rows
        rows = pl.ds(pl.multiple_of(row, STEP), STEP)
        within = pl.ds(pl.multiple_of(row % owned, STEP), STEP)
        lev = cols[i, within, 3:4]
        tap = cols[i, within, 0:3]
        left = gh[0, rows, :].astype(jnp.float32)
        here = go[rows, :]
        right = gh[1, rows, :].astype(jnp.float32)
        part = (
            tap[:, 0:1] * moved(left, here, right, lev, 1)
            + tap[:, 1:2] * here
            + tap[:, 2:3] * moved(left, here, right, lev, -1)
        )
        begin = (t * blocks + k) * head_rows + row % head_rows
        up = pl.ds(pl.multiple_of(begin, STEP), STEP)
        whole = jnp.concatenate([gp[xs, up, :] + gr[xs, up, :] for xs in range(CROSS)], axis=1)
        value = (whole + part).astype(jnp.bfloat16)
        begin = (k * CROSS + x) * head_rows + row % head_rows
        low, high = value[:, :own_rows], value[:, own_rows:]

        @pl.when(x == 0)
        def _():
            out[pl.ds(pl.multiple_of(begin, STEP), STEP), :] = low
            fs[rows, :] = high

        @pl.when(x != 0)
        def _():
            out[pl.ds(pl.multiple_of(begin, STEP), STEP), :] = high
            fs[rows, :] = low

    def final_chunk(ch, carry):
        @pl.when(has_down)
        def _():
            gz_copy(ch, 0, s).wait_recv()

        @pl.when(has_up)
        def _():
            gz_copy(ch, 1, s).wait_recv()

        def one(i, inner):
            final_rows(ch * small + i * STEP)
            return inner

        lax.fori_loop(0, small // STEP, one, 0)
        f_copy(ch, out_rows(ch)).start()
        return carry

    lax.fori_loop(0, chunks, final_chunk, 0)

    def s_wait(frm, carry):
        @pl.when(jnp.logical_not(in_column) | (frm != z))
        def _():
            s_copy(0, frm).wait_recv()

        return carry

    lax.fori_loop(0, chain, s_wait, 0)
    total = sv[0]
    for frm in range(1, chain):
        total = total + sv[frm]
    tg[...] = total[0:3, 0:owned] * norm

    def w_done(shard, carry):
        def one(c, inner):
            block = wb.at[w_rows(shard, c, g), :]

            @pl.when((shard <= z) & has_up)
            def _():
                w_hop(shard, c, block, z, 0).wait_send()

            @pl.when((shard >= z) & has_down)
            def _():
                w_hop(shard, c, block, z, 1).wait_send()

            @pl.when(shard != z)
            def _():
                w_swap(shard, c, g).wait_send()

            return inner

        lax.fori_loop(0, PARTS, one, 0)

        def p_one(c, inner):
            block = p_part(shard, c, g)

            @pl.when((shard <= z) & has_up)
            def _():
                p_hop(shard, c, block, z, 0).wait_send()

            @pl.when((shard >= z) & has_down)
            def _():
                p_hop(shard, c, block, z, 1).wait_send()

            @pl.when(shard != z)
            def _():
                p_swap(shard, c, g).wait_send()

            return inner

        lax.fori_loop(0, p_parts, p_one, 0)
        for xs in range(CROSS):
            g_copy(shard, xs).wait_send()

        @pl.when((shard != z) & in_column)
        def _():
            t_copy(shard, z).wait_send()

        return carry

    lax.fori_loop(0, chain, w_done, 0)

    @pl.when(jnp.logical_not(in_column))
    def _():
        u_copy(my_slot).wait_send()

    for c in range(ADJ_PARTS):
        a_copy(c, x).wait_send()
    for k in range(blocks):
        x_copy(k, 1 - x, x).wait_send()

    def slot_done(i, carry):
        @pl.when(has_up)
        def _():
            xz_copy(i, 0, s).wait_send()

        @pl.when(has_down)
        def _():
            xz_copy(i, 1, s).wait_send()

        @pl.when(jnp.logical_not(s_mine(i)))
        def _():
            s_copy(i, z).wait_send()

        return carry

    lax.fori_loop(0, slots, slot_done, 0)

    def chunk_done(ch, carry):
        c_copy(ch).wait_send()

        @pl.when(has_up)
        def _():
            gz_copy(ch, 0, s).wait_send()

        @pl.when(has_down)
        def _():
            gz_copy(ch, 1, s).wait_send()

        f_copy(ch, out_rows(ch)).wait()
        return carry

    lax.fori_loop(0, chunks, chunk_done, 0)


def hand_over(grad, taps, grad_out, taps_out, sem):
    copies = [
        pltpu.make_async_copy(grad, grad_out, sem.at[0]),
        pltpu.make_async_copy(taps, taps_out, sem.at[1]),
    ]
    for copy in copies:
        copy.start()
    for copy in copies:
        copy.wait()


def fused(
    chain,
    section_input,
    conv_taps,
    dilation_level,
    pointwise_matrix,
    head_weight,
    pred_error,
    tail_mask,
    track_scale,
):
    own, own_rows = section_input.shape
    owned = own // (chain * CROSS)
    head_rows, tracks = head_weight.shape
    pair_rows = CROSS * own_rows
    cols = pointwise_matrix.shape[1]
    blocks = chain // CROSS
    slots = blocks * CROSS
    chunks = slots * CHUNKS
    kept = blocks * head_rows
    bf16, f32 = jnp.bfloat16, jnp.float32
    dma = pltpu.SemaphoreType.DMA
    anywhere = pl.BlockSpec(memory_space=pltpu.HBM)
    vmem = pl.BlockSpec(memory_space=pltpu.VMEM)
    input_grad, taps_grad = pl.pallas_call(
        functools.partial(fused_kernel, chain),
        out_shape=(
            pltpu.VMEM((own, own_rows), bf16),
            pltpu.VMEM((3, owned), f32),
        ),
        in_specs=[anywhere] * 8,
        out_specs=(vmem, vmem),
        scratch_shapes=[
            pltpu.VMEM((3, owned), f32),
            pltpu.VMEM((1, owned), jnp.int32),
            pltpu.VMEM((tracks,), f32),
            pltpu.VMEM((chain * head_rows, tracks), bf16),
            pltpu.VMEM((CROSS, tracks, own_rows), bf16),
            pltpu.VMEM((tracks, own_rows), bf16),
            pltpu.VMEM((tracks, own_rows), jnp.int32),
            pltpu.VMEM((chain, cols, own), bf16),
            pltpu.VMEM((CROSS, chain * head_rows, own_rows), f32),
            pltpu.VMEM((CROSS, chain * head_rows, own_rows), f32),
            pltpu.VMEM((chain * head_rows, pair_rows), bf16),
            pltpu.VMEM((blocks, CROSS * head_rows, pair_rows), bf16),
            pltpu.VMEM((blocks, CROSS * head_rows, pair_rows), f32),
            pltpu.VMEM((kept, pair_rows), bf16),
            pltpu.VMEM((kept, pair_rows), bf16),
            pltpu.VMEM((2, kept, pair_rows), bf16),
            pltpu.VMEM((kept, pair_rows), f32),
            pltpu.VMEM((kept, pair_rows), bf16),
            pltpu.VMEM((2, kept, pair_rows), bf16),
            pltpu.VMEM((kept, own_rows), bf16),
            pltpu.VMEM((8, 128), f32),
            pltpu.VMEM((slots, 8, 128), f32),
            pltpu.VMEM((slots, 128, 128), f32),
            pltpu.VMEM((slots, 128, 128), f32),
            pltpu.VMEM((slots, 8, 128), f32),
            pltpu.VMEM((chain, 8, 128), f32),
            dma((3,)),
            dma((2 + blocks + 2 * ADJ_PARTS,)),
            dma((2, chain * PARTS)),
            dma((chain * PARTS,)),
            dma((chain * PARTS,)),
            dma((chain * PARTS,)),
            dma((2, chain * blocks)),
            dma((chain * blocks,)),
            dma((chain * blocks,)),
            dma((chain * blocks,)),
            dma((ADJ_PARTS,)),
            dma((ADJ_PARTS,)),
            dma((chain, CROSS)),
            dma((chain, CROSS)),
            dma((blocks,)),
            dma((blocks,)),
            dma((2, slots)),
            dma((2, slots)),
            dma,
            dma,
            dma((chain,)),
            dma((chain,)),
            dma((chunks,)),
            dma((chunks,)),
            dma((2, chunks)),
            dma((2, chunks)),
            dma((slots,)),
            dma((chain,)),
            dma((chunks,)),
            dma((chunks,)),
        ],
        compiler_params=pltpu.CompilerParams(
            collective_id=0, has_side_effects=True, vmem_limit_bytes=63 * 1024 * 1024
        ),
        name="fused_section",
    )(
        section_input,
        conv_taps.T,
        dilation_level[None, :],
        pointwise_matrix.T,
        head_weight,
        pred_error.T,
        tail_mask.T,
        track_scale,
    )
    input_grad, taps_grad = pl.pallas_call(
        hand_over,
        out_shape=(
            jax.ShapeDtypeStruct((own, own_rows), bf16),
            jax.ShapeDtypeStruct((3, owned), f32),
        ),
        in_specs=[vmem, vmem],
        out_specs=(anywhere, anywhere),
        scratch_shapes=[dma((2,))],
        name="hand_over",
    )(pltpu.with_memory_space_constraint(input_grad, pltpu.VMEM), pltpu.with_memory_space_constraint(taps_grad, pltpu.VMEM))
    return input_grad, taps_grad.T


def local_or_fused(sizes, *args):
    section_input, head_weight, pred_error = args[0], args[4], args[5]
    seq = sizes["seq"]
    own, own_rows = section_input.shape
    fits = (
        sizes["groups"] == 2
        and sizes["track"] == 2
        and seq == 8
        and head_weight.shape[0] % (2 * PARTS * 16) == 0
        and own % (seq * 16 * CHUNKS) == 0
        and own_rows % 128 == 0
        and CROSS * own_rows == BASE_DILATION * 2 ** (DILATION_COUNT - 1)
        and pred_error.shape[1] % 16 == 0
        and pred_error.shape[1] >= 128 * ADJ_PARTS
        and args[3].shape[1] % 32 == 0
        and own // seq <= 128
        and head_weight.shape[0] * 4 == own
        and own // 2 % 128 == 0
    )
    if fits:
        return fused(seq // CROSS, *args)
    return local(*args)


def solution(mesh):
    in_specs = (
        P("track", ("groups", "seq")),
        P(("track", "seq"), None),
        P(("track", "seq")),
        P("track", "seq"),
        P("seq", "track"),
        P(("groups", "seq"), "track"),
        P(("groups", "seq"), "track"),
        P("track"),
    )
    sizes = dict(mesh.shape)
    body = functools.partial(local_or_fused, sizes)
    out_specs = (P("track", ("groups", "seq")), P(("groups", "track", "seq"), None))
    return jax.shard_map(body, mesh=mesh, in_specs=in_specs, out_specs=out_specs, check_vma=False)
```
